32 devices in a mesh: cuts: 2 (over y), group: 16 (over z, x, core).
Axes of the slice: x: 2, y: 2, z: 4, core: 2. Of those that a mesh axis runs over, the one named last changes fastest.
Arguments:
- stem_blocks: bfloat16 [2, 64, 1024, 512], P('cuts', None, 'group'), may hold values from -6 to 6
- cap_tensor: bfloat16 [2, 2, 256, 256], P('cuts'), may hold values from -0.1875 to 0.1875
- slot_rows: int32 [64, 1024], P('group'), may hold values from 0 to 1023
- counts: int32 [64], P('group'), may hold values from 128 to 1024, as said below
Outputs:
- amplitudes: bfloat16 [1024, 64, 512], P('cuts', 'group')
The draws below stay inside these ranges and needn't reach their ends.
Inputs may be any that keep to these rules, and one draw needn't show every extreme that they name: `counts`: some group has exactly 1024 live slots in every draw.
All inputs are finite; a program needn't handle non-finite values.
Results may differ from the reference program's by a relative error of at most 0.0052.
Values may be sent and summed in bfloat16 or wider, within the bound.
No kernel may reach another device: no remote copies, remote signals or barrier semaphores. Data moves between devices by JAX's collectives and lax.ppermute only.
A program may use at most 64 MiB of HBM per device.

```python
import jax
import jax.numpy as jnp
from jax import lax

K = 256
S = 256
ROWS = 1024
CAP = 1024
GROUPS = 64
N_CUTS = 2


def draw_counts(key, part):
    first_key, second_key = jax.random.split(jax.random.fold_in(key, 17))
    base_counts = jax.random.randint(first_key, (GROUPS,), CAP // 8, 2 * CAP // 3 + 1)
    chosen = jax.random.randint(second_key, (), 0, GROUPS)
    return jnp.where(jnp.arange(GROUPS) == chosen, CAP, base_counts).astype(jnp.int32)


def set_ends(drawn, rng, low, high):
    extent = drawn.shape
    spot = [jax.random.randint(jax.random.fold_in(rng, axis), (), 0, extent[axis]) for axis in range(len(extent))]
    drawn = drawn.at[tuple(spot)].set(low)
    longest = extent.index(max(extent))
    spot[longest] = (spot[longest] + 1) % extent[longest]
    return drawn.at[tuple(spot)].set(high)


def level_of(rng, dims, shards, low, high):
    loudness, own = 1.0, jax.random.fold_in(rng, 6)
    for dim, parts in shards:
        heights = jnp.exp(jax.random.uniform(jax.random.fold_in(own, dim), (parts,), jnp.float32, low / len(shards), high / len(shards)))
        loudness = loudness * jnp.repeat(heights, dims[dim] // parts).reshape([-1 if axis == dim else 1 for axis in range(len(dims))])
    return loudness


def bell_draw(key, extent, deviation, most, cuts=(), kind=jnp.bfloat16):
    values = jax.random.normal(key, extent, jnp.float32) * deviation
    if len(cuts) > 0:
        values = level_of(key, extent, cuts, -0.22, 0.18) * values
    return jnp.clip(values, min=-most, max=most).astype(kind)


def setup_inputs(seed: int = 0) -> dict:
    arg_keys = jax.random.split(jax.random.key(seed), 5)
    return {
        "stem_blocks": bell_draw(arg_keys[0], (N_CUTS, GROUPS, ROWS, 2 * K), 1.0, 6.0, ((0, 2), (2, 16))),
        "cap_tensor": bell_draw(arg_keys[1], (N_CUTS, 2, K, S), (2 * K * N_CUTS) ** -0.5, 0.1875, ((0, 2),)),
        "slot_rows": set_ends(jax.random.randint(arg_keys[2], (GROUPS, CAP), 0, ROWS), jax.random.fold_in(arg_keys[2], 1), 0, ROWS - 1).astype(jnp.int32),
        "counts": draw_counts(jax.random.fold_in(arg_keys[4], 71), 0),
    }


def build_matrix(cap_pair):
    real_part = cap_pair[0]
    imag_part = cap_pair[1]
    upper = jnp.concatenate([real_part, imag_part], axis=1)
    lower = jnp.concatenate([-imag_part, real_part], axis=1)
    return jnp.concatenate([upper, lower], axis=0)


def reference(stem_blocks, cap_tensor, slot_rows, counts):
    summed = jnp.zeros((GROUPS, CAP, 2 * S), jnp.float32)
    for slice_idx in range(N_CUTS):
        matrix = build_matrix(cap_tensor[slice_idx])

        def one_group(pair):
            group_rows, group_slots = pair
            picked = jnp.take(group_rows, group_slots, axis=0)
            product = jnp.dot(picked, matrix, preferred_element_type=jnp.float32)
            return product.astype(jnp.bfloat16).astype(jnp.float32)

        summed = summed + lax.map(one_group, (stem_blocks[slice_idx], slot_rows))
    live_mask = jnp.arange(CAP, dtype=jnp.int32)[None, :] < counts[:, None]
    summed = jnp.where(live_mask[:, :, None], summed, jnp.float32(0.0))
    return jnp.transpose(summed, (1, 0, 2)).astype(jnp.bfloat16)
```

```python
import functools

import jax
import jax.numpy as jnp
from jax import lax
from jax.experimental import pallas as pl
from jax.experimental.pallas import tpu as pltpu
from jax.sharding import PartitionSpec as P


def build_matrix(cap_pair):
    real_part = cap_pair[0]
    imag_part = cap_pair[1]
    upper = jnp.concatenate([real_part, imag_part], axis=1)
    lower = jnp.concatenate([-imag_part, real_part], axis=1)
    return jnp.concatenate([upper, lower], axis=0)


def select_kernel(block, share, rows_ref, matrix_ref, slots_ref, *refs):
    outs, terms = refs[:-1], refs[-1]
    row_total = rows_ref.shape[0]
    for start in range(0, row_total, block):
        terms[pl.ds(start, block), :] = jnp.dot(
            rows_ref[pl.ds(start, block), :], matrix_ref[...], preferred_element_type=jnp.float32
        ).astype(terms.dtype)
    columns = lax.broadcasted_iota(jnp.int32, (block, row_total), 1)
    for part, out in enumerate(outs):
        for start in range(0, share, block):
            slots = slots_ref[pl.ds(part * share + start, block), :]
            chosen = jnp.where(columns == slots, 1.0, 0.0).astype(terms.dtype)
            out[pl.ds(start, block), :] = jnp.dot(
                chosen, terms[...], preferred_element_type=jnp.float32
            ).astype(out.dtype)


def select(rows, matrix, slots, parts):
    row_total, width = rows.shape
    slot_total = slots.shape[0]
    share = slot_total // parts
    block = min(256, share)
    out = jax.ShapeDtypeStruct((share, matrix.shape[1]), rows.dtype)
    flops = 2 * row_total * matrix.shape[1] * (width + slot_total)
    return pl.pallas_call(
        functools.partial(select_kernel, block, share),
        out_shape=[out] * parts,
        in_specs=[pl.BlockSpec(memory_space=pltpu.VMEM)] * 3,
        out_specs=[pl.BlockSpec(memory_space=pltpu.VMEM)] * parts,
        scratch_shapes=[pltpu.VMEM((row_total, matrix.shape[1]), rows.dtype)],
        cost_estimate=pl.CostEstimate(
            flops=flops,
            bytes_accessed=2 * (rows.size + slot_total * matrix.shape[1]),
            transcendentals=0,
        ),
        compiler_params=pltpu.CompilerParams(vmem_limit_bytes=24 << 20),
    )(rows, matrix, slots)


def local(stem_blocks, cap_tensor, slot_rows, counts):
    cuts, groups = lax.axis_size("cuts"), lax.axis_size("group")
    stem = stem_blocks[0]
    group_total, own_rows, width = stem.shape
    mine = group_total // groups
    slot_total = slot_rows.shape[1]
    share = slot_total // cuts
    matrix = build_matrix(cap_tensor[0])

    positions = jnp.arange(slot_total, dtype=jnp.int32)
    marked = jnp.where(positions[None, :] < counts[:, None], slot_rows, -1)
    me = lax.axis_index("cuts")
    doubled = jnp.concatenate([marked, marked], axis=1)
    turned = lax.dynamic_slice_in_dim(doubled, (me + 1) * share, slot_total, 1)
    by_owner = stem.reshape(groups, mine, own_rows, width)

    sums, selected = [], []
    for k in range(mine):
        outgoing = by_owner[:, k]
        if k >= 2:
            outgoing, selected[k - 2] = lax.optimization_barrier((outgoing, selected[k - 2]))
        got = lax.all_to_all(outgoing, "group", split_axis=0, concat_axis=0, tiled=True)
        parts = select(got.reshape(groups * own_rows, width), matrix, turned[k][:, None], cuts)
        selected.append(parts)
    for parts in selected:
        total = parts[-1].astype(jnp.float32)
        for step in range(1, cuts):
            ring = [(i, (i + step) % cuts) for i in range(cuts)]
            total = total + lax.ppermute(parts[step - 1], "cuts", ring).astype(jnp.float32)
        sums.append(total.astype(stem.dtype))
    return jnp.stack(sums, axis=1)


def solution(mesh):
    in_specs = (
        P("cuts", None, "group", None),
        P("cuts", None, None, None),
        P("group", None),
        P("group"),
    )
    out_specs = P("cuts", "group", None)
    return jax.shard_map(local, mesh=mesh, in_specs=in_specs, out_specs=out_specs, check_vma=False)
```

```python
import functools

import jax
import jax.numpy as jnp
from jax import lax
from jax.experimental import pallas as pl
from jax.experimental.pallas import tpu as pltpu
from jax.sharding import PartitionSpec as P


def build_matrix(cap_pair):
    real_part = cap_pair[0]
    imag_part = cap_pair[1]
    upper = jnp.concatenate([real_part, imag_part], axis=1)
    lower = jnp.concatenate([-imag_part, real_part], axis=1)
    return jnp.concatenate([upper, lower], axis=0)


def select_kernel(block, share, rows_ref, matrix_ref, slots_ref, *refs):
    outs, terms = refs[:-1], refs[-1]
    row_total = rows_ref.shape[0]
    for start in range(0, row_total, block):
        terms[pl.ds(start, block), :] = jnp.dot(
            rows_ref[pl.ds(start, block), :], matrix_ref[...], preferred_element_type=jnp.float32
        ).astype(terms.dtype)
    columns = lax.broadcasted_iota(jnp.int32, (block, row_total), 1)
    for part, out in enumerate(outs):
        for start in range(0, share, block):
            slots = slots_ref[pl.ds(part * share + start, block), :]
            chosen = jnp.where(columns == slots, 1.0, 0.0).astype(terms.dtype)
            out[pl.ds(start, block), :] = jnp.dot(
                chosen, terms[...], preferred_element_type=jnp.float32
            ).astype(out.dtype)


def select(rows, matrix, slots, parts):
    row_total, width = rows.shape
    slot_total = slots.shape[0]
    share = slot_total // parts
    block = min(256, share)
    out = jax.ShapeDtypeStruct((share, matrix.shape[1]), rows.dtype)
    flops = 2 * row_total * matrix.shape[1] * (width + slot_total)
    return pl.pallas_call(
        functools.partial(select_kernel, block, share),
        out_shape=[out] * parts,
        in_specs=[pl.BlockSpec(memory_space=pltpu.VMEM)] * 3,
        out_specs=[pl.BlockSpec(memory_space=pltpu.VMEM)] * parts,
        scratch_shapes=[pltpu.VMEM((row_total, matrix.shape[1]), rows.dtype)],
        cost_estimate=pl.CostEstimate(
            flops=flops,
            bytes_accessed=2 * (rows.size + slot_total * matrix.shape[1]),
            transcendentals=0,
        ),
        compiler_params=pltpu.CompilerParams(vmem_limit_bytes=24 << 20),
    )(rows, matrix, slots)


def static_plan(stem, matrix, turned, cuts):
    groups = lax.axis_size("group")
    group_total, own_rows, width = stem.shape
    mine = group_total // groups
    by_owner = stem.reshape(groups, mine, own_rows, width)
    sums, selected = [], []
    for k in range(mine):
        outgoing = by_owner[:, k]
        if k >= 2:
            outgoing, selected[k - 2] = lax.optimization_barrier((outgoing, selected[k - 2]))
        got = lax.all_to_all(outgoing, "group", split_axis=0, concat_axis=0, tiled=True)
        parts = select(got.reshape(groups * own_rows, width), matrix, turned[k][:, None], cuts)
        selected.append(parts)
    for parts in selected:
        total = parts[-1].astype(jnp.float32)
        for step in range(1, cuts):
            ring = [(i, (i + step) % cuts) for i in range(cuts)]
            total = total + lax.ppermute(parts[step - 1], "cuts", ring).astype(jnp.float32)
        sums.append(total.astype(stem.dtype))
    return jnp.stack(sums, axis=1)


KINDS = 8
LANES = 128


def dot(a, b):
    return jnp.dot(a, b, preferred_element_type=jnp.float32)


def dot_nt(a, b):
    return lax.dot_general(a, b, (((1,), (1,)), ((), ())), preferred_element_type=jnp.float32)


def iota(shape, dim):
    return lax.broadcasted_iota(jnp.int32, shape, dim)


def mark(condition):
    return jnp.where(condition, 1.0, 0.0).astype(jnp.bfloat16)


def needs_kernel(own_rows, capacity, slots_ref, counts_ref, flags_ref):
    mine, slot_total = slots_ref.shape
    side = flags_ref.shape[0]
    hits = jnp.zeros((side, LANES), jnp.float32)
    place = iota((1, slot_total), 1)
    down = iota((side, slot_total), 0)
    across = iota((LANES, slot_total), 0)
    per = LANES // own_rows
    for k in range(mine):
        slots = slots_ref[k : k + 1, :]
        half = jnp.where(place >= slot_total // 2, 2, 0)
        row_key = (slots // own_rows) * KINDS + half + k // per
        row_key = jnp.where(place < counts_ref[k], row_key, -1)
        lane_key = slots % own_rows + (k % per) * own_rows
        hits = hits + dot_nt(mark(down == row_key), mark(across == lane_key))
    flags = jnp.minimum(hits, 1.0)
    row, column = iota((side, side), 0), iota((side, side), 1)
    kind, back = row % KINDS, row - column
    first = (kind == 4) & ((back == 4) | (back == 3))
    second = (kind == 5) & ((back == 3) | (back == 2))
    sums = dot(flags.astype(jnp.bfloat16), jnp.ones((LANES, LANES), jnp.bfloat16))
    counted = dot(mark(first | second), sums.astype(jnp.bfloat16))
    kind = iota((side, LANES), 0) % KINDS
    room = jnp.where(kind == 4, 2.0 * capacity, 1.0 * capacity)
    spill = jnp.max(jnp.where((kind == 4) | (kind == 5), counted - room, 0.0))
    flags_ref[...] = jnp.where(kind == 6, jnp.where(spill > 0.0, 1.0, 0.0), flags)


def needs(slot_rows, counts, own_rows, capacity, groups):
    return pl.pallas_call(
        functools.partial(needs_kernel, own_rows, capacity),
        out_shape=jax.ShapeDtypeStruct((groups * KINDS, LANES), jnp.float32),
        in_specs=[pl.BlockSpec(memory_space=pltpu.VMEM), pl.BlockSpec(memory_space=pltpu.SMEM)],
        out_specs=pl.BlockSpec(memory_space=pltpu.VMEM),
        cost_estimate=pl.CostEstimate(flops=1 << 28, bytes_accessed=1 << 17, transcendentals=0),
    )(slot_rows, counts)


def keys_of(flags):
    side = flags.shape[0]
    marks = flags.astype(jnp.bfloat16)
    lower = mark(iota((LANES, LANES), 0) < iota((LANES, LANES), 1))
    inside = dot(marks, lower)
    totals = dot(marks, jnp.ones((LANES, LANES), jnp.bfloat16))
    row, column = iota((side, side), 0), iota((side, side), 1)
    follows = ((row % KINDS == 1) | (row % KINDS == 3)) & (row - column == 1)
    ranks = inside + dot(mark(follows), totals.astype(jnp.bfloat16))
    return jnp.where(flags > 0.0, ranks, -1.0)


def pack_kernel(capacity, plans, batch, plane_ref, flags_ref, stem_ref, matrix_ref, *refs):
    outs, keys_ref, picked = refs[: len(plans)], refs[-2], refs[-1]
    step = pl.program_id(0)

    @pl.when(step == 0)
    def _():
        keys_ref[...] = keys_of(flags_ref[...])

    plane = plane_ref[0]
    rank = iota((capacity, LANES), 0).astype(jnp.float32)
    for out, plan in zip(outs, plans):
        for i in range(batch):
            keys = keys_ref[pl.ds((step * batch + i) * KINDS, KINDS), :]
            if plan == "early":
                upper, lower = keys[0:1], keys[1:2]
            else:
                second = plane == (0 if plan == "send" else 1)
                upper = jnp.where(second, keys[2:3], keys[0:1] - capacity)
                lower = jnp.where(second, keys[3:4], keys[1:2] - capacity)
            chosen = jnp.concatenate([mark(rank == upper), mark(rank == lower)], axis=1)
            rows = stem_ref[i]
            picked[pl.ds(i * capacity, capacity), :] = dot(chosen, rows).astype(picked.dtype)
        terms = dot(picked[...], matrix_ref[...]).astype(out.dtype)
        out[...] = terms.reshape(out.shape)


def pack(plans, plane, flags, stem, matrix, capacity):
    groups, rows, width = stem.shape
    batch = 4 if groups % 4 == 0 else 1
    out = jax.ShapeDtypeStruct((groups, capacity, matrix.shape[1]), stem.dtype)
    whole = lambda a: pl.BlockSpec(a.shape, lambda i: (0, 0))
    return pl.pallas_call(
        functools.partial(pack_kernel, capacity, plans, batch),
        grid=(groups // batch,),
        out_shape=[out] * len(plans),
        in_specs=[
            pl.BlockSpec(memory_space=pltpu.SMEM),
            whole(flags),
            pl.BlockSpec((batch, rows, width), lambda i: (i, 0, 0)),
            whole(matrix),
        ],
        out_specs=[pl.BlockSpec((batch, capacity, matrix.shape[1]), lambda i: (i, 0, 0))] * len(plans),
        scratch_shapes=[
            pltpu.VMEM(flags.shape, jnp.float32),
            pltpu.VMEM((batch * capacity, width), stem.dtype),
        ],
        cost_estimate=pl.CostEstimate(
            flops=len(plans) * 2 * groups * capacity * (rows + width) * width,
            bytes_accessed=2 * stem.size,
            transcendentals=0,
        ),
        compiler_params=pltpu.CompilerParams(vmem_limit_bytes=24 << 20),
    )(plane, flags, stem, matrix)


def places_kernel(own_rows, capacity, plane_ref, slots_ref, places_ref):
    mine, share = slots_ref.shape
    rows = mine * own_rows
    down = iota((own_rows, share), 0)
    across = iota((LANES, share), 0)
    wanted = []
    for k in range(mine):
        slots = slots_ref[k : k + 1, :]
        source = jnp.where(slots >= 0, slots // own_rows, -1)
        wanted.append(dot_nt(mark(down == slots % own_rows), mark(across == source)))
    wanted = jnp.minimum(jnp.concatenate(wanted, axis=0), 1.0)
    before = mark(iota((rows, rows), 0) > iota((rows, rows), 1))
    ranks = dot(before, wanted.astype(jnp.bfloat16))
    shift = (plane_ref[0] * capacity).astype(jnp.float32)
    places_ref[...] = jnp.where(wanted > 0.0, ranks + shift, -1.0)


def places(plane, own_slots, own_rows, capacity):
    return pl.pallas_call(
        functools.partial(places_kernel, own_rows, capacity),
        out_shape=jax.ShapeDtypeStruct((own_slots.shape[0] * own_rows, LANES), jnp.float32),
        in_specs=[pl.BlockSpec(memory_space=pltpu.SMEM), pl.BlockSpec(memory_space=pltpu.VMEM)],
        out_specs=pl.BlockSpec(memory_space=pltpu.VMEM),
        cost_estimate=pl.CostEstimate(flops=1 << 28, bytes_accessed=1 << 17, transcendentals=0),
    )(plane, own_slots)


def spread_kernel(own_rows, places_ref, slots_ref, early_ref, late_ref, out_ref, table):
    groups, capacity, width = early_ref.shape
    mine, row_total, _ = table.shape
    share = slots_ref.shape[0] // mine
    rank = iota((mine * own_rows, 2 * capacity), 1).astype(jnp.float32)
    for s in range(groups):
        chosen = mark(rank == places_ref[:, s : s + 1])
        rows = dot(chosen[:, :capacity], early_ref[s]) + dot(chosen[:, capacity:], late_ref[s])
        table[:, s * own_rows : (s + 1) * own_rows, :] = rows.astype(table.dtype).reshape(mine, own_rows, width)
    block = min(256, share)
    columns = iota((block, row_total), 1)
    for k in range(mine):
        for start in range(0, share, block):
            chosen = mark(columns == slots_ref[pl.ds(k * share + start, block), :])
            out_ref[k, pl.ds(start, block), :] = dot(chosen, table[k]).astype(out_ref.dtype)


def spread(where, slots, early, late, own_rows):
    groups, capacity, width = early.shape
    mine = where.shape[0] // own_rows
    share = slots.shape[0] // mine
    return pl.pallas_call(
        functools.partial(spread_kernel, own_rows),
        out_shape=jax.ShapeDtypeStruct((mine, share, width), early.dtype),
        in_specs=[pl.BlockSpec(memory_space=pltpu.VMEM)] * 4,
        out_specs=pl.BlockSpec(memory_space=pltpu.VMEM),
        scratch_shapes=[pltpu.VMEM((mine, groups * own_rows, width), early.dtype)],
        cost_estimate=pl.CostEstimate(
            flops=4 * mine * share * groups * own_rows * width,
            bytes_accessed=4 * early.size,
            transcendentals=0,
        ),
        compiler_params=pltpu.CompilerParams(vmem_limit_bytes=32 << 20),
    )(where, slots, early, late)


def exchange(blocks):
    return lax.all_to_all(blocks, "group", split_axis=0, concat_axis=0, tiled=True)


def needed_plan(stem, matrix, flags, own_slots, capacity):
    groups = lax.axis_size("group")
    group_total, own_rows, width = stem.shape
    mine = group_total // groups
    plane = lax.axis_index("cuts").astype(jnp.int32)[None]
    by_owner = stem.reshape(groups, mine * own_rows, width)
    (early,) = pack(("early",), plane, flags, by_owner, matrix, capacity)
    send, keep = pack(("send", "keep"), plane, flags, by_owner, matrix, capacity)
    where = places(plane, own_slots, own_rows, capacity)
    columns = own_slots.reshape(-1, 1)

    early = exchange(early)
    late = keep.astype(jnp.float32) + lax.ppermute(send, "cuts", [(0, 1), (1, 0)]).astype(jnp.float32)
    late = exchange(late.astype(stem.dtype))
    early = early.astype(jnp.float32) + lax.ppermute(early, "cuts", [(1, 0)]).astype(jnp.float32)
    out = spread(where, columns, early.astype(stem.dtype), late, own_rows)
    return jnp.transpose(out, (1, 0, 2))


def local(stem_blocks, cap_tensor, slot_rows, counts):
    cuts, groups = lax.axis_size("cuts"), lax.axis_size("group")
    stem = stem_blocks[0]
    group_total, own_rows, width = stem.shape
    mine = group_total // groups
    slot_total = slot_rows.shape[1]
    share = slot_total // cuts
    matrix = build_matrix(cap_tensor[0])

    positions = jnp.arange(slot_total, dtype=jnp.int32)
    marked = jnp.where(positions[None, :] < counts[:, None], slot_rows, -1)
    me = lax.axis_index("cuts")
    doubled = jnp.concatenate([marked, marked], axis=1)
    turned = lax.dynamic_slice_in_dim(doubled, (me + 1) * share, slot_total, 1)

    if cuts != 2 or mine * own_rows != 2 * LANES or LANES % own_rows or groups > LANES:
        return static_plan(stem, matrix, turned, cuts)
    capacity = mine * own_rows // 4
    flags = needs(slot_rows, counts, own_rows, capacity, groups)
    flags = exchange(flags.reshape(groups, KINDS, LANES))
    spilled = jnp.max(flags[:, 6, :]) > 0.0
    flags = flags.reshape(groups * KINDS, LANES)
    return lax.cond(
        spilled,
        lambda: static_plan(stem, matrix, turned, cuts),
        lambda: needed_plan(stem, matrix, flags, turned[:, (cuts - 1) * share :], capacity),
    )


def solution(mesh):
    in_specs = (
        P("cuts", None, "group", None),
        P("cuts", None, None, None),
        P("group", None),
        P("group"),
    )
    out_specs = P("cuts", "group", None)
    return jax.shard_map(local, mesh=mesh, in_specs=in_specs, out_specs=out_specs, check_vma=False)
```

```python
import functools

import jax
import jax.numpy as jnp
from jax import lax
from jax.experimental import pallas as pl
from jax.experimental.pallas import tpu as pltpu
from jax.sharding import PartitionSpec as P


def build_matrix(cap_pair):
    real_part = cap_pair[0]
    imag_part = cap_pair[1]
    upper = jnp.concatenate([real_part, imag_part], axis=1)
    lower = jnp.concatenate([-imag_part, real_part], axis=1)
    return jnp.concatenate([upper, lower], axis=0)


def terms_kernel(rows_ref, matrix_ref, out_ref):
    out_ref[...] = dot(rows_ref[...], matrix_ref[...]).astype(out_ref.dtype)


def terms_of(rows, matrix):
    total, width = rows.shape
    block = min(1024, total)
    return pl.pallas_call(
        terms_kernel,
        grid=(total // block,),
        out_shape=jax.ShapeDtypeStruct((total, matrix.shape[1]), rows.dtype),
        in_specs=[pl.BlockSpec((block, width), lambda i: (i, 0)), pl.BlockSpec(matrix.shape, lambda i: (0, 0))],
        out_specs=pl.BlockSpec((block, matrix.shape[1]), lambda i: (i, 0)),
        cost_estimate=pl.CostEstimate(
            flops=2 * total * width * matrix.shape[1], bytes_accessed=4 * rows.size, transcendentals=0
        ),
    )(rows, matrix)


def select_kernel(block, share, terms_ref, slots_ref, *outs):
    columns = iota((block, terms_ref.shape[0]), 1)
    for part, out in enumerate(outs):
        for start in range(0, share, block):
            chosen = mark(columns == slots_ref[pl.ds(part * share + start, block), :])
            out[pl.ds(start, block), :] = dot(chosen, terms_ref[...]).astype(out.dtype)


def select(terms, slots, parts):
    row_total, width = terms.shape
    slot_total = slots.shape[0]
    share = slot_total // parts
    return pl.pallas_call(
        functools.partial(select_kernel, min(256, share), share),
        out_shape=[jax.ShapeDtypeStruct((share, width), terms.dtype)] * parts,
        in_specs=[pl.BlockSpec(memory_space=pltpu.VMEM)] * 2,
        out_specs=[pl.BlockSpec(memory_space=pltpu.VMEM)] * parts,
        cost_estimate=pl.CostEstimate(
            flops=2 * row_total * width * slot_total,
            bytes_accessed=2 * (terms.size + slot_total * width),
            transcendentals=0,
        ),
        compiler_params=pltpu.CompilerParams(vmem_limit_bytes=24 << 20),
    )(terms, slots)


def static_plan(terms, turned, cuts):
    groups = lax.axis_size("group")
    group_total, own_rows, width = terms.shape
    mine = group_total // groups
    by_owner = terms.reshape(groups, mine, own_rows, width)
    sums, selected = [], []
    for k in range(mine):
        outgoing = by_owner[:, k]
        if k >= 2:
            outgoing, selected[k - 2] = lax.optimization_barrier((outgoing, selected[k - 2]))
        got = lax.all_to_all(outgoing, "group", split_axis=0, concat_axis=0, tiled=True)
        parts = select(got.reshape(groups * own_rows, width), turned[k][:, None], cuts)
        selected.append(parts)
    for parts in selected:
        total = parts[-1].astype(jnp.float32)
        for step in range(1, cuts):
            ring = [(i, (i + step) % cuts) for i in range(cuts)]
            total = total + lax.ppermute(parts[step - 1], "cuts", ring).astype(jnp.float32)
        sums.append(total.astype(terms.dtype))
    return jnp.stack(sums, axis=1)


KINDS = 8
LANES = 128


def dot(a, b):
    return jnp.dot(a, b, preferred_element_type=jnp.float32)


def dot_nt(a, b):
    return lax.dot_general(a, b, (((1,), (1,)), ((), ())), preferred_element_type=jnp.float32)


def iota(shape, dim):
    return lax.broadcasted_iota(jnp.int32, shape, dim)


def mark(condition):
    return jnp.where(condition, 1.0, 0.0).astype(jnp.bfloat16)


def needs_kernel(own_rows, capacity, slots_ref, counts_ref, flags_ref):
    mine, slot_total = slots_ref.shape
    side = flags_ref.shape[0]
    hits = jnp.zeros((side, LANES), jnp.float32)
    place = iota((1, slot_total), 1)
    down = iota((side, slot_total), 0)
    across = iota((LANES, slot_total), 0)
    per = LANES // own_rows
    for k in range(mine):
        slots = slots_ref[k : k + 1, :]
        half = jnp.where(place >= slot_total // 2, 2, 0)
        row_key = (slots // own_rows) * KINDS + half + k // per
        row_key = jnp.where(place < counts_ref[k], row_key, -1)
        lane_key = slots % own_rows + (k % per) * own_rows
        hits = hits + dot_nt(mark(down == row_key), mark(across == lane_key))
    flags = jnp.minimum(hits, 1.0)
    row, column = iota((side, side), 0), iota((side, side), 1)
    kind, back = row % KINDS, row - column
    first = (kind == 4) & ((back == 4) | (back == 3))
    second = (kind == 5) & ((back == 3) | (back == 2))
    sums = dot(flags.astype(jnp.bfloat16), jnp.ones((LANES, LANES), jnp.bfloat16))
    counted = dot(mark(first | second), sums.astype(jnp.bfloat16))
    kind = iota((side, LANES), 0) % KINDS
    room = jnp.where(kind == 4, 2.0 * capacity, 1.0 * capacity)
    spill = jnp.max(jnp.where((kind == 4) | (kind == 5), counted - room, 0.0))
    flags_ref[...] = jnp.where(kind == 6, jnp.where(spill > 0.0, 1.0, 0.0), flags).astype(flags_ref.dtype)


def needs(slot_rows, counts, own_rows, capacity, groups):
    return pl.pallas_call(
        functools.partial(needs_kernel, own_rows, capacity),
        out_shape=jax.ShapeDtypeStruct((groups * KINDS, LANES), jnp.bfloat16),
        in_specs=[pl.BlockSpec(memory_space=pltpu.VMEM), pl.BlockSpec(memory_space=pltpu.SMEM)],
        out_specs=pl.BlockSpec(memory_space=pltpu.VMEM),
        cost_estimate=pl.CostEstimate(flops=1 << 28, bytes_accessed=1 << 17, transcendentals=0),
    )(slot_rows, counts)


def keys_of(flags):
    side = flags.shape[0]
    marks = flags
    lower = mark(iota((LANES, LANES), 0) < iota((LANES, LANES), 1))
    inside = dot(marks, lower)
    totals = dot(marks, jnp.ones((LANES, LANES), jnp.bfloat16))
    row, column = iota((side, side), 0), iota((side, side), 1)
    follows = ((row % KINDS == 1) | (row % KINDS == 3)) & (row - column == 1)
    ranks = inside + dot(mark(follows), totals.astype(jnp.bfloat16))
    return jnp.where(flags.astype(jnp.float32) > 0.0, ranks, -1.0)


def pack_kernel(plane_ref, flags_ref, terms_ref, early_ref, send_ref, keep_ref, keys_ref):
    groups, capacity, _ = early_ref.shape
    keys_ref[...] = keys_of(flags_ref[...])
    rank = iota((capacity, LANES), 0).astype(jnp.float32)

    def one(upper, lower):
        return jnp.concatenate([mark(rank == upper), mark(rank == lower)], axis=1)

    plane = plane_ref[0]
    for d in range(groups):
        keys = keys_ref[d * KINDS : (d + 1) * KINDS, :]
        first, second = (keys[0:1], keys[1:2]), (keys[2:3], keys[3:4])
        beyond = tuple(key - capacity for key in first)
        sent = [jnp.where(plane == 0, b, a) for a, b in zip(beyond, second)]
        kept = [jnp.where(plane == 0, a, b) for a, b in zip(beyond, second)]
        chosen = jnp.concatenate([one(*first), one(*sent), one(*kept)], axis=0)
        packed = dot(chosen, terms_ref[d]).astype(early_ref.dtype)
        early_ref[d] = packed[:capacity]
        send_ref[d] = packed[capacity : 2 * capacity]
        keep_ref[d] = packed[2 * capacity :]


def pack(plane, flags, terms, capacity):
    groups, rows, width = terms.shape
    vmem = pl.BlockSpec(memory_space=pltpu.VMEM)
    return pl.pallas_call(
        pack_kernel,
        out_shape=[jax.ShapeDtypeStruct((groups, capacity, width), terms.dtype)] * 3,
        in_specs=[pl.BlockSpec(memory_space=pltpu.SMEM), vmem, vmem],
        out_specs=[vmem] * 3,
        scratch_shapes=[pltpu.VMEM(flags.shape, jnp.float32)],
        cost_estimate=pl.CostEstimate(
            flops=6 * groups * capacity * rows * width, bytes_accessed=4 * terms.size, transcendentals=0
        ),
        compiler_params=pltpu.CompilerParams(vmem_limit_bytes=24 << 20),
    )(plane, flags, terms)


def places_kernel(own_rows, capacity, plane_ref, slots_ref, column_ref, early_ref, late_ref):
    mine, share = slots_ref.shape
    rows = mine * own_rows
    down = iota((own_rows, share), 0)
    across = iota((LANES, share), 0)
    wanted = []
    for k in range(mine):
        slots = slots_ref[k : k + 1, :]
        source = jnp.where(slots >= 0, slots // own_rows, -1)
        wanted.append(dot_nt(mark(down == slots % own_rows), mark(across == source)))
    wanted = jnp.minimum(jnp.concatenate(wanted, axis=0), 1.0)
    before = mark(iota((rows, rows), 0) > iota((rows, rows), 1))
    ranks = dot(before, wanted.astype(jnp.bfloat16)).astype(jnp.bfloat16)
    shift = plane_ref[0] * capacity
    block = min(512, column_ref.shape[0])
    group = iota((block, 1), 0) % mine
    for start in range(0, column_ref.shape[0], block):
        slots = column_ref[pl.ds(start, block), :]
        source = slots // own_rows
        row = jnp.where(slots >= 0, group * own_rows + slots % own_rows, -1)
        looked = dot(mark(iota((block, rows), 1) == row), ranks)
        found = jnp.where(iota((block, LANES), 1) == source, looked, 0.0)
        rank = jnp.sum(found, axis=1, keepdims=True).astype(jnp.int32) + shift
        base = source * capacity
        live = slots >= 0
        early_ref[pl.ds(start, block), :] = jnp.where(live & (rank < capacity), base + rank, -1)
        late_ref[pl.ds(start, block), :] = jnp.where(live & (rank >= capacity), base + rank - capacity, -1)


def places(plane, own_slots, own_rows, capacity):
    column = own_slots.T.reshape(-1, 1)
    vmem = pl.BlockSpec(memory_space=pltpu.VMEM)
    return pl.pallas_call(
        functools.partial(places_kernel, own_rows, capacity),
        out_shape=[jax.ShapeDtypeStruct(column.shape, jnp.int32)] * 2,
        in_specs=[pl.BlockSpec(memory_space=pltpu.SMEM), vmem, vmem],
        out_specs=[vmem] * 2,
        cost_estimate=pl.CostEstimate(flops=1 << 28, bytes_accessed=1 << 20, transcendentals=0),
    )(plane, own_slots, column)


def early_kernel(places_ref, own_ref, other_ref, out_ref, table):
    groups, capacity, width = own_ref.shape
    both = own_ref[...].astype(jnp.float32) + other_ref[...].astype(jnp.float32)
    table[...] = both.astype(table.dtype).reshape(table.shape)
    block = min(256, out_ref.shape[0])
    columns = iota((block, groups * capacity), 1)
    for start in range(0, out_ref.shape[0], block):
        chosen = mark(columns == places_ref[pl.ds(start, block), :])
        out_ref[pl.ds(start, block), :] = dot(chosen, table[...]).astype(out_ref.dtype)


def late_kernel(places_ref, late_ref, early_ref, out_ref):
    rows, width = early_ref.shape
    share, mine, _ = out_ref.shape
    block = min(256, rows)
    columns = iota((block, late_ref.shape[0]), 1)
    for start in range(0, rows, block):
        chosen = mark(columns == places_ref[pl.ds(start, block), :])
        total = dot(chosen, late_ref[...]) + early_ref[pl.ds(start, block), :].astype(jnp.float32)
        out_ref[pl.ds(start // mine, block // mine)] = total.astype(out_ref.dtype).reshape(block // mine, mine, width)


def early_part(where, own, other):
    groups, capacity, width = own.shape
    vmem = pl.BlockSpec(memory_space=pltpu.VMEM)
    return pl.pallas_call(
        early_kernel,
        out_shape=jax.ShapeDtypeStruct((where.shape[0], width), own.dtype),
        in_specs=[vmem] * 3,
        out_specs=vmem,
        scratch_shapes=[pltpu.VMEM((groups * capacity, width), own.dtype)],
        cost_estimate=pl.CostEstimate(
            flops=2 * where.shape[0] * groups * capacity * width, bytes_accessed=6 * own.size, transcendentals=0
        ),
        compiler_params=pltpu.CompilerParams(vmem_limit_bytes=24 << 20),
    )(where, own, other)


def late_part(where, late, early, mine):
    rows, width = early.shape
    vmem = pl.BlockSpec(memory_space=pltpu.VMEM)
    return pl.pallas_call(
        late_kernel,
        out_shape=jax.ShapeDtypeStruct((rows // mine, mine, width), early.dtype),
        in_specs=[vmem] * 3,
        out_specs=vmem,
        cost_estimate=pl.CostEstimate(
            flops=2 * rows * late.shape[0] * width, bytes_accessed=4 * late.size, transcendentals=0
        ),
        compiler_params=pltpu.CompilerParams(vmem_limit_bytes=24 << 20),
    )(where, late, early)


def exchange(blocks):
    return lax.all_to_all(blocks, "group", split_axis=0, concat_axis=0, tiled=True)


def needed_plan(terms, flags, own_slots, capacity):
    groups = lax.axis_size("group")
    group_total, own_rows, width = terms.shape
    mine = group_total // groups
    plane = lax.axis_index("cuts").astype(jnp.int32)[None]
    early, send, keep = pack(plane, flags, terms.reshape(groups, mine * own_rows, width), capacity)
    late = keep.astype(jnp.float32) + lax.ppermute(send, "cuts", [(0, 1), (1, 0)]).astype(jnp.float32)
    early = exchange(early)
    other = lax.ppermute(early, "cuts", [(1, 0)])
    late = exchange(late.astype(terms.dtype))
    where_early, where_late = places(plane, own_slots, own_rows, capacity)
    out = early_part(where_early, early, other)
    return late_part(where_late, late.reshape(groups * capacity, width), out, mine)


def local(stem_blocks, cap_tensor, slot_rows, counts):
    cuts, groups = lax.axis_size("cuts"), lax.axis_size("group")
    group_total, own_rows, width = stem_blocks.shape[1:]
    mine = group_total // groups
    slot_total = slot_rows.shape[1]
    share = slot_total // cuts
    matrix = build_matrix(cap_tensor[0])
    terms = terms_of(stem_blocks.reshape(group_total * own_rows, width), matrix)
    terms = terms.reshape(group_total, own_rows, matrix.shape[1])

    positions = jnp.arange(slot_total, dtype=jnp.int32)
    marked = jnp.where(positions[None, :] < counts[:, None], slot_rows, -1)
    me = lax.axis_index("cuts")
    doubled = jnp.concatenate([marked, marked], axis=1)
    turned = lax.dynamic_slice_in_dim(doubled, (me + 1) * share, slot_total, 1)

    if cuts != 2 or mine * own_rows != 2 * LANES or LANES % own_rows or groups > LANES:
        return static_plan(terms, turned, cuts)
    capacity = mine * own_rows // 4
    flags = needs(slot_rows, counts, own_rows, capacity, groups)
    flags = exchange(flags.reshape(groups, KINDS, LANES))
    spilled = jnp.max(flags[:, 6, :].astype(jnp.float32)) > 0.0
    flags = flags.reshape(groups * KINDS, LANES)
    return lax.cond(
        spilled,
        lambda: static_plan(terms, turned, cuts),
        lambda: needed_plan(terms, flags, turned[:, (cuts - 1) * share :], capacity),
    )


def solution(mesh):
    in_specs = (
        P("cuts", None, "group", None),
        P("cuts", None, None, None),
        P("group", None),
        P("group"),
    )
    out_specs = P("cuts", "group", None)
    return jax.shard_map(local, mesh=mesh, in_specs=in_specs, out_specs=out_specs, check_vma=False)
```

```python
import functools

import jax
import jax.numpy as jnp
from jax import lax
from jax.experimental import pallas as pl
from jax.experimental.pallas import tpu as pltpu
from jax.sharding import PartitionSpec as P


def terms_kernel(rows_ref, pair_ref, out_ref, matrix):
    half = pair_ref.shape[1]

    @pl.when(pl.program_id(0) == 0)
    def _():
        real_part, imag_part = pair_ref[0], pair_ref[1]
        matrix[:half, :half] = real_part
        matrix[:half, half:] = imag_part
        matrix[half:, :half] = -imag_part
        matrix[half:, half:] = real_part

    out_ref[...] = dot(rows_ref[...], matrix[...]).astype(out_ref.dtype)


def terms_of(rows, pair):
    total, width = rows.shape
    block = min(512, total)
    out_width = 2 * pair.shape[2]
    return pl.pallas_call(
        terms_kernel,
        grid=(total // block,),
        out_shape=jax.ShapeDtypeStruct((total, out_width), rows.dtype),
        in_specs=[pl.BlockSpec((block, width), lambda i: (i, 0)), pl.BlockSpec(pair.shape, lambda i: (0, 0, 0))],
        out_specs=pl.BlockSpec((block, out_width), lambda i: (i, 0)),
        scratch_shapes=[pltpu.VMEM((width, out_width), rows.dtype)],
        cost_estimate=pl.CostEstimate(
            flops=2 * total * width * out_width, bytes_accessed=4 * rows.size, transcendentals=0
        ),
    )(rows, pair)


def select_kernel(block, share, terms_ref, slots_ref, *outs):
    columns = iota((block, terms_ref.shape[0]), 1)
    for part, out in enumerate(outs):
        for start in range(0, share, block):
            chosen = mark(columns == slots_ref[pl.ds(part * share + start, block), :])
            out[pl.ds(start, block), :] = dot(chosen, terms_ref[...]).astype(out.dtype)


def select(terms, slots, parts):
    row_total, width = terms.shape
    slot_total = slots.shape[0]
    share = slot_total // parts
    return pl.pallas_call(
        functools.partial(select_kernel, min(256, share), share),
        out_shape=[jax.ShapeDtypeStruct((share, width), terms.dtype)] * parts,
        in_specs=[pl.BlockSpec(memory_space=pltpu.VMEM)] * 2,
        out_specs=[pl.BlockSpec(memory_space=pltpu.VMEM)] * parts,
        cost_estimate=pl.CostEstimate(
            flops=2 * row_total * width * slot_total,
            bytes_accessed=2 * (terms.size + slot_total * width),
            transcendentals=0,
        ),
        compiler_params=pltpu.CompilerParams(vmem_limit_bytes=24 << 20),
    )(terms, slots)


def static_plan(terms, turned, cuts):
    groups = lax.axis_size("group")
    group_total, own_rows, width = terms.shape
    mine = group_total // groups
    by_owner = terms.reshape(groups, mine, own_rows, width)
    sums, selected = [], []
    for k in range(mine):
        outgoing = by_owner[:, k]
        if k >= 2:
            outgoing, selected[k - 2] = lax.optimization_barrier((outgoing, selected[k - 2]))
        got = lax.all_to_all(outgoing, "group", split_axis=0, concat_axis=0, tiled=True)
        parts = select(got.reshape(groups * own_rows, width), turned[k][:, None], cuts)
        selected.append(parts)
    for parts in selected:
        total = parts[-1].astype(jnp.float32)
        for step in range(1, cuts):
            ring = [(i, (i + step) % cuts) for i in range(cuts)]
            total = total + lax.ppermute(parts[step - 1], "cuts", ring).astype(jnp.float32)
        sums.append(total.astype(terms.dtype))
    return jnp.stack(sums, axis=1)


KINDS = 8
LANES = 128
EARLY, LATE = 56, 72


def dot(a, b):
    return jnp.dot(a, b, preferred_element_type=jnp.float32)


def dot_nt(a, b):
    return lax.dot_general(a, b, (((1,), (1,)), ((), ())), preferred_element_type=jnp.float32)


def iota(shape, dim):
    return lax.broadcasted_iota(jnp.int32, shape, dim)


def mark(condition):
    return jnp.where(condition, 1.0, 0.0).astype(jnp.bfloat16)


def needs_kernel(own_rows, early, late, slots_ref, counts_ref, flags_ref):
    mine, slot_total = slots_ref.shape
    side = flags_ref.shape[0]
    hits = jnp.zeros((side, LANES), jnp.float32)
    place = iota((1, slot_total), 1)
    down = iota((side, slot_total), 0)
    across = iota((LANES, slot_total), 0)
    per = LANES // own_rows
    for k in range(mine):
        slots = slots_ref[k : k + 1, :]
        half = jnp.where(place >= slot_total // 2, 2, 0)
        row_key = (slots // own_rows) * KINDS + half + k // per
        row_key = jnp.where(place < counts_ref[k], row_key, -1)
        lane_key = slots % own_rows + (k % per) * own_rows
        hits = hits + dot_nt(mark(down == row_key), mark(across == lane_key))
    flags = jnp.minimum(hits, 1.0)
    row, column = iota((side, side), 0), iota((side, side), 1)
    kind, back = row % KINDS, row - column
    first = (kind == 4) & ((back == 4) | (back == 3))
    second = (kind == 5) & ((back == 3) | (back == 2))
    sums = dot(flags.astype(jnp.bfloat16), jnp.ones((LANES, LANES), jnp.bfloat16))
    counted = dot(mark(first | second), sums.astype(jnp.bfloat16))
    kind = iota((side, LANES), 0) % KINDS
    room = jnp.where(kind == 4, 1.0 * (early + late), 1.0 * late)
    spill = jnp.max(jnp.where((kind == 4) | (kind == 5), counted - room, 0.0))
    flags_ref[...] = jnp.where(kind == 6, jnp.where(spill > 0.0, 1.0, 0.0), flags).astype(flags_ref.dtype)


def needs(slot_rows, counts, own_rows, early, late, groups):
    return pl.pallas_call(
        functools.partial(needs_kernel, own_rows, early, late),
        out_shape=jax.ShapeDtypeStruct((groups * KINDS, LANES), jnp.bfloat16),
        in_specs=[pl.BlockSpec(memory_space=pltpu.VMEM), pl.BlockSpec(memory_space=pltpu.SMEM)],
        out_specs=pl.BlockSpec(memory_space=pltpu.VMEM),
        cost_estimate=pl.CostEstimate(flops=1 << 28, bytes_accessed=1 << 17, transcendentals=0),
    )(slot_rows, counts)


def keys_of(flags):
    side = flags.shape[0]
    marks = flags
    lower = mark(iota((LANES, LANES), 0) < iota((LANES, LANES), 1))
    inside = dot(marks, lower)
    totals = dot(marks, jnp.ones((LANES, LANES), jnp.bfloat16))
    row, column = iota((side, side), 0), iota((side, side), 1)
    follows = ((row % KINDS == 1) | (row % KINDS == 3)) & (row - column == 1)
    ranks = inside + dot(mark(follows), totals.astype(jnp.bfloat16))
    return jnp.where(flags.astype(jnp.float32) > 0.0, ranks, -1.0)


def chosen_rows(capacity, upper, lower):
    rank = iota((capacity, LANES), 0).astype(jnp.float32)
    return jnp.concatenate([mark(rank == upper), mark(rank == lower)], axis=1)


def pack_late_kernel(first_rank, plane_ref, flags_ref, terms_ref, send_ref, keep_ref, keys_ref):
    batch, capacity, _ = send_ref.shape
    step = pl.program_id(0)

    @pl.when(step == 0)
    def _():
        keys_ref[...] = keys_of(flags_ref[...])

    plane = plane_ref[0]
    for i in range(batch):
        keys = keys_ref[pl.ds((step * batch + i) * KINDS, KINDS), :]
        second = keys[2:3], keys[3:4]
        beyond = keys[0:1] - first_rank, keys[1:2] - first_rank
        sent = [jnp.where(plane == 0, b, a) for a, b in zip(beyond, second)]
        kept = [jnp.where(plane == 0, a, b) for a, b in zip(beyond, second)]
        chosen = jnp.concatenate([chosen_rows(capacity, *sent), chosen_rows(capacity, *kept)], axis=0)
        packed = dot(chosen, terms_ref[i]).astype(send_ref.dtype)
        send_ref[i] = packed[:capacity]
        keep_ref[i] = packed[capacity:]


def pack_late(plane, flags, terms, first_rank, capacity):
    groups, rows, width = terms.shape
    batch = 4 if groups % 4 == 0 else 1
    out = jax.ShapeDtypeStruct((groups, capacity, width), terms.dtype)
    block = pl.BlockSpec((batch, capacity, width), lambda i: (i, 0, 0))
    table = pl.BlockSpec(flags.shape, lambda i: (0, 0))
    return pl.pallas_call(
        functools.partial(pack_late_kernel, first_rank),
        grid=(groups // batch,),
        out_shape=[out, out, jax.ShapeDtypeStruct(flags.shape, jnp.float32)],
        in_specs=[
            pl.BlockSpec(memory_space=pltpu.SMEM),
            table,
            pl.BlockSpec((batch, rows, width), lambda i: (i, 0, 0)),
        ],
        out_specs=[block, block, table],
        cost_estimate=pl.CostEstimate(
            flops=4 * groups * capacity * rows * width, bytes_accessed=4 * terms.size, transcendentals=0
        ),
    )(plane, flags, terms)


def pack_early_kernel(keys_ref, terms_ref, out_ref):
    batch, capacity, _ = out_ref.shape
    step = pl.program_id(0)
    for i in range(batch):
        keys = keys_ref[pl.ds((step * batch + i) * KINDS, KINDS), :]
        chosen = chosen_rows(capacity, keys[0:1], keys[1:2])
        out_ref[i] = dot(chosen, terms_ref[i]).astype(out_ref.dtype)


def pack_early(keys, terms, capacity):
    groups, rows, width = terms.shape
    batch = 4 if groups % 4 == 0 else 1
    return pl.pallas_call(
        pack_early_kernel,
        grid=(groups // batch,),
        out_shape=jax.ShapeDtypeStruct((groups, capacity, width), terms.dtype),
        in_specs=[
            pl.BlockSpec(keys.shape, lambda i: (0, 0)),
            pl.BlockSpec((batch, rows, width), lambda i: (i, 0, 0)),
        ],
        out_specs=pl.BlockSpec((batch, capacity, width), lambda i: (i, 0, 0)),
        cost_estimate=pl.CostEstimate(
            flops=2 * groups * capacity * rows * width, bytes_accessed=3 * terms.size, transcendentals=0
        ),
    )(keys, terms)


def places_kernel(own_rows, early, late, plane_ref, slots_ref, column_ref, early_ref, late_ref):
    mine, share = slots_ref.shape
    rows = mine * own_rows
    down = iota((own_rows, share), 0)
    across = iota((LANES, share), 0)
    wanted = []
    for k in range(mine):
        slots = slots_ref[k : k + 1, :]
        source = jnp.where(slots >= 0, slots // own_rows, -1)
        wanted.append(dot_nt(mark(down == slots % own_rows), mark(across == source)))
    wanted = jnp.minimum(jnp.concatenate(wanted, axis=0), 1.0)
    before = mark(iota((rows, rows), 0) > iota((rows, rows), 1))
    ranks = dot(before, wanted.astype(jnp.bfloat16)).astype(jnp.bfloat16)
    shift = plane_ref[0] * early
    group = iota((LANES, 1), 0) % mine
    lane = iota((LANES, LANES), 1)
    in_early = jnp.full((LANES, LANES), -1, jnp.int32)
    in_late = in_early
    for block in range(mine * share // LANES):
        slots = column_ref[:, block : block + 1]
        source = slots // own_rows
        row = jnp.where(slots >= 0, group * own_rows + slots % own_rows, -1)
        looked = dot(mark(iota((LANES, rows), 1) == row), ranks)
        found = jnp.where(lane == source, looked, 0.0)
        rank = jnp.sum(found, axis=1, keepdims=True).astype(jnp.int32) + shift
        live, low = slots >= 0, rank < early
        in_early = jnp.where((lane == block) & live & low, source * early + rank, in_early)
        in_late = jnp.where((lane == block) & live & ~low, source * late + rank - early, in_late)
    early_ref[...] = in_early
    late_ref[...] = in_late


def places(plane, own_slots, own_rows, early, late):
    column = own_slots.T.reshape(-1, LANES).T
    vmem = pl.BlockSpec(memory_space=pltpu.VMEM)
    return pl.pallas_call(
        functools.partial(places_kernel, own_rows, early, late),
        out_shape=[jax.ShapeDtypeStruct((LANES, LANES), jnp.int32)] * 2,
        in_specs=[pl.BlockSpec(memory_space=pltpu.SMEM), vmem, vmem],
        out_specs=[vmem] * 2,
        cost_estimate=pl.CostEstimate(flops=1 << 28, bytes_accessed=1 << 18, transcendentals=0),
    )(plane, own_slots, column)


def early_kernel(places_ref, own_ref, other_ref, out_ref, table):
    both = own_ref[...].astype(jnp.float32) + other_ref[...].astype(jnp.float32)
    table[...] = both.astype(table.dtype)
    columns = iota((LANES, table.shape[0]), 1)
    for block in range(out_ref.shape[0] // LANES):
        chosen = mark(columns == places_ref[:, block : block + 1])
        out_ref[block * LANES : (block + 1) * LANES, :] = dot(chosen, table[...]).astype(out_ref.dtype)


def late_kernel(places_ref, late_ref, early_ref, out_ref):
    rows, width = early_ref.shape
    share, mine, _ = out_ref.shape
    per = LANES // mine
    columns = iota((LANES, late_ref.shape[0]), 1)
    for block in range(rows // LANES):
        chosen = mark(columns == places_ref[:, block : block + 1])
        early = early_ref[block * LANES : (block + 1) * LANES, :].astype(jnp.float32)
        total = (dot(chosen, late_ref[...]) + early).astype(out_ref.dtype)
        out_ref[block * per : (block + 1) * per] = total.reshape(per, mine, width)


def early_part(where, own, other, slots):
    rows, width = own.shape
    vmem = pl.BlockSpec(memory_space=pltpu.VMEM)
    return pl.pallas_call(
        early_kernel,
        out_shape=jax.ShapeDtypeStruct((slots, width), own.dtype),
        in_specs=[vmem] * 3,
        out_specs=vmem,
        scratch_shapes=[pltpu.VMEM((rows, width), own.dtype)],
        cost_estimate=pl.CostEstimate(
            flops=2 * slots * rows * width, bytes_accessed=6 * own.size, transcendentals=0
        ),
        compiler_params=pltpu.CompilerParams(vmem_limit_bytes=12 << 20),
    )(where, own, other)


def late_part(where, late, early, mine):
    rows, width = early.shape
    vmem = pl.BlockSpec(memory_space=pltpu.VMEM)
    return pl.pallas_call(
        late_kernel,
        out_shape=jax.ShapeDtypeStruct((rows // mine, mine, width), early.dtype),
        in_specs=[vmem] * 3,
        out_specs=vmem,
        cost_estimate=pl.CostEstimate(
            flops=2 * rows * late.shape[0] * width, bytes_accessed=4 * late.size, transcendentals=0
        ),
        compiler_params=pltpu.CompilerParams(vmem_limit_bytes=12 << 20),
    )(where, late, early)


def exchange(blocks):
    return lax.all_to_all(blocks, "group", split_axis=0, concat_axis=0, tiled=True)


def local(stem_blocks, cap_tensor, slot_rows, counts):
    cuts, groups = lax.axis_size("cuts"), lax.axis_size("group")
    group_total, own_rows, width = stem_blocks.shape[1:]
    mine = group_total // groups
    slot_total = slot_rows.shape[1]
    share = slot_total // cuts
    terms = terms_of(stem_blocks.reshape(group_total * own_rows, width), cap_tensor[0])
    width = terms.shape[1]

    positions = jnp.arange(slot_total, dtype=jnp.int32)
    marked = jnp.where(positions[None, :] < counts[:, None], slot_rows, -1)
    me = lax.axis_index("cuts").astype(jnp.int32)
    doubled = jnp.concatenate([marked, marked], axis=1)
    turned = lax.dynamic_slice_in_dim(doubled, (me + 1) * share, slot_total, 1)

    def all_rows():
        return static_plan(terms.reshape(group_total, own_rows, width), turned, cuts)

    if cuts != 2 or mine * own_rows != 2 * LANES or LANES % own_rows or groups > LANES:
        return all_rows()

    early, late = EARLY, LATE
    plane = me[None]
    flags = needs(slot_rows, counts, own_rows, early, late, groups)
    flags = exchange(flags.reshape(groups, KINDS, LANES))
    spilled = jnp.max(flags[:, 6, :].astype(jnp.float32)) > 0.0
    by_owner = terms.reshape(groups, mine * own_rows, width)
    send, keep, keys = pack_late(plane, flags.reshape(groups * KINDS, LANES), by_owner, early, late)
    other = lax.ppermute(send, "cuts", [(0, 1), (1, 0)])
    own_early = exchange(pack_early(keys, by_owner, early)).reshape(groups * early, width)
    summed = (keep.astype(jnp.float32) + other.astype(jnp.float32)).astype(terms.dtype)
    other_early = lax.ppermute(own_early, "cuts", [(1, 0)])
    own_late = exchange(summed).reshape(groups * late, width)
    where_early, where_late = places(plane, turned[:, (cuts - 1) * share :], own_rows, early, late)
    sums = early_part(where_early, own_early, other_early, share * mine)
    return lax.cond(spilled, all_rows, lambda: late_part(where_late, own_late, sums, mine))


def solution(mesh):
    in_specs = (
        P("cuts", None, "group", None),
        P("cuts", None, None, None),
        P("group", None),
        P("group"),
    )
    out_specs = P("cuts", "group", None)
    return jax.shard_map(local, mesh=mesh, in_specs=in_specs, out_specs=out_specs, check_vma=False)
```

```python
import functools

import jax
import jax.numpy as jnp
from jax import lax
from jax.experimental import pallas as pl
from jax.experimental.pallas import tpu as pltpu
from jax.sharding import PartitionSpec as P


def terms_kernel(rows_ref, pair_ref, out_ref, matrix):
    half = pair_ref.shape[1]

    @pl.when(pl.program_id(0) == 0)
    def _():
        real_part, imag_part = pair_ref[0], pair_ref[1]
        matrix[:half, :half] = real_part
        matrix[:half, half:] = imag_part
        matrix[half:, :half] = -imag_part
        matrix[half:, half:] = real_part

    out_ref[...] = dot(rows_ref[...], matrix[...]).astype(out_ref.dtype)


def terms_of(rows, pair):
    total, width = rows.shape
    block = min(2048, total)
    out_width = 2 * pair.shape[2]
    return pl.pallas_call(
        terms_kernel,
        grid=(total // block,),
        out_shape=jax.ShapeDtypeStruct((total, out_width), rows.dtype),
        in_specs=[pl.BlockSpec((block, width), lambda i: (i, 0)), pl.BlockSpec(pair.shape, lambda i: (0, 0, 0))],
        out_specs=pl.BlockSpec((block, out_width), lambda i: (i, 0)),
        scratch_shapes=[pltpu.VMEM((width, out_width), rows.dtype)],
        cost_estimate=pl.CostEstimate(
            flops=2 * total * width * out_width, bytes_accessed=4 * rows.size, transcendentals=0
        ),
        compiler_params=pltpu.CompilerParams(vmem_limit_bytes=16 << 20),
    )(rows, pair)


def select_kernel(block, share, terms_ref, slots_ref, *outs):
    columns = iota((block, terms_ref.shape[0]), 1)
    for part, out in enumerate(outs):
        for start in range(0, share, block):
            chosen = mark(columns == slots_ref[pl.ds(part * share + start, block), :])
            out[pl.ds(start, block), :] = dot(chosen, terms_ref[...]).astype(out.dtype)


def select(terms, slots, parts):
    row_total, width = terms.shape
    slot_total = slots.shape[0]
    share = slot_total // parts
    return pl.pallas_call(
        functools.partial(select_kernel, min(256, share), share),
        out_shape=[jax.ShapeDtypeStruct((share, width), terms.dtype)] * parts,
        in_specs=[pl.BlockSpec(memory_space=pltpu.VMEM)] * 2,
        out_specs=[pl.BlockSpec(memory_space=pltpu.VMEM)] * parts,
        cost_estimate=pl.CostEstimate(
            flops=2 * row_total * width * slot_total,
            bytes_accessed=2 * (terms.size + slot_total * width),
            transcendentals=0,
        ),
        compiler_params=pltpu.CompilerParams(vmem_limit_bytes=24 << 20),
    )(terms, slots)


def static_plan(terms, turned, cuts):
    groups = lax.axis_size("group")
    group_total, own_rows, width = terms.shape
    mine = group_total // groups
    by_owner = terms.reshape(groups, mine, own_rows, width)
    sums, selected = [], []
    for k in range(mine):
        outgoing = by_owner[:, k]
        if k >= 2:
            outgoing, selected[k - 2] = lax.optimization_barrier((outgoing, selected[k - 2]))
        got = lax.all_to_all(outgoing, "group", split_axis=0, concat_axis=0, tiled=True)
        parts = select(got.reshape(groups * own_rows, width), turned[k][:, None], cuts)
        selected.append(parts)
    for parts in selected:
        total = parts[-1].astype(jnp.float32)
        for step in range(1, cuts):
            ring = [(i, (i + step) % cuts) for i in range(cuts)]
            total = total + lax.ppermute(parts[step - 1], "cuts", ring).astype(jnp.float32)
        sums.append(total.astype(terms.dtype))
    return jnp.stack(sums, axis=1)


KINDS = 8
LANES = 128
EARLY, LATE = 64, 64
ADD_BYTES, EARLY_BYTES = 1<<34, 1<<34


def dot(a, b):
    return jnp.dot(a, b, preferred_element_type=jnp.float32)


def dot_nt(a, b):
    return lax.dot_general(a, b, (((1,), (1,)), ((), ())), preferred_element_type=jnp.float32)


def iota(shape, dim):
    return lax.broadcasted_iota(jnp.int32, shape, dim)


def mark(condition):
    return jnp.where(condition, 1.0, 0.0).astype(jnp.bfloat16)


def needs_kernel(own_rows, early, late, slots_ref, counts_ref, flags_ref):
    mine, slot_total = slots_ref.shape
    side = flags_ref.shape[0]
    hits = jnp.zeros((side, LANES), jnp.float32)
    place = iota((1, slot_total), 1)
    down = iota((side, slot_total), 0)
    across = iota((LANES, slot_total), 0)
    per = LANES // own_rows
    for k in range(mine):
        slots = slots_ref[k : k + 1, :]
        half = jnp.where(place >= slot_total // 2, 2, 0)
        row_key = (slots // own_rows) * KINDS + half + k // per
        row_key = jnp.where(place < counts_ref[k], row_key, -1)
        lane_key = slots % own_rows + (k % per) * own_rows
        hits = hits + dot_nt(mark(down == row_key), mark(across == lane_key))
    flags = jnp.minimum(hits, 1.0)
    row, column = iota((side, side), 0), iota((side, side), 1)
    kind, back = row % KINDS, row - column
    first = (kind == 4) & ((back == 4) | (back == 3))
    second = (kind == 5) & ((back == 3) | (back == 2))
    sums = dot(flags.astype(jnp.bfloat16), jnp.ones((LANES, LANES), jnp.bfloat16))
    counted = dot(mark(first | second), sums.astype(jnp.bfloat16))
    kind = iota((side, LANES), 0) % KINDS
    room = jnp.where(kind == 4, 1.0 * (early + late), 1.0 * late)
    spill = jnp.max(jnp.where((kind == 4) | (kind == 5), counted - room, 0.0))
    flags_ref[...] = jnp.where(kind == 6, jnp.where(spill > 0.0, 1.0, 0.0), flags).astype(flags_ref.dtype)


def needs(slot_rows, counts, own_rows, early, late, groups):
    return pl.pallas_call(
        functools.partial(needs_kernel, own_rows, early, late),
        out_shape=jax.ShapeDtypeStruct((groups * KINDS, LANES), jnp.bfloat16),
        in_specs=[pl.BlockSpec(memory_space=pltpu.VMEM), pl.BlockSpec(memory_space=pltpu.SMEM)],
        out_specs=pl.BlockSpec(memory_space=pltpu.VMEM),
        cost_estimate=pl.CostEstimate(flops=1 << 28, bytes_accessed=1 << 17, transcendentals=0),
    )(slot_rows, counts)


def keys_of(flags):
    side = flags.shape[0]
    marks = flags
    lower = mark(iota((LANES, LANES), 0) < iota((LANES, LANES), 1))
    inside = dot(marks, lower)
    totals = dot(marks, jnp.ones((LANES, LANES), jnp.bfloat16))
    row, column = iota((side, side), 0), iota((side, side), 1)
    follows = ((row % KINDS == 1) | (row % KINDS == 3)) & (row - column == 1)
    ranks = inside + dot(mark(follows), totals.astype(jnp.bfloat16))
    return jnp.where(flags.astype(jnp.float32) > 0.0, ranks, -1.0)


def chosen_rows(capacity, upper, lower):
    rank = iota((capacity, LANES), 0).astype(jnp.float32)
    return jnp.concatenate([mark(rank == upper), mark(rank == lower)], axis=1)


def pack_kernel(plane_ref, flags_ref, terms_ref, early_ref, send_ref, keep_ref, keys_ref):
    batch, early, _ = early_ref.shape
    late = send_ref.shape[1]
    step = pl.program_id(0)

    @pl.when(step == 0)
    def _():
        keys_ref[...] = keys_of(flags_ref[...])

    plane = plane_ref[0]
    for i in range(batch):
        keys = keys_ref[pl.ds((step * batch + i) * KINDS, KINDS), :]
        second = keys[2:3], keys[3:4]
        beyond = keys[0:1] - early, keys[1:2] - early
        sent = [jnp.where(plane == 0, b, a) for a, b in zip(beyond, second)]
        kept = [jnp.where(plane == 0, a, b) for a, b in zip(beyond, second)]
        chosen = [chosen_rows(late, *sent), chosen_rows(late, *kept), chosen_rows(early, keys[0:1], keys[1:2])]
        packed = dot(jnp.concatenate(chosen, axis=0), terms_ref[i]).astype(early_ref.dtype)
        send_ref[i] = packed[:late]
        keep_ref[i] = packed[late : 2 * late]
        early_ref[i] = packed[2 * late :]


def pack(plane, flags, terms, early, late):
    groups, rows, width = terms.shape
    batch = 8 if groups % 8 == 0 else 1

    def out(capacity):
        block = pl.BlockSpec((batch, capacity, width), lambda i: (i, 0, 0))
        return jax.ShapeDtypeStruct((groups, capacity, width), terms.dtype), block

    shapes, blocks = zip(out(early), out(late), out(late))
    return pl.pallas_call(
        pack_kernel,
        grid=(groups // batch,),
        out_shape=shapes,
        in_specs=[
            pl.BlockSpec(memory_space=pltpu.SMEM),
            pl.BlockSpec(flags.shape, lambda i: (0, 0)),
            pl.BlockSpec((batch, rows, width), lambda i: (i, 0, 0)),
        ],
        out_specs=blocks,
        scratch_shapes=[pltpu.VMEM(flags.shape, jnp.float32)],
        cost_estimate=pl.CostEstimate(
            flops=2 * groups * (early + 2 * late) * rows * width, bytes_accessed=4 * terms.size, transcendentals=0
        ),
        compiler_params=pltpu.CompilerParams(vmem_limit_bytes=16 << 20),
    )(plane, flags, terms)


def add_kernel(a_ref, b_ref, out_ref):
    out_ref[...] = (a_ref[...].astype(jnp.float32) + b_ref[...].astype(jnp.float32)).astype(out_ref.dtype)


def add(a, b):
    vmem = pl.BlockSpec(memory_space=pltpu.VMEM)
    return pl.pallas_call(
        add_kernel,
        out_shape=jax.ShapeDtypeStruct(a.shape, a.dtype),
        in_specs=[vmem] * 2,
        out_specs=vmem,
        cost_estimate=pl.CostEstimate(flops=ADD_BYTES, bytes_accessed=ADD_BYTES, transcendentals=0),
        compiler_params=pltpu.CompilerParams(vmem_limit_bytes=8 << 20),
    )(a, b)


def places_kernel(own_rows, early, late, plane_ref, slots_ref, column_ref, early_ref, late_ref):
    mine, share = slots_ref.shape
    rows = mine * own_rows
    down = iota((own_rows, share), 0)
    across = iota((LANES, share), 0)
    wanted = []
    for k in range(mine):
        slots = slots_ref[k : k + 1, :]
        source = jnp.where(slots >= 0, slots // own_rows, -1)
        wanted.append(dot_nt(mark(down == slots % own_rows), mark(across == source)))
    wanted = jnp.minimum(jnp.concatenate(wanted, axis=0), 1.0)
    before = mark(iota((rows, rows), 0) > iota((rows, rows), 1))
    ranks = dot(before, wanted.astype(jnp.bfloat16)).astype(jnp.bfloat16)
    shift = plane_ref[0] * early
    group = iota((LANES, 1), 0) % mine
    lane = iota((LANES, LANES), 1)
    in_early = jnp.full((LANES, LANES), -1, jnp.int32)
    in_late = in_early
    for block in range(mine * share // LANES):
        slots = column_ref[:, block : block + 1]
        source = slots // own_rows
        row = jnp.where(slots >= 0, group * own_rows + slots % own_rows, -1)
        looked = dot(mark(iota((LANES, rows), 1) == row), ranks)
        found = jnp.where(lane == source, looked, 0.0)
        rank = jnp.sum(found, axis=1, keepdims=True).astype(jnp.int32) + shift
        live, low = slots >= 0, rank < early
        in_early = jnp.where((lane == block) & live & low, source * early + rank, in_early)
        in_late = jnp.where((lane == block) & live & ~low, source * late + rank - early, in_late)
    early_ref[...] = in_early
    late_ref[...] = in_late


def places(plane, own_slots, own_rows, early, late):
    column = own_slots.T.reshape(-1, LANES).T
    vmem = pl.BlockSpec(memory_space=pltpu.VMEM)
    return pl.pallas_call(
        functools.partial(places_kernel, own_rows, early, late),
        out_shape=[jax.ShapeDtypeStruct((LANES, LANES), jnp.int32)] * 2,
        in_specs=[pl.BlockSpec(memory_space=pltpu.SMEM), vmem, vmem],
        out_specs=[vmem] * 2,
        cost_estimate=pl.CostEstimate(flops=1 << 28, bytes_accessed=1 << 18, transcendentals=0),
    )(plane, own_slots, column)


BLOCK = 2 * LANES


def chosen_places(places_ref, block, total):
    columns = iota((LANES, total), 1)
    first = block * BLOCK // LANES
    picks = [mark(columns == places_ref[:, first + i : first + i + 1]) for i in range(BLOCK // LANES)]
    return jnp.concatenate(picks, axis=0)


def early_kernel(places_ref, own_ref, other_ref, out_ref, table):
    both = own_ref[...].astype(jnp.float32) + other_ref[...].astype(jnp.float32)
    table[...] = both.astype(table.dtype)
    for block in range(out_ref.shape[0] // BLOCK):
        chosen = chosen_places(places_ref, block, table.shape[0])
        out_ref[block * BLOCK : (block + 1) * BLOCK, :] = dot(chosen, table[...]).astype(out_ref.dtype)


def late_kernel(places_ref, late_ref, early_ref, out_ref):
    rows, width = early_ref.shape
    share, mine, _ = out_ref.shape
    per = BLOCK // mine
    for block in range(rows // BLOCK):
        chosen = chosen_places(places_ref, block, late_ref.shape[0])
        early = early_ref[block * BLOCK : (block + 1) * BLOCK, :].astype(jnp.float32)
        total = (dot(chosen, late_ref[...]) + early).astype(out_ref.dtype)
        out_ref[block * per : (block + 1) * per] = total.reshape(per, mine, width)


def early_part(where, own, other, slots):
    rows, width = own.shape
    vmem = pl.BlockSpec(memory_space=pltpu.VMEM)
    return pl.pallas_call(
        early_kernel,
        out_shape=jax.ShapeDtypeStruct((slots, width), own.dtype),
        in_specs=[vmem] * 3,
        out_specs=vmem,
        scratch_shapes=[pltpu.VMEM((rows, width), own.dtype)],
        cost_estimate=pl.CostEstimate(
            flops=EARLY_BYTES, bytes_accessed=EARLY_BYTES, transcendentals=0
        ),
        compiler_params=pltpu.CompilerParams(vmem_limit_bytes=12 << 20),
    )(where, own, other)


def late_part(where, late, early, mine):
    rows, width = early.shape
    vmem = pl.BlockSpec(memory_space=pltpu.VMEM)
    return pl.pallas_call(
        late_kernel,
        out_shape=jax.ShapeDtypeStruct((rows // mine, mine, width), early.dtype),
        in_specs=[vmem] * 3,
        out_specs=vmem,
        cost_estimate=pl.CostEstimate(
            flops=2 * rows * late.shape[0] * width, bytes_accessed=4 * late.size, transcendentals=0
        ),
        compiler_params=pltpu.CompilerParams(vmem_limit_bytes=12 << 20),
    )(where, late, early)


def exchange(blocks):
    return lax.all_to_all(blocks, "group", split_axis=0, concat_axis=0, tiled=True)


def local(stem_blocks, cap_tensor, slot_rows, counts):
    cuts, groups = lax.axis_size("cuts"), lax.axis_size("group")
    group_total, own_rows, width = stem_blocks.shape[1:]
    mine = group_total // groups
    slot_total = slot_rows.shape[1]
    share = slot_total // cuts
    stem = stem_blocks.reshape(group_total * own_rows, width)
    width = 2 * cap_tensor.shape[3]

    positions = jnp.arange(slot_total, dtype=jnp.int32)
    marked = jnp.where(positions[None, :] < counts[:, None], slot_rows, -1)
    me = lax.axis_index("cuts").astype(jnp.int32)
    doubled = jnp.concatenate([marked, marked], axis=1)
    turned = lax.dynamic_slice_in_dim(doubled, (me + 1) * share, slot_total, 1)

    def all_rows():
        terms = terms_of(stem, cap_tensor[0])
        return static_plan(terms.reshape(group_total, own_rows, width), turned, cuts)

    if cuts != 2 or mine * own_rows != 2 * LANES or LANES % own_rows or groups > LANES:
        return all_rows()

    early, late = EARLY, LATE
    plane = me[None]
    terms = terms_of(stem, cap_tensor[0])
    flags = needs(slot_rows, counts, own_rows, early, late, groups)
    flags = exchange(flags.reshape(groups, KINDS, LANES))
    spilled = jnp.max(flags[:, 6, :].astype(jnp.float32)) > 0.0
    by_owner = terms.reshape(groups, mine * own_rows, width)
    first, send, keep = pack(plane, flags.reshape(groups * KINDS, LANES), by_owner, early, late)
    other = lax.ppermute(send, "cuts", [(0, 1), (1, 0)])
    own_early = exchange(first).reshape(groups * early, width)
    own_early, summed = lax.optimization_barrier((own_early, add(keep, other)))
    other_early = lax.ppermute(own_early, "cuts", [(1, 0)])
    own_late = exchange(summed).reshape(groups * late, width)
    where_early, where_late = places(plane, turned[:, (cuts - 1) * share :], own_rows, early, late)
    sums = early_part(where_early, own_early, other_early, share * mine)
    return lax.cond(spilled, all_rows, lambda: late_part(where_late, own_late, sums, mine))


def solution(mesh):
    in_specs = (
        P("cuts", None, "group", None),
        P("cuts", None, None, None),
        P("group", None),
        P("group"),
    )
    out_specs = P("cuts", "group", None)
    return jax.shard_map(local, mesh=mesh, in_specs=in_specs, out_specs=out_specs, check_vma=False)
```

```python
import functools

import jax
import jax.numpy as jnp
from jax import lax
from jax.experimental import pallas as pl
from jax.experimental.pallas import tpu as pltpu
from jax.sharding import PartitionSpec as P


def terms_kernel(rows_ref, pair_ref, out_ref, matrix):
    half = pair_ref.shape[1]

    @pl.when(pl.program_id(0) == 0)
    def _():
        real_part, imag_part = pair_ref[0], pair_ref[1]
        matrix[:half, :half] = real_part
        matrix[:half, half:] = imag_part
        matrix[half:, :half] = -imag_part
        matrix[half:, half:] = real_part

    out_ref[...] = dot(rows_ref[...], matrix[...]).astype(out_ref.dtype)


def terms_of(rows, pair):
    total, width = rows.shape
    block = min(2048, total)
    out_width = 2 * pair.shape[2]
    return pl.pallas_call(
        terms_kernel,
        grid=(total // block,),
        out_shape=jax.ShapeDtypeStruct((total, out_width), rows.dtype),
        in_specs=[pl.BlockSpec((block, width), lambda i: (i, 0)), pl.BlockSpec(pair.shape, lambda i: (0, 0, 0))],
        out_specs=pl.BlockSpec((block, out_width), lambda i: (i, 0)),
        scratch_shapes=[pltpu.VMEM((width, out_width), rows.dtype)],
        cost_estimate=pl.CostEstimate(
            flops=2 * total * width * out_width, bytes_accessed=4 * rows.size, transcendentals=0
        ),
        compiler_params=pltpu.CompilerParams(vmem_limit_bytes=16 << 20),
    )(pltpu.with_memory_space_constraint(rows, pltpu.HBM), pltpu.with_memory_space_constraint(pair, pltpu.HBM))


def select_kernel(block, share, terms_ref, slots_ref, *outs):
    columns = iota((block, terms_ref.shape[0]), 1)
    for part, out in enumerate(outs):
        for start in range(0, share, block):
            chosen = mark(columns == slots_ref[pl.ds(part * share + start, block), :])
            out[pl.ds(start, block), :] = dot(chosen, terms_ref[...]).astype(out.dtype)


def select(terms, slots, parts):
    row_total, width = terms.shape
    slot_total = slots.shape[0]
    share = slot_total // parts
    return pl.pallas_call(
        functools.partial(select_kernel, min(256, share), share),
        out_shape=[jax.ShapeDtypeStruct((share, width), terms.dtype)] * parts,
        in_specs=[pl.BlockSpec(memory_space=pltpu.VMEM)] * 2,
        out_specs=[pl.BlockSpec(memory_space=pltpu.VMEM)] * parts,
        cost_estimate=pl.CostEstimate(
            flops=2 * row_total * width * slot_total,
            bytes_accessed=2 * (terms.size + slot_total * width),
            transcendentals=0,
        ),
        compiler_params=pltpu.CompilerParams(vmem_limit_bytes=24 << 20),
    )(terms, slots)


def static_plan(terms, turned, cuts):
    groups = lax.axis_size("group")
    group_total, own_rows, width = terms.shape
    mine = group_total // groups
    by_owner = terms.reshape(groups, mine, own_rows, width)
    sums, selected = [], []
    for k in range(mine):
        outgoing = by_owner[:, k]
        if k >= 2:
            outgoing, selected[k - 2] = lax.optimization_barrier((outgoing, selected[k - 2]))
        got = lax.all_to_all(outgoing, "group", split_axis=0, concat_axis=0, tiled=True)
        parts = select(got.reshape(groups * own_rows, width), turned[k][:, None], cuts)
        selected.append(parts)
    for parts in selected:
        total = parts[-1].astype(jnp.float32)
        for step in range(1, cuts):
            ring = [(i, (i + step) % cuts) for i in range(cuts)]
            total = total + lax.ppermute(parts[step - 1], "cuts", ring).astype(jnp.float32)
        sums.append(total.astype(terms.dtype))
    return jnp.stack(sums, axis=1)


KINDS = 8
LANES = 128
STEP = 4
EARLY, LATE = 64, 64
ADD_BYTES, EARLY_BYTES = 1<<34, 1<<34


def dot(a, b):
    return jnp.dot(a, b, preferred_element_type=jnp.float32)


def dot_nt(a, b):
    return lax.dot_general(a, b, (((1,), (1,)), ((), ())), preferred_element_type=jnp.float32)


def iota(shape, dim):
    return lax.broadcasted_iota(jnp.int32, shape, dim)


def mark(condition):
    return jnp.where(condition, 1.0, 0.0).astype(jnp.bfloat16)


def needs_kernel(own_rows, early, late, slots_ref, counts_ref, flags_ref):
    mine, slot_total = slots_ref.shape
    side = flags_ref.shape[0]
    hits = jnp.zeros((side, LANES), jnp.float32)
    place = iota((1, slot_total), 1)
    down = iota((side, slot_total), 0)
    across = iota((LANES, slot_total), 0)
    per = LANES // own_rows
    for k in range(mine):
        slots = slots_ref[k : k + 1, :]
        half = jnp.where(place >= slot_total // 2, 2, 0)
        row_key = (slots // own_rows) * KINDS + half + k // per
        row_key = jnp.where(place < counts_ref[k], row_key, -1)
        lane_key = slots % own_rows + (k % per) * own_rows
        hits = hits + dot_nt(mark(down == row_key), mark(across == lane_key))
    flags = jnp.minimum(hits, 1.0)
    row, column = iota((side, side), 0), iota((side, side), 1)
    kind, back = row % KINDS, row - column
    first = (kind == 4) & ((back == 4) | (back == 3))
    second = (kind == 5) & ((back == 3) | (back == 2))
    sums = dot(flags.astype(jnp.bfloat16), jnp.ones((LANES, LANES), jnp.bfloat16))
    counted = dot(mark(first | second), sums.astype(jnp.bfloat16))
    kind = iota((side, LANES), 0) % KINDS
    room = jnp.where(kind == 4, 1.0 * (early + late), 1.0 * late)
    spill = jnp.max(jnp.where((kind == 4) | (kind == 5), counted - room, 0.0))
    flags_ref[...] = jnp.where(kind == 6, jnp.where(spill > 0.0, 1.0, 0.0), flags).astype(flags_ref.dtype)


def needs(slot_rows, counts, own_rows, early, late, groups):
    return pl.pallas_call(
        functools.partial(needs_kernel, own_rows, early, late),
        out_shape=jax.ShapeDtypeStruct((groups * KINDS, LANES), jnp.bfloat16),
        in_specs=[pl.BlockSpec(memory_space=pltpu.VMEM), pl.BlockSpec(memory_space=pltpu.SMEM)],
        out_specs=pl.BlockSpec(memory_space=pltpu.VMEM),
        cost_estimate=pl.CostEstimate(flops=1 << 28, bytes_accessed=1 << 17, transcendentals=0),
    )(slot_rows, counts)


def keys_of(flags):
    side = flags.shape[0]
    marks = flags
    lower = mark(iota((LANES, LANES), 0) < iota((LANES, LANES), 1))
    inside = dot(marks, lower)
    totals = dot(marks, jnp.ones((LANES, LANES), jnp.bfloat16))
    row, column = iota((side, side), 0), iota((side, side), 1)
    follows = ((row % KINDS == 1) | (row % KINDS == 3)) & (row - column == 1)
    ranks = inside + dot(mark(follows), totals.astype(jnp.bfloat16))
    return jnp.where(flags.astype(jnp.float32) > 0.0, ranks, -1.0)


def chosen_rows(capacity, upper, lower):
    rank = iota((capacity, LANES), 0).astype(jnp.float32)
    return jnp.concatenate([mark(rank == upper), mark(rank == lower)], axis=1)


def pack_kernel(plane_ref, flags_ref, terms_ref, early_ref, send_ref, keep_ref, keys_ref):
    batch, early, _ = early_ref.shape
    late = send_ref.shape[1]
    step = pl.program_id(0)

    @pl.when(step == 0)
    def _():
        keys_ref[...] = keys_of(flags_ref[...])

    plane = plane_ref[0]
    for i in range(batch):
        keys = keys_ref[pl.ds((step * batch + i) * KINDS, KINDS), :]
        second = keys[2:3], keys[3:4]
        beyond = keys[0:1] - early, keys[1:2] - early
        sent = [jnp.where(plane == 0, b, a) for a, b in zip(beyond, second)]
        kept = [jnp.where(plane == 0, a, b) for a, b in zip(beyond, second)]
        chosen = [chosen_rows(late, *sent), chosen_rows(late, *kept), chosen_rows(early, keys[0:1], keys[1:2])]
        packed = dot(jnp.concatenate(chosen, axis=0), terms_ref[i]).astype(early_ref.dtype)
        send_ref[i] = packed[:late]
        keep_ref[i] = packed[late : 2 * late]
        early_ref[i] = packed[2 * late :]


def pack(plane, flags, terms, early, late):
    groups, rows, width = terms.shape
    batch = 8 if groups % 8 == 0 else 1

    def out(capacity):
        block = pl.BlockSpec((batch, capacity, width), lambda i: (i, 0, 0))
        return jax.ShapeDtypeStruct((groups, capacity, width), terms.dtype), block

    shapes, blocks = zip(out(early), out(late), out(late))
    return pl.pallas_call(
        pack_kernel,
        grid=(groups // batch,),
        out_shape=shapes,
        in_specs=[
            pl.BlockSpec(memory_space=pltpu.SMEM),
            pl.BlockSpec(flags.shape, lambda i: (0, 0)),
            pl.BlockSpec((batch, rows, width), lambda i: (i, 0, 0)),
        ],
        out_specs=blocks,
        scratch_shapes=[pltpu.VMEM(flags.shape, jnp.float32)],
        cost_estimate=pl.CostEstimate(
            flops=2 * groups * (early + 2 * late) * rows * width, bytes_accessed=4 * terms.size, transcendentals=0
        ),
        compiler_params=pltpu.CompilerParams(vmem_limit_bytes=16 << 20),
    )(plane, flags, terms)


def add_kernel(a_ref, b_ref, out_ref):
    out_ref[...] = (a_ref[...].astype(jnp.float32) + b_ref[...].astype(jnp.float32)).astype(out_ref.dtype)


def add(a, b):
    vmem = pl.BlockSpec(memory_space=pltpu.VMEM)
    return pl.pallas_call(
        add_kernel,
        out_shape=jax.ShapeDtypeStruct(a.shape, a.dtype),
        in_specs=[vmem] * 2,
        out_specs=vmem,
        cost_estimate=pl.CostEstimate(flops=ADD_BYTES, bytes_accessed=ADD_BYTES, transcendentals=0),
        compiler_params=pltpu.CompilerParams(vmem_limit_bytes=8 << 20),
    )(a, b)


def places_kernel(own_rows, early, late, plane_ref, slots_ref, column_ref, early_ref, late_ref):
    mine, share = slots_ref.shape
    rows = mine * own_rows
    down = iota((own_rows, share), 0)
    across = iota((LANES, share), 0)
    wanted = []
    for k in range(mine):
        slots = slots_ref[k : k + 1, :]
        source = jnp.where(slots >= 0, slots // own_rows, -1)
        wanted.append(dot_nt(mark(down == slots % own_rows), mark(across == source)))
    wanted = jnp.minimum(jnp.concatenate(wanted, axis=0), 1.0)
    before = mark(iota((rows, rows), 0) > iota((rows, rows), 1))
    ranks = dot(before, wanted.astype(jnp.bfloat16)).astype(jnp.bfloat16)
    shift = plane_ref[0] * early
    group = iota((LANES, 1), 0) % mine
    lane = iota((LANES, LANES), 1)
    for block in range(mine * share // LANES):
        at, spot = block // STEP, block % STEP
        if spot == 0:
            in_early = jnp.full((LANES, LANES), -1, jnp.int32)
            in_late = in_early
        slots = column_ref[:, block : block + 1]
        source = slots // own_rows
        row = jnp.where(slots >= 0, group * own_rows + slots % own_rows, -1)
        looked = dot(mark(iota((LANES, rows), 1) == row), ranks)
        found = jnp.where(lane == source, looked, 0.0)
        rank = jnp.sum(found, axis=1, keepdims=True).astype(jnp.int32) + shift
        live, low = slots >= 0, rank < early
        in_early = jnp.where((lane == spot) & live & low, source * early + rank, in_early)
        in_late = jnp.where((lane == spot) & live & ~low, source * late + rank - early, in_late)
        if spot == STEP - 1:
            early_ref[at] = in_early
            late_ref[at] = in_late


def places(plane, own_slots, own_rows, early, late):
    column = own_slots.T.reshape(-1, LANES).T
    vmem = pl.BlockSpec(memory_space=pltpu.VMEM)
    return pl.pallas_call(
        functools.partial(places_kernel, own_rows, early, late),
        out_shape=[jax.ShapeDtypeStruct((own_slots.size // (STEP * LANES), LANES, LANES), jnp.int32)] * 2,
        in_specs=[pl.BlockSpec(memory_space=pltpu.SMEM), vmem, vmem],
        out_specs=[vmem] * 2,
        cost_estimate=pl.CostEstimate(flops=1 << 28, bytes_accessed=1 << 18, transcendentals=0),
    )(plane, own_slots, column)


def chosen_places(places_ref, total):
    columns = iota((LANES, total), 1)
    return jnp.concatenate([mark(columns == places_ref[0, :, i : i + 1]) for i in range(STEP)], axis=0)


def early_kernel(places_ref, own_ref, other_ref, out_ref, table):
    @pl.when(pl.program_id(0) == 0)
    def _():
        both = own_ref[...].astype(jnp.float32) + other_ref[...].astype(jnp.float32)
        table[...] = both.astype(table.dtype)

    out_ref[...] = dot(chosen_places(places_ref, table.shape[0]), table[...]).astype(out_ref.dtype)


def late_kernel(places_ref, late_ref, early_ref, out_ref):
    total = dot(chosen_places(places_ref, late_ref.shape[0]), late_ref[...]) + early_ref[...].astype(jnp.float32)
    out_ref[...] = total.astype(out_ref.dtype).reshape(out_ref.shape)


def early_part(where, own, other):
    rows, width = own.shape
    blocks = where.shape[0]
    whole = pl.BlockSpec(own.shape, lambda i: (0, 0))
    slots = blocks * STEP * LANES
    return pl.pallas_call(
        early_kernel,
        grid=(blocks,),
        out_shape=jax.ShapeDtypeStruct((slots, width), own.dtype),
        in_specs=[pl.BlockSpec((1, LANES, LANES), lambda i: (i, 0, 0)), whole, whole],
        out_specs=pl.BlockSpec((STEP * LANES, width), lambda i: (i, 0)),
        scratch_shapes=[pltpu.VMEM((rows, width), own.dtype)],
        cost_estimate=pl.CostEstimate(flops=EARLY_BYTES, bytes_accessed=EARLY_BYTES, transcendentals=0),
        compiler_params=pltpu.CompilerParams(vmem_limit_bytes=12 << 20),
    )(where, own, other)


def late_part(where, late, early, mine):
    rows, width = early.shape
    blocks = where.shape[0]
    step = STEP * LANES
    return pl.pallas_call(
        late_kernel,
        grid=(blocks,),
        out_shape=jax.ShapeDtypeStruct((rows // mine, mine, width), early.dtype),
        in_specs=[
            pl.BlockSpec((1, LANES, LANES), lambda i: (i, 0, 0)),
            pl.BlockSpec(late.shape, lambda i: (0, 0)),
            pl.BlockSpec((step, width), lambda i: (i, 0)),
        ],
        out_specs=pl.BlockSpec((step // mine, mine, width), lambda i: (i, 0, 0)),
        cost_estimate=pl.CostEstimate(
            flops=2 * rows * late.shape[0] * width, bytes_accessed=4 * late.size, transcendentals=0
        ),
        compiler_params=pltpu.CompilerParams(vmem_limit_bytes=12 << 20),
    )(where, late, early)


def exchange(blocks):
    return lax.all_to_all(blocks, "group", split_axis=0, concat_axis=0, tiled=True)


def local(stem_blocks, cap_tensor, slot_rows, counts):
    cuts, groups = lax.axis_size("cuts"), lax.axis_size("group")
    group_total, own_rows, width = stem_blocks.shape[1:]
    mine = group_total // groups
    slot_total = slot_rows.shape[1]
    share = slot_total // cuts
    stem = stem_blocks.reshape(group_total * own_rows, width)
    terms = terms_of(stem, cap_tensor[0])
    width = terms.shape[1]

    positions = jnp.arange(slot_total, dtype=jnp.int32)
    marked = jnp.where(positions[None, :] < counts[:, None], slot_rows, -1)
    me = lax.axis_index("cuts").astype(jnp.int32)
    doubled = jnp.concatenate([marked, marked], axis=1)
    turned = lax.dynamic_slice_in_dim(doubled, (me + 1) * share, slot_total, 1)

    def all_rows():
        return static_plan(terms.reshape(group_total, own_rows, width), turned, cuts)

    unfit = mine * own_rows != 2 * LANES or LANES % own_rows or groups > LANES or share * mine % (STEP * LANES)
    if cuts != 2 or unfit:
        return all_rows()

    early, late = EARLY, LATE
    plane = me[None]
    flags = needs(slot_rows, counts, own_rows, early, late, groups)
    flags = exchange(flags.reshape(groups, KINDS, LANES))
    spilled = jnp.max(flags[:, 6, :].astype(jnp.float32)) > 0.0
    by_owner = terms.reshape(groups, mine * own_rows, width)
    first, send, keep = pack(plane, flags.reshape(groups * KINDS, LANES), by_owner, early, late)
    other = lax.ppermute(send, "cuts", [(0, 1), (1, 0)])
    own_early = exchange(first).reshape(groups * early, width)
    own_early, summed = lax.optimization_barrier((own_early, add(keep, other)))
    other_early = lax.ppermute(own_early, "cuts", [(1, 0)])
    own_late = exchange(summed).reshape(groups * late, width)
    where_early, where_late = places(plane, turned[:, (cuts - 1) * share :], own_rows, early, late)
    sums = early_part(where_early, own_early, other_early)
    return lax.cond(spilled, all_rows, lambda: late_part(where_late, own_late, sums, mine))


def solution(mesh):
    in_specs = (
        P("cuts", None, "group", None),
        P("cuts", None, None, None),
        P("group", None),
        P("group"),
    )
    out_specs = P("cuts", "group", None)
    return jax.shard_map(local, mesh=mesh, in_specs=in_specs, out_specs=out_specs, check_vma=False)
```

```python
import functools

import jax
import jax.numpy as jnp
from jax import lax
from jax.experimental import pallas as pl
from jax.experimental.pallas import tpu as pltpu
from jax.sharding import PartitionSpec as P


def terms_kernel(rows_ref, pair_ref, out_ref, matrix):
    half = pair_ref.shape[1]

    @pl.when(pl.program_id(0) == 0)
    def _():
        real_part, imag_part = pair_ref[0], pair_ref[1]
        matrix[:half, :half] = real_part
        matrix[:half, half:] = imag_part
        matrix[half:, :half] = -imag_part
        matrix[half:, half:] = real_part

    out_ref[...] = dot(rows_ref[...], matrix[...]).astype(out_ref.dtype)


def terms_of(rows, pair):
    total, width = rows.shape
    block = min(2048, total)
    out_width = 2 * pair.shape[2]
    return pl.pallas_call(
        terms_kernel,
        grid=(total // block,),
        out_shape=jax.ShapeDtypeStruct((total, out_width), rows.dtype),
        in_specs=[pl.BlockSpec((block, width), lambda i: (i, 0)), pl.BlockSpec(pair.shape, lambda i: (0, 0, 0))],
        out_specs=pl.BlockSpec((block, out_width), lambda i: (i, 0)),
        scratch_shapes=[pltpu.VMEM((width, out_width), rows.dtype)],
        cost_estimate=pl.CostEstimate(
            flops=2 * total * width * out_width, bytes_accessed=4 * rows.size, transcendentals=0
        ),
        compiler_params=pltpu.CompilerParams(vmem_limit_bytes=16 << 20),
    )(pltpu.with_memory_space_constraint(rows, pltpu.HBM), pltpu.with_memory_space_constraint(pair, pltpu.HBM))


def select_kernel(block, share, terms_ref, slots_ref, *outs):
    columns = iota((block, terms_ref.shape[0]), 1)
    for part, out in enumerate(outs):
        for start in range(0, share, block):
            chosen = mark(columns == slots_ref[pl.ds(part * share + start, block), :])
            out[pl.ds(start, block), :] = dot(chosen, terms_ref[...]).astype(out.dtype)


def select(terms, slots, parts):
    row_total, width = terms.shape
    slot_total = slots.shape[0]
    share = slot_total // parts
    return pl.pallas_call(
        functools.partial(select_kernel, min(256, share), share),
        out_shape=[jax.ShapeDtypeStruct((share, width), terms.dtype)] * parts,
        in_specs=[pl.BlockSpec(memory_space=pltpu.VMEM)] * 2,
        out_specs=[pl.BlockSpec(memory_space=pltpu.VMEM)] * parts,
        cost_estimate=pl.CostEstimate(
            flops=2 * row_total * width * slot_total,
            bytes_accessed=2 * (terms.size + slot_total * width),
            transcendentals=0,
        ),
        compiler_params=pltpu.CompilerParams(vmem_limit_bytes=24 << 20),
    )(terms, slots)


def static_plan(terms, turned, cuts):
    groups = lax.axis_size("group")
    group_total, own_rows, width = terms.shape
    mine = group_total // groups
    by_owner = terms.reshape(groups, mine, own_rows, width)
    sums, selected = [], []
    for k in range(mine):
        outgoing = by_owner[:, k]
        if k >= 2:
            outgoing, selected[k - 2] = lax.optimization_barrier((outgoing, selected[k - 2]))
        got = lax.all_to_all(outgoing, "group", split_axis=0, concat_axis=0, tiled=True)
        parts = select(got.reshape(groups * own_rows, width), turned[k][:, None], cuts)
        selected.append(parts)
    for parts in selected:
        total = parts[-1].astype(jnp.float32)
        for step in range(1, cuts):
            ring = [(i, (i + step) % cuts) for i in range(cuts)]
            total = total + lax.ppermute(parts[step - 1], "cuts", ring).astype(jnp.float32)
        sums.append(total.astype(terms.dtype))
    return jnp.stack(sums, axis=1)


KINDS = 8
LANES = 128
STEP = 2
UNROLL = 4
LADDER = (56, 56), (56, 64), (72, 72)
ADD_BYTES, EARLY_BYTES = 1<<34, 1<<34


def dot(a, b):
    return jnp.dot(a, b, preferred_element_type=jnp.float32)


def dot_nt(a, b):
    return lax.dot_general(a, b, (((1,), (1,)), ((), ())), preferred_element_type=jnp.float32)


def iota(shape, dim):
    return lax.broadcasted_iota(jnp.int32, shape, dim)


def mark(condition):
    return jnp.where(condition, 1.0, 0.0).astype(jnp.bfloat16)


def needs_kernel(own_rows, slots_ref, counts_ref, flags_ref):
    mine, slot_total = slots_ref.shape
    side = flags_ref.shape[0]
    hits = jnp.zeros((side, LANES), jnp.float32)
    place = iota((1, slot_total), 1)
    down = iota((side, slot_total), 0)
    across = iota((LANES, slot_total), 0)
    per = LANES // own_rows
    for k in range(mine):
        slots = slots_ref[k : k + 1, :]
        half = jnp.where(place >= slot_total // 2, 2, 0)
        row_key = (slots // own_rows) * KINDS + half + k // per
        row_key = jnp.where(place < counts_ref[k], row_key, -1)
        lane_key = slots % own_rows + (k % per) * own_rows
        hits = hits + dot_nt(mark(down == row_key), mark(across == lane_key))
    flags = jnp.minimum(hits, 1.0)
    row, column = iota((side, side), 0), iota((side, side), 1)
    kind, back = row % KINDS, row - column
    first = (kind == 4) & ((back == 4) | (back == 3))
    second = (kind == 5) & ((back == 3) | (back == 2))
    sums = dot(flags.astype(jnp.bfloat16), jnp.ones((LANES, LANES), jnp.bfloat16))
    counted = dot(mark(first | second), sums.astype(jnp.bfloat16))
    kind = iota((side, LANES), 0) % KINDS
    level = jnp.zeros((side, LANES), jnp.float32)
    for early, late in LADDER:
        room = jnp.where(kind == 4, 1.0 * (early + late), jnp.where(kind == 5, 1.0 * late, 1.0 * LANES * KINDS))
        level = level + jnp.where(counted > room, 1.0, 0.0)
    flags_ref[...] = jnp.where(kind == 6, jnp.max(level), flags).astype(flags_ref.dtype)


def needs(slot_rows, counts, own_rows, groups):
    return pl.pallas_call(
        functools.partial(needs_kernel, own_rows),
        out_shape=jax.ShapeDtypeStruct((groups * KINDS, LANES), jnp.bfloat16),
        in_specs=[pl.BlockSpec(memory_space=pltpu.VMEM), pl.BlockSpec(memory_space=pltpu.SMEM)],
        out_specs=pl.BlockSpec(memory_space=pltpu.VMEM),
        cost_estimate=pl.CostEstimate(flops=1 << 28, bytes_accessed=1 << 17, transcendentals=0),
    )(slot_rows, counts)


def keys_of(flags):
    side = flags.shape[0]
    marks = flags
    lower = mark(iota((LANES, LANES), 0) < iota((LANES, LANES), 1))
    inside = dot(marks, lower)
    totals = dot(marks, jnp.ones((LANES, LANES), jnp.bfloat16))
    row, column = iota((side, side), 0), iota((side, side), 1)
    follows = ((row % KINDS == 1) | (row % KINDS == 3)) & (row - column == 1)
    ranks = inside + dot(mark(follows), totals.astype(jnp.bfloat16))
    return jnp.where(flags.astype(jnp.float32) > 0.0, ranks, -1.0)


def chosen_rows(capacity, upper, lower):
    rank = iota((capacity, LANES), 0).astype(jnp.float32)
    return jnp.concatenate([mark(rank == upper), mark(rank == lower)], axis=1)


def pack_kernel(plane_ref, flags_ref, terms_ref, early_ref, send_ref, keep_ref, rows, packed_early, keys_ref, came, went):
    groups, early, _ = packed_early.shape
    late = send_ref.shape[1]

    def arrival(d):
        return pltpu.make_async_copy(terms_ref.at[d], rows.at[d], came.at[d])

    def departure(d):
        return pltpu.make_async_copy(packed_early.at[d], early_ref.at[d], went.at[d])

    @pl.loop(0, groups)
    def _(d):
        arrival(d).start()

    keys_ref[...] = keys_of(flags_ref[...])
    plane = plane_ref[0]

    def one(d):
        keys = keys_ref[pl.ds(pl.multiple_of(d * KINDS, KINDS), KINDS), :]
        second = keys[2:3], keys[3:4]
        beyond = keys[0:1] - early, keys[1:2] - early
        sent = [jnp.where(plane == 0, b, a) for a, b in zip(beyond, second)]
        kept = [jnp.where(plane == 0, a, b) for a, b in zip(beyond, second)]
        chosen = [chosen_rows(late, *sent), chosen_rows(late, *kept), chosen_rows(early, keys[0:1], keys[1:2])]
        arrival(d).wait()
        packed = dot(jnp.concatenate(chosen, axis=0), rows[d]).astype(packed_early.dtype)
        send_ref[d] = packed[:late]
        keep_ref[d] = packed[late : 2 * late]
        packed_early[d] = packed[2 * late :]
        departure(d).start()

    unroll = UNROLL if groups % UNROLL == 0 else 1

    @pl.loop(0, groups // unroll)
    def _(step):
        for i in range(unroll):
            one(step * unroll + i)

    @pl.loop(0, groups)
    def _(d):
        departure(d).wait()


def pack(plane, flags, terms, early, late):
    groups, rows, width = terms.shape
    vmem, hbm = pl.BlockSpec(memory_space=pltpu.VMEM), pl.BlockSpec(memory_space=pltpu.HBM)
    shapes = [jax.ShapeDtypeStruct((groups, capacity, width), terms.dtype) for capacity in (early, late, late)]
    return pl.pallas_call(
        pack_kernel,
        out_shape=shapes,
        in_specs=[pl.BlockSpec(memory_space=pltpu.SMEM), vmem, hbm],
        out_specs=[hbm, vmem, vmem],
        scratch_shapes=[
            pltpu.VMEM(terms.shape, terms.dtype),
            pltpu.VMEM((groups, early, width), terms.dtype),
            pltpu.VMEM(flags.shape, jnp.float32),
            pltpu.SemaphoreType.DMA((groups,)),
            pltpu.SemaphoreType.DMA((groups,)),
        ],
        cost_estimate=pl.CostEstimate(
            flops=2 * groups * (early + 2 * late) * rows * width, bytes_accessed=4 * terms.size, transcendentals=0
        ),
        compiler_params=pltpu.CompilerParams(vmem_limit_bytes=16 << 20),
    )(plane, flags, terms)


def add_kernel(a_ref, b_ref, out_ref):
    out_ref[...] = (a_ref[...].astype(jnp.float32) + b_ref[...].astype(jnp.float32)).astype(out_ref.dtype)


def add(a, b):
    vmem = pl.BlockSpec(memory_space=pltpu.VMEM)
    return pl.pallas_call(
        add_kernel,
        out_shape=jax.ShapeDtypeStruct(a.shape, a.dtype),
        in_specs=[vmem] * 2,
        out_specs=vmem,
        cost_estimate=pl.CostEstimate(flops=ADD_BYTES, bytes_accessed=ADD_BYTES, transcendentals=0),
        compiler_params=pltpu.CompilerParams(vmem_limit_bytes=8 << 20),
    )(a, b)


def places_kernel(own_rows, early, late, plane_ref, slots_ref, column_ref, early_ref, late_ref):
    mine, share = slots_ref.shape
    rows = mine * own_rows
    down = iota((own_rows, share), 0)
    across = iota((LANES, share), 0)
    wanted = []
    for k in range(mine):
        slots = slots_ref[k : k + 1, :]
        source = jnp.where(slots >= 0, slots // own_rows, -1)
        wanted.append(dot_nt(mark(down == slots % own_rows), mark(across == source)))
    wanted = jnp.minimum(jnp.concatenate(wanted, axis=0), 1.0)
    before = mark(iota((rows, rows), 0) > iota((rows, rows), 1))
    ranks = dot(before, wanted.astype(jnp.bfloat16)).astype(jnp.bfloat16)
    shift = plane_ref[0] * early
    group = iota((LANES, 1), 0) % mine
    lane = iota((LANES, LANES), 1)
    for block in range(mine * share // LANES):
        at, spot = block // STEP, block % STEP
        if spot == 0:
            in_early = jnp.full((LANES, LANES), -1, jnp.int32)
            in_late = in_early
        slots = column_ref[:, block : block + 1]
        source = slots // own_rows
        row = jnp.where(slots >= 0, group * own_rows + slots % own_rows, -1)
        looked = dot(mark(iota((LANES, rows), 1) == row), ranks)
        found = jnp.where(lane == source, looked, 0.0)
        rank = jnp.sum(found, axis=1, keepdims=True).astype(jnp.int32) + shift
        live, low = slots >= 0, rank < early
        in_early = jnp.where((lane == spot) & live & low, source * early + rank, in_early)
        in_late = jnp.where((lane == spot) & live & ~low, source * late + rank - early, in_late)
        if spot == STEP - 1:
            early_ref[at] = in_early
            late_ref[at] = in_late


def places(plane, own_slots, own_rows, early, late):
    column = own_slots.T.reshape(-1, LANES).T
    vmem = pl.BlockSpec(memory_space=pltpu.VMEM)
    return pl.pallas_call(
        functools.partial(places_kernel, own_rows, early, late),
        out_shape=[jax.ShapeDtypeStruct((own_slots.size // (STEP * LANES), LANES, LANES), jnp.int32)] * 2,
        in_specs=[pl.BlockSpec(memory_space=pltpu.SMEM), vmem, vmem],
        out_specs=[vmem] * 2,
        cost_estimate=pl.CostEstimate(flops=1 << 28, bytes_accessed=1 << 18, transcendentals=0),
    )(plane, own_slots, column)


def chosen_places(places_ref, block, total):
    columns = iota((LANES, total), 1)
    held = places_ref[block]
    return jnp.concatenate([mark(columns == held[:, i : i + 1]) for i in range(STEP)], axis=0)


def rows_of(block, ref):
    return ref.at[pl.ds(pl.multiple_of(block * STEP * LANES, STEP * LANES), STEP * LANES)]


def early_kernel(places_ref, own_ref, other_ref, out_ref, table, chosen_sums, went):
    both = own_ref[...].astype(jnp.float32) + other_ref[...].astype(jnp.float32)
    table[...] = both.astype(table.dtype)
    blocks = places_ref.shape[0]

    def departure(block):
        return pltpu.make_async_copy(rows_of(block, chosen_sums), rows_of(block, out_ref), went.at[block])

    @pl.loop(0, blocks)
    def _(block):
        chosen = chosen_places(places_ref, block, table.shape[0])
        rows_of(block, chosen_sums)[...] = dot(chosen, table[...]).astype(chosen_sums.dtype)
        departure(block).start()

    @pl.loop(0, blocks)
    def _(block):
        departure(block).wait()


def late_kernel(places_ref, late_ref, early_ref, out_ref, early, sums, came, went):
    blocks = places_ref.shape[0]
    share, mine, width = out_ref.shape
    per = share // blocks

    def arrival(block):
        return pltpu.make_async_copy(rows_of(block, early_ref), rows_of(block, early), came.at[block])

    def departure(block):
        at = pl.ds(block * per, per)
        return pltpu.make_async_copy(sums.at[at], out_ref.at[at], went.at[block])

    @pl.loop(0, blocks)
    def _(block):
        arrival(block).start()

    @pl.loop(0, blocks)
    def _(block):
        total = dot(chosen_places(places_ref, block, late_ref.shape[0]), late_ref[...])
        arrival(block).wait()
        total = total + rows_of(block, early)[...].astype(jnp.float32)
        sums[pl.ds(block * per, per)] = total.astype(sums.dtype).reshape(per, mine, width)
        departure(block).start()

    @pl.loop(0, blocks)
    def _(block):
        departure(block).wait()


def early_part(where, own, other):
    rows, width = own.shape
    blocks = where.shape[0]
    slots = blocks * STEP * LANES
    vmem, hbm = pl.BlockSpec(memory_space=pltpu.VMEM), pl.BlockSpec(memory_space=pltpu.HBM)
    return pl.pallas_call(
        early_kernel,
        out_shape=pltpu.HBM((slots, width), own.dtype),
        in_specs=[vmem] * 3,
        out_specs=hbm,
        scratch_shapes=[
            pltpu.VMEM((rows, width), own.dtype),
            pltpu.VMEM((slots, width), own.dtype),
            pltpu.SemaphoreType.DMA((blocks,)),
        ],
        cost_estimate=pl.CostEstimate(flops=EARLY_BYTES, bytes_accessed=EARLY_BYTES, transcendentals=0),
        compiler_params=pltpu.CompilerParams(vmem_limit_bytes=12 << 20),
    )(pltpu.with_memory_space_constraint(where, pltpu.HBM), own, other)


def late_part(where, late, early, mine):
    rows, width = early.shape
    blocks = where.shape[0]
    vmem, hbm = pl.BlockSpec(memory_space=pltpu.VMEM), pl.BlockSpec(memory_space=pltpu.HBM)
    out = jax.ShapeDtypeStruct((rows // mine, mine, width), early.dtype)
    return pl.pallas_call(
        late_kernel,
        out_shape=out,
        in_specs=[vmem, vmem, hbm],
        out_specs=hbm,
        scratch_shapes=[
            pltpu.VMEM(early.shape, early.dtype),
            pltpu.VMEM(out.shape, out.dtype),
            pltpu.SemaphoreType.DMA((blocks,)),
            pltpu.SemaphoreType.DMA((blocks,)),
        ],
        cost_estimate=pl.CostEstimate(
            flops=2 * rows * late.shape[0] * width, bytes_accessed=4 * late.size, transcendentals=0
        ),
        compiler_params=pltpu.CompilerParams(vmem_limit_bytes=12 << 20),
    )(pltpu.with_memory_space_constraint(where, pltpu.HBM), late, pltpu.with_memory_space_constraint(early, pltpu.HBM))


def exchange(blocks):
    return lax.all_to_all(blocks, "group", split_axis=0, concat_axis=0, tiled=True)


def local(stem_blocks, cap_tensor, slot_rows, counts):
    cuts, groups = lax.axis_size("cuts"), lax.axis_size("group")
    group_total, own_rows, width = stem_blocks.shape[1:]
    mine = group_total // groups
    slot_total = slot_rows.shape[1]
    share = slot_total // cuts
    stem = stem_blocks.reshape(group_total * own_rows, width)
    terms = terms_of(stem, cap_tensor[0])
    width = terms.shape[1]

    positions = jnp.arange(slot_total, dtype=jnp.int32)
    marked = jnp.where(positions[None, :] < counts[:, None], slot_rows, -1)
    me = lax.axis_index("cuts").astype(jnp.int32)
    doubled = jnp.concatenate([marked, marked], axis=1)
    turned = lax.dynamic_slice_in_dim(doubled, (me + 1) * share, slot_total, 1)

    def all_rows():
        return static_plan(terms.reshape(group_total, own_rows, width), turned, cuts)

    unfit = mine * own_rows != 2 * LANES or LANES % own_rows or groups > LANES or share * mine % (STEP * LANES)
    if cuts != 2 or unfit:
        return all_rows()

    plane = me[None]
    flags = needs(slot_rows, counts, own_rows, groups)
    flags = exchange(flags.reshape(groups, KINDS, LANES))
    level = jnp.max(flags[:, 6, :].astype(jnp.float32)).astype(jnp.int32)
    flags = flags.reshape(groups * KINDS, LANES)
    by_owner = terms.reshape(groups, mine * own_rows, width)
    own_slots = turned[:, (cuts - 1) * share :]

    def needed_rows(early, late):
        first, send, keep = pack(plane, flags, by_owner, early, late)
        other = lax.ppermute(send, "cuts", [(0, 1), (1, 0)])
        own_early = exchange(first).reshape(groups * early, width)
        own_early, summed = lax.optimization_barrier((own_early, add(keep, other)))
        other_early = lax.ppermute(own_early, "cuts", [(1, 0)])
        own_late = exchange(summed).reshape(groups * late, width)
        where_early, where_late = places(plane, own_slots, own_rows, early, late)
        sums = early_part(where_early, own_early, other_early)
        return late_part(where_late, own_late, sums, mine)

    plans = [functools.partial(needed_rows, *sizes) for sizes in LADDER]
    return lax.switch(level, plans + [all_rows])


def solution(mesh):
    in_specs = (
        P("cuts", None, "group", None),
        P("cuts", None, None, None),
        P("group", None),
        P("group"),
    )
    out_specs = P("cuts", "group", None)
    return jax.shard_map(local, mesh=mesh, in_specs=in_specs, out_specs=out_specs, check_vma=False)
```

```python
import functools

import jax
import jax.numpy as jnp
from jax import lax
from jax.experimental import pallas as pl
from jax.experimental.pallas import tpu as pltpu
from jax.sharding import PartitionSpec as P


def terms_kernel(rows_ref, pair_ref, out_ref, matrix):
    half = pair_ref.shape[1]

    @pl.when(pl.program_id(0) == 0)
    def _():
        real_part, imag_part = pair_ref[0], pair_ref[1]
        matrix[:half, :half] = real_part
        matrix[:half, half:] = imag_part
        matrix[half:, :half] = -imag_part
        matrix[half:, half:] = real_part

    out_ref[...] = dot(rows_ref[...], matrix[...]).astype(out_ref.dtype)


def terms_of(rows, pair):
    total, width = rows.shape
    block = min(2048, total)
    out_width = 2 * pair.shape[2]
    return pl.pallas_call(
        terms_kernel,
        grid=(total // block,),
        out_shape=jax.ShapeDtypeStruct((total, out_width), rows.dtype),
        in_specs=[pl.BlockSpec((block, width), lambda i: (i, 0)), pl.BlockSpec(pair.shape, lambda i: (0, 0, 0))],
        out_specs=pl.BlockSpec((block, out_width), lambda i: (i, 0)),
        scratch_shapes=[pltpu.VMEM((width, out_width), rows.dtype)],
        cost_estimate=pl.CostEstimate(
            flops=2 * total * width * out_width, bytes_accessed=4 * rows.size, transcendentals=0
        ),
        compiler_params=pltpu.CompilerParams(vmem_limit_bytes=16 << 20),
    )(pltpu.with_memory_space_constraint(rows, pltpu.HBM), pltpu.with_memory_space_constraint(pair, pltpu.HBM))


def select_kernel(block, share, terms_ref, slots_ref, *outs):
    columns = iota((block, terms_ref.shape[0]), 1)
    for part, out in enumerate(outs):
        for start in range(0, share, block):
            chosen = mark(columns == slots_ref[pl.ds(part * share + start, block), :])
            out[pl.ds(start, block), :] = dot(chosen, terms_ref[...]).astype(out.dtype)


def select(terms, slots, parts):
    row_total, width = terms.shape
    slot_total = slots.shape[0]
    share = slot_total // parts
    return pl.pallas_call(
        functools.partial(select_kernel, min(256, share), share),
        out_shape=[jax.ShapeDtypeStruct((share, width), terms.dtype)] * parts,
        in_specs=[pl.BlockSpec(memory_space=pltpu.VMEM)] * 2,
        out_specs=[pl.BlockSpec(memory_space=pltpu.VMEM)] * parts,
        cost_estimate=pl.CostEstimate(
            flops=2 * row_total * width * slot_total,
            bytes_accessed=2 * (terms.size + slot_total * width),
            transcendentals=0,
        ),
        compiler_params=pltpu.CompilerParams(vmem_limit_bytes=24 << 20),
    )(terms, slots)


def static_plan(terms, turned, cuts):
    groups = lax.axis_size("group")
    group_total, own_rows, width = terms.shape
    mine = group_total // groups
    by_owner = terms.reshape(groups, mine, own_rows, width)
    sums, selected = [], []
    for k in range(mine):
        outgoing = by_owner[:, k]
        if k >= 2:
            outgoing, selected[k - 2] = lax.optimization_barrier((outgoing, selected[k - 2]))
        got = lax.all_to_all(outgoing, "group", split_axis=0, concat_axis=0, tiled=True)
        parts = select(got.reshape(groups * own_rows, width), turned[k][:, None], cuts)
        selected.append(parts)
    for parts in selected:
        total = parts[-1].astype(jnp.float32)
        for step in range(1, cuts):
            ring = [(i, (i + step) % cuts) for i in range(cuts)]
            total = total + lax.ppermute(parts[step - 1], "cuts", ring).astype(jnp.float32)
        sums.append(total.astype(terms.dtype))
    return jnp.stack(sums, axis=1)


KINDS = 8
LANES = 128
STEP = 8
PART = 2
EARLY, LATE = 64, 64
ADD_BYTES, EARLY_BYTES = 1<<34, 1<<34


def dot(a, b):
    return jnp.dot(a, b, preferred_element_type=jnp.float32)


def dot_nt(a, b):
    return lax.dot_general(a, b, (((1,), (1,)), ((), ())), preferred_element_type=jnp.float32)


def iota(shape, dim):
    return lax.broadcasted_iota(jnp.int32, shape, dim)


def mark(condition):
    return jnp.where(condition, 1.0, 0.0).astype(jnp.bfloat16)


def needs_kernel(own_rows, early, late, slots_ref, counts_ref, flags_ref):
    mine, slot_total = slots_ref.shape
    side = flags_ref.shape[0]
    hits = jnp.zeros((side, LANES), jnp.float32)
    place = iota((1, slot_total), 1)
    down = iota((side, slot_total), 0)
    across = iota((LANES, slot_total), 0)
    per = LANES // own_rows
    for k in range(mine):
        slots = slots_ref[k : k + 1, :]
        half = jnp.where(place >= slot_total // 2, 2, 0)
        row_key = (slots // own_rows) * KINDS + half + k // per
        row_key = jnp.where(place < counts_ref[k], row_key, -1)
        lane_key = slots % own_rows + (k % per) * own_rows
        hits = hits + dot_nt(mark(down == row_key), mark(across == lane_key))
    flags = jnp.minimum(hits, 1.0)
    row, column = iota((side, side), 0), iota((side, side), 1)
    kind, back = row % KINDS, row - column
    first = (kind == 4) & ((back == 4) | (back == 3))
    second = (kind == 5) & ((back == 3) | (back == 2))
    sums = dot(flags.astype(jnp.bfloat16), jnp.ones((LANES, LANES), jnp.bfloat16))
    counted = dot(mark(first | second), sums.astype(jnp.bfloat16))
    kind = iota((side, LANES), 0) % KINDS
    room = jnp.where(kind == 4, 1.0 * (early + late), 1.0 * late)
    spill = jnp.max(jnp.where((kind == 4) | (kind == 5), counted - room, 0.0))
    flags_ref[...] = jnp.where(kind == 6, jnp.where(spill > 0.0, 1.0, 0.0), flags).astype(flags_ref.dtype)


def needs(slot_rows, counts, own_rows, early, late, groups):
    return pl.pallas_call(
        functools.partial(needs_kernel, own_rows, early, late),
        out_shape=jax.ShapeDtypeStruct((groups * KINDS, LANES), jnp.bfloat16),
        in_specs=[pl.BlockSpec(memory_space=pltpu.VMEM), pl.BlockSpec(memory_space=pltpu.SMEM)],
        out_specs=pl.BlockSpec(memory_space=pltpu.VMEM),
        cost_estimate=pl.CostEstimate(flops=1 << 28, bytes_accessed=1 << 17, transcendentals=0),
    )(slot_rows, counts)


def keys_of(flags):
    side = flags.shape[0]
    marks = flags
    lower = mark(iota((LANES, LANES), 0) < iota((LANES, LANES), 1))
    inside = dot(marks, lower)
    totals = dot(marks, jnp.ones((LANES, LANES), jnp.bfloat16))
    row, column = iota((side, side), 0), iota((side, side), 1)
    follows = ((row % KINDS == 1) | (row % KINDS == 3)) & (row - column == 1)
    ranks = inside + dot(mark(follows), totals.astype(jnp.bfloat16))
    return jnp.where(flags.astype(jnp.float32) > 0.0, ranks, -1.0)


def chosen_rows(capacity, upper, lower):
    rank = iota((capacity, LANES), 0).astype(jnp.float32)
    return jnp.concatenate([mark(rank == upper), mark(rank == lower)], axis=1)


def pack_kernel(plane_ref, flags_ref, terms_ref, early_ref, send_ref, keep_ref, keys_ref):
    batch, early, _ = early_ref.shape
    late = send_ref.shape[1]
    step = pl.program_id(0)

    @pl.when(step == 0)
    def _():
        keys_ref[...] = keys_of(flags_ref[...])

    plane = plane_ref[0]
    for i in range(batch):
        keys = keys_ref[pl.ds((step * batch + i) * KINDS, KINDS), :]
        second = keys[2:3], keys[3:4]
        beyond = keys[0:1] - early, keys[1:2] - early
        sent = [jnp.where(plane == 0, b, a) for a, b in zip(beyond, second)]
        kept = [jnp.where(plane == 0, a, b) for a, b in zip(beyond, second)]
        chosen = [chosen_rows(late, *sent), chosen_rows(late, *kept), chosen_rows(early, keys[0:1], keys[1:2])]
        packed = dot(jnp.concatenate(chosen, axis=0), terms_ref[i]).astype(early_ref.dtype)
        send_ref[i] = packed[:late]
        keep_ref[i] = packed[late : 2 * late]
        early_ref[i] = packed[2 * late :]


def pack(plane, flags, terms, early, late):
    groups, rows, width = terms.shape
    batch = 8 if groups % 8 == 0 else 1

    def out(capacity):
        block = pl.BlockSpec((batch, capacity, width), lambda i: (i, 0, 0))
        return jax.ShapeDtypeStruct((groups, capacity, width), terms.dtype), block

    shapes, blocks = zip(out(early), out(late), out(late))
    return pl.pallas_call(
        pack_kernel,
        grid=(groups // batch,),
        out_shape=shapes,
        in_specs=[
            pl.BlockSpec(memory_space=pltpu.SMEM),
            pl.BlockSpec(flags.shape, lambda i: (0, 0)),
            pl.BlockSpec((batch, rows, width), lambda i: (i, 0, 0)),
        ],
        out_specs=blocks,
        scratch_shapes=[pltpu.VMEM(flags.shape, jnp.float32)],
        cost_estimate=pl.CostEstimate(
            flops=2 * groups * (early + 2 * late) * rows * width, bytes_accessed=4 * terms.size, transcendentals=0
        ),
        compiler_params=pltpu.CompilerParams(vmem_limit_bytes=16 << 20),
    )(plane, flags, terms)


def add_kernel(a_ref, b_ref, out_ref):
    out_ref[...] = (a_ref[...].astype(jnp.float32) + b_ref[...].astype(jnp.float32)).astype(out_ref.dtype)


def add(a, b):
    vmem = pl.BlockSpec(memory_space=pltpu.VMEM)
    return pl.pallas_call(
        add_kernel,
        out_shape=jax.ShapeDtypeStruct(a.shape, a.dtype),
        in_specs=[vmem] * 2,
        out_specs=vmem,
        cost_estimate=pl.CostEstimate(flops=ADD_BYTES, bytes_accessed=ADD_BYTES, transcendentals=0),
        compiler_params=pltpu.CompilerParams(vmem_limit_bytes=8 << 20),
    )(a, b)


def places_kernel(own_rows, early, late, plane_ref, slots_ref, column_ref, early_ref, late_ref):
    mine, share = slots_ref.shape
    rows = mine * own_rows
    down = iota((own_rows, share), 0)
    across = iota((LANES, share), 0)
    wanted = []
    for k in range(mine):
        slots = slots_ref[k : k + 1, :]
        source = jnp.where(slots >= 0, slots // own_rows, -1)
        wanted.append(dot_nt(mark(down == slots % own_rows), mark(across == source)))
    wanted = jnp.minimum(jnp.concatenate(wanted, axis=0), 1.0)
    before = mark(iota((rows, rows), 0) > iota((rows, rows), 1))
    ranks = dot(before, wanted.astype(jnp.bfloat16)).astype(jnp.bfloat16)
    shift = plane_ref[0] * early
    group = iota((LANES, 1), 0) % mine
    lane = iota((LANES, LANES), 1)
    for block in range(mine * share // LANES):
        at, spot = block // STEP, block % STEP
        if spot == 0:
            in_early = jnp.full((LANES, LANES), -1, jnp.int32)
            in_late = in_early
        slots = column_ref[:, block : block + 1]
        source = slots // own_rows
        row = jnp.where(slots >= 0, group * own_rows + slots % own_rows, -1)
        looked = dot(mark(iota((LANES, rows), 1) == row), ranks)
        found = jnp.where(lane == source, looked, 0.0)
        rank = jnp.sum(found, axis=1, keepdims=True).astype(jnp.int32) + shift
        live, low = slots >= 0, rank < early
        in_early = jnp.where((lane == spot) & live & low, source * early + rank, in_early)
        in_late = jnp.where((lane == spot) & live & ~low, source * late + rank - early, in_late)
        if spot == STEP - 1:
            early_ref[at] = in_early
            late_ref[at] = in_late


def places(plane, own_slots, own_rows, early, late):
    column = own_slots.T.reshape(-1, LANES).T
    vmem = pl.BlockSpec(memory_space=pltpu.VMEM)
    return pl.pallas_call(
        functools.partial(places_kernel, own_rows, early, late),
        out_shape=[jax.ShapeDtypeStruct((own_slots.size // (STEP * LANES), LANES, LANES), jnp.int32)] * 2,
        in_specs=[pl.BlockSpec(memory_space=pltpu.SMEM), vmem, vmem],
        out_specs=[vmem] * 2,
        cost_estimate=pl.CostEstimate(flops=1 << 28, bytes_accessed=1 << 18, transcendentals=0),
    )(plane, own_slots, column)


def chosen_places(places, part, total):
    columns = iota((LANES, total), 1)
    first = part * PART
    return jnp.concatenate([mark(columns == places[:, first + i : first + i + 1]) for i in range(PART)], axis=0)


def early_kernel(places_ref, own_ref, other_ref, out_ref, table):
    both = own_ref[...].astype(jnp.float32) + other_ref[...].astype(jnp.float32)
    table[...] = both.astype(table.dtype)
    size = PART * LANES
    for block in range(places_ref.shape[0]):
        for part in range(STEP // PART):
            chosen = chosen_places(places_ref.at[block], part, table.shape[0])
            at = (block * STEP + part * PART) * LANES
            out_ref[at : at + size, :] = dot(chosen, table[...]).astype(out_ref.dtype)


def late_kernel(places_ref, late_ref, early_ref, out_ref):
    size = PART * LANES
    per = out_ref.shape[0] // (STEP // PART)
    for part in range(STEP // PART):
        chosen = chosen_places(places_ref.at[0], part, late_ref.shape[0])
        early = early_ref[part * size : (part + 1) * size, :].astype(jnp.float32)
        total = (dot(chosen, late_ref[...]) + early).astype(out_ref.dtype)
        out_ref[part * per : (part + 1) * per] = total.reshape(per, *out_ref.shape[1:])


def early_part(where, own, other):
    rows, width = own.shape
    slots = where.shape[0] * STEP * LANES
    vmem = pl.BlockSpec(memory_space=pltpu.VMEM)
    return pl.pallas_call(
        early_kernel,
        out_shape=jax.ShapeDtypeStruct((slots, width), own.dtype),
        in_specs=[vmem] * 3,
        out_specs=vmem,
        scratch_shapes=[pltpu.VMEM((rows, width), own.dtype)],
        cost_estimate=pl.CostEstimate(flops=EARLY_BYTES, bytes_accessed=EARLY_BYTES, transcendentals=0),
        compiler_params=pltpu.CompilerParams(vmem_limit_bytes=12 << 20),
    )(pltpu.with_memory_space_constraint(where, pltpu.HBM), own, other)


def late_part(where, late, early, mine):
    rows, width = early.shape
    blocks = where.shape[0]
    step = STEP * LANES
    return pl.pallas_call(
        late_kernel,
        grid=(blocks,),
        out_shape=jax.ShapeDtypeStruct((rows // mine, mine, width), early.dtype),
        in_specs=[
            pl.BlockSpec((1, LANES, LANES), lambda i: (i, 0, 0)),
            pl.BlockSpec(late.shape, lambda i: (0, 0)),
            pl.BlockSpec((step, width), lambda i: (i, 0)),
        ],
        out_specs=pl.BlockSpec((step // mine, mine, width), lambda i: (i, 0, 0)),
        cost_estimate=pl.CostEstimate(
            flops=2 * rows * late.shape[0] * width, bytes_accessed=4 * late.size, transcendentals=0
        ),
        compiler_params=pltpu.CompilerParams(vmem_limit_bytes=12 << 20),
    )(pltpu.with_memory_space_constraint(where, pltpu.HBM), late, early)


def exchange(blocks):
    return lax.all_to_all(blocks, "group", split_axis=0, concat_axis=0, tiled=True)


def local(stem_blocks, cap_tensor, slot_rows, counts):
    cuts, groups = lax.axis_size("cuts"), lax.axis_size("group")
    group_total, own_rows, width = stem_blocks.shape[1:]
    mine = group_total // groups
    slot_total = slot_rows.shape[1]
    share = slot_total // cuts
    stem = stem_blocks.reshape(group_total * own_rows, width)
    terms = terms_of(stem, cap_tensor[0])
    width = terms.shape[1]

    positions = jnp.arange(slot_total, dtype=jnp.int32)
    marked = jnp.where(positions[None, :] < counts[:, None], slot_rows, -1)
    me = lax.axis_index("cuts").astype(jnp.int32)
    doubled = jnp.concatenate([marked, marked], axis=1)
    turned = lax.dynamic_slice_in_dim(doubled, (me + 1) * share, slot_total, 1)

    def all_rows():
        return static_plan(terms.reshape(group_total, own_rows, width), turned, cuts)

    unfit = mine * own_rows != 2 * LANES or LANES % own_rows or groups > LANES or share * mine % (STEP * LANES)
    if cuts != 2 or unfit:
        return all_rows()

    early, late = EARLY, LATE
    plane = me[None]
    flags = needs(slot_rows, counts, own_rows, early, late, groups)
    flags = exchange(flags.reshape(groups, KINDS, LANES))
    spilled = jnp.max(flags[:, 6, :].astype(jnp.float32)) > 0.0
    by_owner = terms.reshape(groups, mine * own_rows, width)
    first, send, keep = pack(plane, flags.reshape(groups * KINDS, LANES), by_owner, early, late)
    other = lax.ppermute(send, "cuts", [(0, 1), (1, 0)])
    own_early = exchange(first).reshape(groups * early, width)
    own_early, summed = lax.optimization_barrier((own_early, add(keep, other)))
    other_early = lax.ppermute(own_early, "cuts", [(0, 1), (1, 0)])
    own_late = exchange(summed).reshape(groups * late, width)
    where_early, where_late = places(plane, turned[:, (cuts - 1) * share :], own_rows, early, late)
    sums = early_part(where_early, own_early, other_early)
    return lax.cond(spilled, all_rows, lambda: late_part(where_late, own_late, sums, mine))


def solution(mesh):
    in_specs = (
        P("cuts", None, "group", None),
        P("cuts", None, None, None),
        P("group", None),
        P("group"),
    )
    out_specs = P("cuts", "group", None)
    return jax.shard_map(local, mesh=mesh, in_specs=in_specs, out_specs=out_specs, check_vma=False)
```

```python
import functools

import jax
import jax.numpy as jnp
from jax import lax
from jax.experimental import pallas as pl
from jax.experimental.pallas import tpu as pltpu
from jax.sharding import PartitionSpec as P


def build_matrix(pair_ref, matrix):
    half = pair_ref.shape[1]
    real_part, imag_part = pair_ref[0], pair_ref[1]
    matrix[:half, :half] = real_part
    matrix[:half, half:] = imag_part
    matrix[half:, :half] = -imag_part
    matrix[half:, half:] = real_part


def terms_kernel(rows_ref, pair_ref, out_ref, matrix):
    @pl.when(pl.program_id(0) == 0)
    def _():
        build_matrix(pair_ref, matrix)

    out_ref[...] = dot(rows_ref[...], matrix[...]).astype(out_ref.dtype)


def terms_of(rows, pair):
    total, width = rows.shape
    block = min(2048, total)
    out_width = 2 * pair.shape[2]
    return pl.pallas_call(
        terms_kernel,
        grid=(total // block,),
        out_shape=jax.ShapeDtypeStruct((total, out_width), rows.dtype),
        in_specs=[pl.BlockSpec((block, width), lambda i: (i, 0)), pl.BlockSpec(pair.shape, lambda i: (0, 0, 0))],
        out_specs=pl.BlockSpec((block, out_width), lambda i: (i, 0)),
        scratch_shapes=[pltpu.VMEM((width, out_width), rows.dtype)],
        cost_estimate=pl.CostEstimate(
            flops=2 * total * width * out_width, bytes_accessed=4 * rows.size, transcendentals=0
        ),
        compiler_params=pltpu.CompilerParams(vmem_limit_bytes=16 << 20),
    )(pltpu.with_memory_space_constraint(rows, pltpu.HBM), pltpu.with_memory_space_constraint(pair, pltpu.HBM))


def select_kernel(block, share, terms_ref, slots_ref, *outs):
    columns = iota((block, terms_ref.shape[0]), 1)
    for part, out in enumerate(outs):
        for start in range(0, share, block):
            chosen = mark(columns == slots_ref[pl.ds(part * share + start, block), :])
            out[pl.ds(start, block), :] = dot(chosen, terms_ref[...]).astype(out.dtype)


def select(terms, slots, parts):
    row_total, width = terms.shape
    slot_total = slots.shape[0]
    share = slot_total // parts
    return pl.pallas_call(
        functools.partial(select_kernel, min(256, share), share),
        out_shape=[jax.ShapeDtypeStruct((share, width), terms.dtype)] * parts,
        in_specs=[pl.BlockSpec(memory_space=pltpu.VMEM)] * 2,
        out_specs=[pl.BlockSpec(memory_space=pltpu.VMEM)] * parts,
        cost_estimate=pl.CostEstimate(
            flops=2 * row_total * width * slot_total,
            bytes_accessed=2 * (terms.size + slot_total * width),
            transcendentals=0,
        ),
        compiler_params=pltpu.CompilerParams(vmem_limit_bytes=24 << 20),
    )(terms, slots)


def static_plan(terms, turned, cuts):
    groups = lax.axis_size("group")
    group_total, own_rows, width = terms.shape
    mine = group_total // groups
    by_owner = terms.reshape(groups, mine, own_rows, width)
    sums, selected = [], []
    for k in range(mine):
        outgoing = by_owner[:, k]
        if k >= 2:
            outgoing, selected[k - 2] = lax.optimization_barrier((outgoing, selected[k - 2]))
        got = lax.all_to_all(outgoing, "group", split_axis=0, concat_axis=0, tiled=True)
        parts = select(got.reshape(groups * own_rows, width), turned[k][:, None], cuts)
        selected.append(parts)
    for parts in selected:
        total = parts[-1].astype(jnp.float32)
        for step in range(1, cuts):
            ring = [(i, (i + step) % cuts) for i in range(cuts)]
            total = total + lax.ppermute(parts[step - 1], "cuts", ring).astype(jnp.float32)
        sums.append(total.astype(terms.dtype))
    return jnp.stack(sums, axis=1)


KINDS = 8
LANES = 128
STEP = 8
PART = 2
EARLY, LATE = 64, 64
ADD_BYTES, EARLY_BYTES = 1<<34, 1<<34


def dot(a, b):
    return jnp.dot(a, b, preferred_element_type=jnp.float32)


def dot_nt(a, b):
    return lax.dot_general(a, b, (((1,), (1,)), ((), ())), preferred_element_type=jnp.float32)


def iota(shape, dim):
    return lax.broadcasted_iota(jnp.int32, shape, dim)


def mark(condition):
    return jnp.where(condition, 1.0, 0.0).astype(jnp.bfloat16)


def needs_kernel(own_rows, early, late, slots_ref, counts_ref, flags_ref):
    mine, slot_total = slots_ref.shape
    side = flags_ref.shape[0]
    hits = jnp.zeros((side, LANES), jnp.float32)
    place = iota((1, slot_total), 1)
    down = iota((side, slot_total), 0)
    across = iota((LANES, slot_total), 0)
    per = LANES // own_rows
    for k in range(mine):
        slots = slots_ref[k : k + 1, :]
        half = jnp.where(place >= slot_total // 2, 2, 0)
        row_key = (slots // own_rows) * KINDS + half + k // per
        row_key = jnp.where(place < counts_ref[k], row_key, -1)
        lane_key = slots % own_rows + (k % per) * own_rows
        hits = hits + dot_nt(mark(down == row_key), mark(across == lane_key))
    flags = jnp.minimum(hits, 1.0)
    sums = jnp.sum(flags, axis=1, keepdims=True)
    pairs = sums + jnp.concatenate([sums[1:], sums[:1]], axis=0)
    kind = iota((side, 1), 0) % KINDS
    over = jnp.where(kind == 0, pairs - (early + late), jnp.where(kind == 2, pairs - late, 0.0))
    spill = jnp.where(jnp.max(over) > 0.0, 1.0, 0.0)
    flags_ref[...] = jnp.where(iota((side, LANES), 0) % KINDS == 6, spill, flags).astype(flags_ref.dtype)


def needs(slot_rows, counts, own_rows, early, late, groups):
    return pl.pallas_call(
        functools.partial(needs_kernel, own_rows, early, late),
        out_shape=jax.ShapeDtypeStruct((groups * KINDS, LANES), jnp.bfloat16),
        in_specs=[pl.BlockSpec(memory_space=pltpu.VMEM), pl.BlockSpec(memory_space=pltpu.SMEM)],
        out_specs=pl.BlockSpec(memory_space=pltpu.VMEM),
        cost_estimate=pl.CostEstimate(flops=1 << 28, bytes_accessed=1 << 17, transcendentals=0),
    )(slot_rows, counts)


def keys_of(flags):
    side = flags.shape[0]
    marks = flags
    lower = mark(iota((LANES, LANES), 0) < iota((LANES, LANES), 1))
    inside = dot(marks, lower)
    totals = dot(marks, jnp.ones((LANES, LANES), jnp.bfloat16))
    row, column = iota((side, side), 0), iota((side, side), 1)
    follows = ((row % KINDS == 1) | (row % KINDS == 3)) & (row - column == 1)
    ranks = inside + dot(mark(follows), totals.astype(jnp.bfloat16))
    return jnp.where(flags.astype(jnp.float32) > 0.0, ranks, -1.0)


def chosen_rows(capacity, upper, lower):
    rank = iota((capacity, LANES), 0).astype(jnp.float32)
    return jnp.concatenate([mark(rank == upper), mark(rank == lower)], axis=1)


def pack_kernel(lists, early, plane_ref, flags_ref, stem_ref, pair_ref, *refs):
    outs, (keys_ref, matrix, picked) = refs[: len(lists)], refs[len(lists) :]
    batch = stem_ref.shape[0]
    step = pl.program_id(0)

    @pl.when(step == 0)
    def _():
        keys_ref[...] = keys_of(flags_ref[...])
        build_matrix(pair_ref, matrix)

    plane = plane_ref[0]
    total = sum(out.shape[1] for out in outs)
    for i in range(batch):
        keys = keys_ref[pl.ds((step * batch + i) * KINDS, KINDS), :]
        second = keys[2:3], keys[3:4]
        beyond = keys[0:1] - early, keys[1:2] - early
        keyed = {
            "first": (keys[0:1], keys[1:2]),
            "send": [jnp.where(plane == 0, b, a) for a, b in zip(beyond, second)],
            "keep": [jnp.where(plane == 0, a, b) for a, b in zip(beyond, second)],
        }
        chosen = [chosen_rows(out.shape[1], *keyed[name]) for name, out in zip(lists, outs)]
        picked[i * total : (i + 1) * total, :] = dot(jnp.concatenate(chosen, axis=0), stem_ref[i]).astype(picked.dtype)
    terms = dot(picked[...], matrix[...]).astype(picked.dtype)
    at = 0
    for i in range(batch):
        for out in outs:
            out[i] = terms[at : at + out.shape[1]]
            at += out.shape[1]


def pack(lists, plane, flags, stem, pair, early, late):
    groups, rows, width = stem.shape
    batch = 8 if groups % 8 == 0 else 1
    out_width = 2 * pair.shape[2]
    sizes = [early if name == "first" else late for name in lists]
    return pl.pallas_call(
        functools.partial(pack_kernel, lists, early),
        grid=(groups // batch,),
        out_shape=[jax.ShapeDtypeStruct((groups, size, out_width), stem.dtype) for size in sizes],
        in_specs=[
            pl.BlockSpec(memory_space=pltpu.SMEM),
            pl.BlockSpec(flags.shape, lambda i: (0, 0)),
            pl.BlockSpec((batch, rows, width), lambda i: (i, 0, 0)),
            pl.BlockSpec(pair.shape, lambda i: (0, 0, 0)),
        ],
        out_specs=[pl.BlockSpec((batch, size, out_width), lambda i: (i, 0, 0)) for size in sizes],
        scratch_shapes=[
            pltpu.VMEM(flags.shape, jnp.float32),
            pltpu.VMEM((width, out_width), stem.dtype),
            pltpu.VMEM((batch * sum(sizes), width), stem.dtype),
        ],
        cost_estimate=pl.CostEstimate(
            flops=2 * groups * sum(sizes) * (rows + out_width) * width, bytes_accessed=3 * stem.size, transcendentals=0
        ),
        compiler_params=pltpu.CompilerParams(vmem_limit_bytes=20 << 20),
    )(plane, flags, pltpu.with_memory_space_constraint(stem, pltpu.HBM), pltpu.with_memory_space_constraint(pair, pltpu.HBM))


def add_kernel(a_ref, b_ref, out_ref):
    out_ref[...] = (a_ref[...].astype(jnp.float32) + b_ref[...].astype(jnp.float32)).astype(out_ref.dtype)


def add(a, b):
    vmem = pl.BlockSpec(memory_space=pltpu.VMEM)
    return pl.pallas_call(
        add_kernel,
        out_shape=jax.ShapeDtypeStruct(a.shape, a.dtype),
        in_specs=[vmem] * 2,
        out_specs=vmem,
        cost_estimate=pl.CostEstimate(flops=ADD_BYTES, bytes_accessed=ADD_BYTES, transcendentals=0),
        compiler_params=pltpu.CompilerParams(vmem_limit_bytes=8 << 20),
    )(a, b)


def places_kernel(own_rows, early, late, plane_ref, slots_ref, column_ref, early_ref, late_ref):
    mine, share = slots_ref.shape
    rows = mine * own_rows
    down = iota((own_rows, share), 0)
    across = iota((LANES, share), 0)
    wanted = []
    for k in range(mine):
        slots = slots_ref[k : k + 1, :]
        source = jnp.where(slots >= 0, slots // own_rows, -1)
        wanted.append(dot_nt(mark(down == slots % own_rows), mark(across == source)))
    wanted = jnp.minimum(jnp.concatenate(wanted, axis=0), 1.0)
    before = mark(iota((rows, rows), 0) > iota((rows, rows), 1))
    ranks = dot(before, wanted.astype(jnp.bfloat16)).astype(jnp.bfloat16)
    shift = plane_ref[0] * early
    group = iota((LANES, 1), 0) % mine
    lane = iota((LANES, LANES), 1)
    for block in range(mine * share // LANES):
        at, spot = block // STEP, block % STEP
        if spot == 0:
            in_early = jnp.full((LANES, LANES), -1, jnp.int32)
            in_late = in_early
        slots = column_ref[:, block : block + 1]
        source = slots // own_rows
        row = jnp.where(slots >= 0, group * own_rows + slots % own_rows, -1)
        looked = dot(mark(iota((LANES, rows), 1) == row), ranks)
        found = jnp.where(lane == source, looked, 0.0)
        rank = jnp.sum(found, axis=1, keepdims=True).astype(jnp.int32) + shift
        live, low = slots >= 0, rank < early
        in_early = jnp.where((lane == spot) & live & low, source * early + rank, in_early)
        in_late = jnp.where((lane == spot) & live & ~low, source * late + rank - early, in_late)
        if spot == STEP - 1:
            early_ref[at] = in_early
            late_ref[at] = in_late


def places(plane, own_slots, own_rows, early, late):
    column = own_slots.T.reshape(-1, LANES).T
    vmem = pl.BlockSpec(memory_space=pltpu.VMEM)
    return pl.pallas_call(
        functools.partial(places_kernel, own_rows, early, late),
        out_shape=[jax.ShapeDtypeStruct((own_slots.size // (STEP * LANES), LANES, LANES), jnp.int32)] * 2,
        in_specs=[pl.BlockSpec(memory_space=pltpu.SMEM), vmem, vmem],
        out_specs=[vmem] * 2,
        cost_estimate=pl.CostEstimate(flops=1 << 28, bytes_accessed=1 << 18, transcendentals=0),
    )(plane, own_slots, column)


def chosen_places(places, part, total):
    columns = iota((LANES, total), 1)
    first = part * PART
    return jnp.concatenate([mark(columns == places[:, first + i : first + i + 1]) for i in range(PART)], axis=0)


def early_kernel(places_ref, own_ref, other_ref, out_ref, table):
    both = own_ref[...].astype(jnp.float32) + other_ref[...].astype(jnp.float32)
    table[...] = both.astype(table.dtype)
    size = PART * LANES
    for block in range(places_ref.shape[0]):
        for part in range(STEP // PART):
            chosen = chosen_places(places_ref.at[block], part, table.shape[0])
            at = (block * STEP + part * PART) * LANES
            out_ref[at : at + size, :] = dot(chosen, table[...]).astype(out_ref.dtype)


def late_kernel(places_ref, late_ref, early_ref, out_ref):
    size = PART * LANES
    per = out_ref.shape[0] // (STEP // PART)
    for part in range(STEP // PART):
        chosen = chosen_places(places_ref.at[0], part, late_ref.shape[0])
        early = early_ref[part * size : (part + 1) * size, :].astype(jnp.float32)
        total = (dot(chosen, late_ref[...]) + early).astype(out_ref.dtype)
        out_ref[part * per : (part + 1) * per] = total.reshape(per, *out_ref.shape[1:])


def early_part(where, own, other):
    rows, width = own.shape
    slots = where.shape[0] * STEP * LANES
    vmem = pl.BlockSpec(memory_space=pltpu.VMEM)
    return pl.pallas_call(
        early_kernel,
        out_shape=jax.ShapeDtypeStruct((slots, width), own.dtype),
        in_specs=[vmem] * 3,
        out_specs=vmem,
        scratch_shapes=[pltpu.VMEM((rows, width), own.dtype)],
        cost_estimate=pl.CostEstimate(flops=EARLY_BYTES, bytes_accessed=EARLY_BYTES, transcendentals=0),
        compiler_params=pltpu.CompilerParams(vmem_limit_bytes=12 << 20),
    )(pltpu.with_memory_space_constraint(where, pltpu.HBM), own, other)


def late_part(where, late, early, mine):
    rows, width = early.shape
    blocks = where.shape[0]
    step = STEP * LANES
    return pl.pallas_call(
        late_kernel,
        grid=(blocks,),
        out_shape=jax.ShapeDtypeStruct((rows // mine, mine, width), early.dtype),
        in_specs=[
            pl.BlockSpec((1, LANES, LANES), lambda i: (i, 0, 0)),
            pl.BlockSpec(late.shape, lambda i: (0, 0)),
            pl.BlockSpec((step, width), lambda i: (i, 0)),
        ],
        out_specs=pl.BlockSpec((step // mine, mine, width), lambda i: (i, 0, 0)),
        cost_estimate=pl.CostEstimate(
            flops=2 * rows * late.shape[0] * width, bytes_accessed=4 * late.size, transcendentals=0
        ),
        compiler_params=pltpu.CompilerParams(vmem_limit_bytes=12 << 20),
    )(pltpu.with_memory_space_constraint(where, pltpu.HBM), late, early)


def exchange(blocks):
    return lax.all_to_all(blocks, "group", split_axis=0, concat_axis=0, tiled=True)


def local(stem_blocks, cap_tensor, slot_rows, counts):
    cuts, groups = lax.axis_size("cuts"), lax.axis_size("group")
    group_total, own_rows, width = stem_blocks.shape[1:]
    mine = group_total // groups
    slot_total = slot_rows.shape[1]
    share = slot_total // cuts
    stem = stem_blocks.reshape(group_total * own_rows, width)
    pair = cap_tensor[0]

    positions = jnp.arange(slot_total, dtype=jnp.int32)
    marked = jnp.where(positions[None, :] < counts[:, None], slot_rows, -1)
    me = lax.axis_index("cuts").astype(jnp.int32)
    doubled = jnp.concatenate([marked, marked], axis=1)
    turned = lax.dynamic_slice_in_dim(doubled, (me + 1) * share, slot_total, 1)

    def all_rows():
        terms = terms_of(stem, pair)
        return static_plan(terms.reshape(group_total, own_rows, terms.shape[1]), turned, cuts)

    unfit = mine * own_rows != 2 * LANES or LANES % own_rows or groups > LANES or share * mine % (STEP * LANES)
    if cuts != 2 or unfit:
        return all_rows()

    early, late = EARLY, LATE
    plane = me[None]
    flags = needs(slot_rows, counts, own_rows, early, late, groups)
    flags = exchange(flags.reshape(groups, KINDS, LANES))
    spilled = jnp.max(flags[:, 6, :].astype(jnp.float32)) > 0.0
    flags = flags.reshape(groups * KINDS, LANES)
    by_owner = stem.reshape(groups, mine * own_rows, width)
    first, send = pack(("first", "send"), plane, flags, by_owner, pair, early, late)
    (keep,) = pack(("keep",), plane, flags, by_owner, pair, early, late)
    other = lax.ppermute(send, "cuts", [(0, 1), (1, 0)])
    own_early = exchange(first).reshape(groups * early, first.shape[2])
    own_early, summed = lax.optimization_barrier((own_early, add(keep, other)))
    other_early = lax.ppermute(own_early, "cuts", [(0, 1), (1, 0)])
    own_late = exchange(summed).reshape(groups * late, summed.shape[2])
    where_early, where_late = places(plane, turned[:, (cuts - 1) * share :], own_rows, early, late)
    sums = early_part(where_early, own_early, other_early)
    return lax.cond(spilled, all_rows, lambda: late_part(where_late, own_late, sums, mine))


def solution(mesh):
    in_specs = (
        P("cuts", None, "group", None),
        P("cuts", None, None, None),
        P("group", None),
        P("group"),
    )
    out_specs = P("cuts", "group", None)
    return jax.shard_map(local, mesh=mesh, in_specs=in_specs, out_specs=out_specs, check_vma=False)
```

```python
import functools

import jax
import jax.numpy as jnp
from jax import lax
from jax.experimental import pallas as pl
from jax.experimental.pallas import tpu as pltpu
from jax.sharding import PartitionSpec as P


def build_matrix(pair_ref, matrix):
    half = pair_ref.shape[1]
    real_part, imag_part = pair_ref[0], pair_ref[1]
    matrix[:half, :half] = real_part
    matrix[:half, half:] = imag_part
    matrix[half:, :half] = -imag_part
    matrix[half:, half:] = real_part


def terms_kernel(rows_ref, pair_ref, out_ref, matrix):
    @pl.when(pl.program_id(0) == 0)
    def _():
        build_matrix(pair_ref, matrix)

    out_ref[...] = dot(rows_ref[...], matrix[...]).astype(out_ref.dtype)


def terms_of(rows, pair):
    total, width = rows.shape
    block = min(512, total)
    out_width = 2 * pair.shape[2]
    return pl.pallas_call(
        terms_kernel,
        grid=(total // block,),
        out_shape=jax.ShapeDtypeStruct((total, out_width), rows.dtype),
        in_specs=[pl.BlockSpec((block, width), lambda i: (i, 0)), pl.BlockSpec(pair.shape, lambda i: (0, 0, 0))],
        out_specs=pl.BlockSpec((block, out_width), lambda i: (i, 0)),
        scratch_shapes=[pltpu.VMEM((width, out_width), rows.dtype)],
        cost_estimate=pl.CostEstimate(
            flops=2 * total * width * out_width, bytes_accessed=4 * rows.size, transcendentals=0
        ),
        compiler_params=pltpu.CompilerParams(vmem_limit_bytes=16 << 20),
    )(pltpu.with_memory_space_constraint(rows, pltpu.HBM), pltpu.with_memory_space_constraint(pair, pltpu.HBM))


def select_kernel(block, share, terms_ref, slots_ref, *outs):
    columns = iota((block, terms_ref.shape[0]), 1)
    for part, out in enumerate(outs):

        @pl.loop(0, share // block)
        def _(step):
            start = pl.multiple_of(step * block, block)
            chosen = mark(columns == slots_ref[pl.ds(part * share + start, block), :])
            out[pl.ds(start, block), :] = dot(chosen, terms_ref[...]).astype(out.dtype)


def select(terms, slots, parts):
    row_total, width = terms.shape
    slot_total = slots.shape[0]
    share = slot_total // parts
    return pl.pallas_call(
        functools.partial(select_kernel, min(256, share), share),
        out_shape=[jax.ShapeDtypeStruct((share, width), terms.dtype)] * parts,
        in_specs=[pl.BlockSpec(memory_space=pltpu.VMEM)] * 2,
        out_specs=[pl.BlockSpec(memory_space=pltpu.VMEM)] * parts,
        cost_estimate=pl.CostEstimate(
            flops=2 * row_total * width * slot_total,
            bytes_accessed=2 * (terms.size + slot_total * width),
            transcendentals=0,
        ),
        compiler_params=pltpu.CompilerParams(vmem_limit_bytes=24 << 20),
    )(terms, slots)


def static_plan(terms, turned, cuts):
    groups = lax.axis_size("group")
    group_total, own_rows, width = terms.shape
    mine = group_total // groups
    by_owner = terms.reshape(groups, mine, own_rows, width)
    sums, selected = [], []
    for k in range(mine):
        outgoing = by_owner[:, k]
        if k >= 2:
            outgoing, selected[k - 2] = lax.optimization_barrier((outgoing, selected[k - 2]))
        got = lax.all_to_all(outgoing, "group", split_axis=0, concat_axis=0, tiled=True)
        parts = select(got.reshape(groups * own_rows, width), turned[k][:, None], cuts)
        selected.append(parts)
    for parts in selected:
        total = parts[-1].astype(jnp.float32)
        for step in range(1, cuts):
            ring = [(i, (i + step) % cuts) for i in range(cuts)]
            total = total + lax.ppermute(parts[step - 1], "cuts", ring).astype(jnp.float32)
        sums.append(total.astype(terms.dtype))
    return jnp.stack(sums, axis=1)


KINDS = 8
LANES = 128
STEP = 8
PART = 2
EARLY = 56
LATES = 56, 64, 72
ADD_BYTES, EARLY_BYTES = 1<<34, 1<<34


def dot(a, b):
    return jnp.dot(a, b, preferred_element_type=jnp.float32)


def dot_nt(a, b):
    return lax.dot_general(a, b, (((1,), (1,)), ((), ())), preferred_element_type=jnp.float32)


def iota(shape, dim):
    return lax.broadcasted_iota(jnp.int32, shape, dim)


def mark(condition):
    return jnp.where(condition, 1.0, 0.0).astype(jnp.bfloat16)


def needs_kernel(own_rows, slots_ref, counts_ref, flags_ref):
    mine, slot_total = slots_ref.shape
    side = flags_ref.shape[0]
    hits = jnp.zeros((side, LANES), jnp.float32)
    place = iota((1, slot_total), 1)
    down = iota((side, slot_total), 0)
    across = iota((LANES, slot_total), 0)
    per = LANES // own_rows
    for k in range(mine):
        slots = slots_ref[k : k + 1, :]
        half = jnp.where(place >= slot_total // 2, 2, 0)
        row_key = (slots // own_rows) * KINDS + half + k // per
        row_key = jnp.where(place < counts_ref[k], row_key, -1)
        lane_key = slots % own_rows + (k % per) * own_rows
        hits = hits + dot_nt(mark(down == row_key), mark(across == lane_key))
    flags = jnp.minimum(hits, 1.0)
    sums = jnp.sum(flags, axis=1, keepdims=True)
    pairs = sums + jnp.concatenate([sums[1:], sums[:1]], axis=0)
    kind = iota((side, 1), 0) % KINDS
    most = jnp.max(jnp.where(kind == 0, pairs - EARLY, jnp.where(kind == 2, pairs, 0.0)), axis=0, keepdims=True)
    level = sum(jnp.where(most > late, 1.0, 0.0) for late in LATES)
    flags_ref[...] = jnp.where(iota((side, LANES), 0) % KINDS == 6, level, flags).astype(flags_ref.dtype)


def needs(slot_rows, counts, own_rows, groups):
    return pl.pallas_call(
        functools.partial(needs_kernel, own_rows),
        out_shape=jax.ShapeDtypeStruct((groups * KINDS, LANES), jnp.bfloat16),
        in_specs=[pl.BlockSpec(memory_space=pltpu.VMEM), pl.BlockSpec(memory_space=pltpu.SMEM)],
        out_specs=pl.BlockSpec(memory_space=pltpu.VMEM),
        cost_estimate=pl.CostEstimate(flops=1 << 28, bytes_accessed=1 << 17, transcendentals=0),
    )(slot_rows, counts)


def keys_of(flags):
    side = flags.shape[0]
    marks = flags
    lower = mark(iota((LANES, LANES), 0) < iota((LANES, LANES), 1))
    inside = dot(marks, lower)
    totals = dot(marks, jnp.ones((LANES, LANES), jnp.bfloat16))
    row, column = iota((side, side), 0), iota((side, side), 1)
    follows = ((row % KINDS == 1) | (row % KINDS == 3)) & (row - column == 1)
    ranks = inside + dot(mark(follows), totals.astype(jnp.bfloat16))
    return jnp.where(flags.astype(jnp.float32) > 0.0, ranks, -1.0)


def chosen_rows(capacity, upper, lower):
    rank = iota((capacity, LANES), 0).astype(jnp.float32)
    return jnp.concatenate([mark(rank == upper), mark(rank == lower)], axis=1)


def pack_kernel(lists, early, plane_ref, flags_ref, stem_ref, pair_ref, *refs):
    outs, (keys_ref, matrix, picked) = refs[: len(lists)], refs[len(lists) :]
    batch = stem_ref.shape[0]
    step = pl.program_id(0)

    @pl.when(step == 0)
    def _():
        keys_ref[...] = keys_of(flags_ref[...])
        build_matrix(pair_ref, matrix)

    plane = plane_ref[0]
    total = sum(out.shape[1] for out in outs)
    for i in range(batch):
        keys = keys_ref[pl.ds((step * batch + i) * KINDS, KINDS), :]
        second = keys[2:3], keys[3:4]
        beyond = keys[0:1] - early, keys[1:2] - early
        keyed = {
            "first": (keys[0:1], keys[1:2]),
            "send": [jnp.where(plane == 0, b, a) for a, b in zip(beyond, second)],
            "keep": [jnp.where(plane == 0, a, b) for a, b in zip(beyond, second)],
        }
        chosen = [chosen_rows(out.shape[1], *keyed[name]) for name, out in zip(lists, outs)]
        picked[i * total : (i + 1) * total, :] = dot(jnp.concatenate(chosen, axis=0), stem_ref[i]).astype(picked.dtype)
    terms = dot(picked[...], matrix[...]).astype(picked.dtype)
    at = 0
    for i in range(batch):
        for out in outs:
            out[i] = terms[at : at + out.shape[1]]
            at += out.shape[1]


def pack(lists, plane, flags, stem, pair, early, late):
    groups, rows, width = stem.shape
    batch = 8 if groups % 8 == 0 else 1
    out_width = 2 * pair.shape[2]
    sizes = [early if name == "first" else late for name in lists]
    return pl.pallas_call(
        functools.partial(pack_kernel, lists, early),
        grid=(groups // batch,),
        out_shape=[jax.ShapeDtypeStruct((groups, size, out_width), stem.dtype) for size in sizes],
        in_specs=[
            pl.BlockSpec(memory_space=pltpu.SMEM),
            pl.BlockSpec(flags.shape, lambda i: (0, 0)),
            pl.BlockSpec((batch, rows, width), lambda i: (i, 0, 0)),
            pl.BlockSpec(pair.shape, lambda i: (0, 0, 0)),
        ],
        out_specs=[pl.BlockSpec((batch, size, out_width), lambda i: (i, 0, 0)) for size in sizes],
        scratch_shapes=[
            pltpu.VMEM(flags.shape, jnp.float32),
            pltpu.VMEM((width, out_width), stem.dtype),
            pltpu.VMEM((batch * sum(sizes), width), stem.dtype),
        ],
        cost_estimate=pl.CostEstimate(
            flops=2 * groups * sum(sizes) * (rows + out_width) * width, bytes_accessed=3 * stem.size, transcendentals=0
        ),
        compiler_params=pltpu.CompilerParams(vmem_limit_bytes=20 << 20),
    )(plane, flags, pltpu.with_memory_space_constraint(stem, pltpu.HBM), pltpu.with_memory_space_constraint(pair, pltpu.HBM))


def add_kernel(a_ref, b_ref, *outs):
    total = a_ref[...].astype(jnp.float32) + b_ref[...].astype(jnp.float32)
    for out in outs:
        out[...] = total[:, : out.shape[1]].astype(out.dtype)


def add(a, b, sizes):
    vmem = pl.BlockSpec(memory_space=pltpu.VMEM)
    return pl.pallas_call(
        add_kernel,
        out_shape=[jax.ShapeDtypeStruct((a.shape[0], size, a.shape[2]), a.dtype) for size in sizes],
        in_specs=[vmem] * 2,
        out_specs=[vmem] * len(sizes),
        cost_estimate=pl.CostEstimate(flops=ADD_BYTES, bytes_accessed=ADD_BYTES, transcendentals=0),
        compiler_params=pltpu.CompilerParams(vmem_limit_bytes=12 << 20),
    )(a, b)


def places_kernel(own_rows, early, late, plane_ref, slots_ref, column_ref, early_ref, late_ref):
    mine, share = slots_ref.shape
    rows = mine * own_rows
    down = iota((own_rows, share), 0)
    across = iota((LANES, share), 0)
    wanted = []
    for k in range(mine):
        slots = slots_ref[k : k + 1, :]
        source = jnp.where(slots >= 0, slots // own_rows, -1)
        wanted.append(dot_nt(mark(down == slots % own_rows), mark(across == source)))
    wanted = jnp.minimum(jnp.concatenate(wanted, axis=0), 1.0)
    before = mark(iota((rows, rows), 0) > iota((rows, rows), 1))
    ranks = dot(before, wanted.astype(jnp.bfloat16)).astype(jnp.bfloat16)
    shift = plane_ref[0] * early
    group = iota((LANES, 1), 0) % mine
    lane = iota((LANES, LANES), 1)
    for block in range(mine * share // LANES):
        at, spot = block // STEP, block % STEP
        if spot == 0:
            in_early = jnp.full((LANES, LANES), -1, jnp.int32)
            in_late = in_early
        slots = column_ref[:, block : block + 1]
        source = slots // own_rows
        row = jnp.where(slots >= 0, group * own_rows + slots % own_rows, -1)
        looked = dot(mark(iota((LANES, rows), 1) == row), ranks)
        found = jnp.where(lane == source, looked, 0.0)
        rank = jnp.sum(found, axis=1, keepdims=True).astype(jnp.int32) + shift
        live, low = slots >= 0, rank < early
        in_early = jnp.where((lane == spot) & live & low, source * early + rank, in_early)
        in_late = jnp.where((lane == spot) & live & ~low, source * late + rank - early, in_late)
        if spot == STEP - 1:
            early_ref[at] = in_early
            late_ref[at] = in_late


def places(plane, own_slots, own_rows, early, late):
    column = own_slots.T.reshape(-1, LANES).T
    vmem = pl.BlockSpec(memory_space=pltpu.VMEM)
    return pl.pallas_call(
        functools.partial(places_kernel, own_rows, early, late),
        out_shape=[jax.ShapeDtypeStruct((own_slots.size // (STEP * LANES), LANES, LANES), jnp.int32)] * 2,
        in_specs=[pl.BlockSpec(memory_space=pltpu.SMEM), vmem, vmem],
        out_specs=[vmem] * 2,
        cost_estimate=pl.CostEstimate(flops=1 << 28, bytes_accessed=1 << 18, transcendentals=0),
    )(plane, own_slots, column)


def chosen_places(places, part, total):
    columns = iota((LANES, total), 1)
    first = part * PART
    return jnp.concatenate([mark(columns == places[:, first + i : first + i + 1]) for i in range(PART)], axis=0)


def early_kernel(places_ref, own_ref, other_ref, out_ref, table):
    both = own_ref[...].astype(jnp.float32) + other_ref[...].astype(jnp.float32)
    table[...] = both.astype(table.dtype)
    size = PART * LANES
    for block in range(places_ref.shape[0]):
        for part in range(STEP // PART):
            chosen = chosen_places(places_ref.at[block], part, table.shape[0])
            at = (block * STEP + part * PART) * LANES
            out_ref[at : at + size, :] = dot(chosen, table[...]).astype(out_ref.dtype)


def late_kernel(places_ref, late_ref, early_ref, out_ref):
    size = PART * LANES
    per = out_ref.shape[0] // (STEP // PART)
    for part in range(STEP // PART):
        chosen = chosen_places(places_ref.at[0], part, late_ref.shape[0])
        early = early_ref[part * size : (part + 1) * size, :].astype(jnp.float32)
        total = (dot(chosen, late_ref[...]) + early).astype(out_ref.dtype)
        out_ref[part * per : (part + 1) * per] = total.reshape(per, *out_ref.shape[1:])


def early_part(where, own, other):
    rows, width = own.shape
    slots = where.shape[0] * STEP * LANES
    vmem = pl.BlockSpec(memory_space=pltpu.VMEM)
    return pl.pallas_call(
        early_kernel,
        out_shape=pltpu.HBM((slots, width), own.dtype),
        in_specs=[vmem] * 3,
        out_specs=vmem,
        scratch_shapes=[pltpu.VMEM((rows, width), own.dtype)],
        cost_estimate=pl.CostEstimate(flops=EARLY_BYTES, bytes_accessed=EARLY_BYTES, transcendentals=0),
        compiler_params=pltpu.CompilerParams(vmem_limit_bytes=12 << 20),
    )(pltpu.with_memory_space_constraint(where, pltpu.HBM), own, other)


def late_part(where, late, early, mine):
    rows, width = early.shape
    blocks = where.shape[0]
    step = STEP * LANES
    return pl.pallas_call(
        late_kernel,
        grid=(blocks,),
        out_shape=jax.ShapeDtypeStruct((rows // mine, mine, width), early.dtype),
        in_specs=[
            pl.BlockSpec((1, LANES, LANES), lambda i: (i, 0, 0)),
            pl.BlockSpec(late.shape, lambda i: (0, 0)),
            pl.BlockSpec((step, width), lambda i: (i, 0)),
        ],
        out_specs=pl.BlockSpec((step // mine, mine, width), lambda i: (i, 0, 0)),
        cost_estimate=pl.CostEstimate(
            flops=2 * rows * late.shape[0] * width, bytes_accessed=4 * late.size, transcendentals=0
        ),
        compiler_params=pltpu.CompilerParams(vmem_limit_bytes=12 << 20),
    )(pltpu.with_memory_space_constraint(where, pltpu.HBM), late, pltpu.with_memory_space_constraint(early, pltpu.HBM))


def exchange(blocks):
    return lax.all_to_all(blocks, "group", split_axis=0, concat_axis=0, tiled=True)


def local(stem_blocks, cap_tensor, slot_rows, counts):
    cuts, groups = lax.axis_size("cuts"), lax.axis_size("group")
    group_total, own_rows, width = stem_blocks.shape[1:]
    mine = group_total // groups
    slot_total = slot_rows.shape[1]
    share = slot_total // cuts
    stem = stem_blocks.reshape(group_total * own_rows, width)
    pair = cap_tensor[0]

    me = lax.axis_index("cuts").astype(jnp.int32)

    def turned_slots():
        positions = jnp.arange(slot_total, dtype=jnp.int32)
        marked = jnp.where(positions[None, :] < counts[:, None], slot_rows, -1)
        doubled = jnp.concatenate([marked, marked], axis=1)
        return lax.dynamic_slice_in_dim(doubled, (me + 1) * share, slot_total, 1)

    def all_rows():
        terms = terms_of(stem, pair)
        return static_plan(terms.reshape(group_total, own_rows, terms.shape[1]), turned_slots(), cuts)

    unfit = mine * own_rows != 2 * LANES or LANES % own_rows or groups > LANES or share * mine % (STEP * LANES)
    if cuts != 2 or unfit:
        return all_rows()

    plane = me[None]
    flags = needs(slot_rows, counts, own_rows, groups)
    flags = exchange(flags.reshape(groups, KINDS, LANES))
    level = jnp.max(flags[:, 6, :].astype(jnp.float32)).astype(jnp.int32)
    flags = flags.reshape(groups * KINDS, LANES)
    by_owner = stem.reshape(groups, mine * own_rows, width)
    first, send = pack(("first", "send"), plane, flags, by_owner, pair, EARLY, LATES[-1])
    (keep,) = pack(("keep",), plane, flags, by_owner, pair, EARLY, LATES[-1])
    other = lax.ppermute(send, "cuts", [(0, 1), (1, 0)])
    own_early = exchange(first).reshape(groups * EARLY, first.shape[2])
    own_early, sums = lax.optimization_barrier((own_early, add(keep, other, LATES)))

    def rest(summed):
        late = summed.shape[1]
        other_early = lax.ppermute(own_early, "cuts", [(0, 1), (1, 0)])
        own_late = exchange(summed).reshape(groups * late, summed.shape[2])
        own_slots = turned_slots()[:, (cuts - 1) * share :]
        where_early, where_late = places(plane, own_slots, own_rows, EARLY, late)
        return late_part(where_late, own_late, early_part(where_early, own_early, other_early), mine)

    return lax.switch(level, [functools.partial(rest, summed) for summed in sums] + [all_rows])


def solution(mesh):
    in_specs = (
        P("cuts", None, "group", None),
        P("cuts", None, None, None),
        P("group", None),
        P("group"),
    )
    out_specs = P("cuts", "group", None)
    return jax.shard_map(local, mesh=mesh, in_specs=in_specs, out_specs=out_specs, check_vma=False)
```

```python
import functools

import jax
import jax.numpy as jnp
from jax import lax
from jax.experimental import pallas as pl
from jax.experimental.pallas import tpu as pltpu
from jax.sharding import PartitionSpec as P


def build_matrix(pair_ref, matrix):
    half = pair_ref.shape[1]
    real_part, imag_part = pair_ref[0], pair_ref[1]
    matrix[:half, :half] = real_part
    matrix[:half, half:] = imag_part
    matrix[half:, :half] = -imag_part
    matrix[half:, half:] = real_part


def terms_kernel(rows_ref, pair_ref, out_ref, matrix):
    @pl.when(pl.program_id(0) == 0)
    def _():
        build_matrix(pair_ref, matrix)

    out_ref[...] = dot(rows_ref[...], matrix[...]).astype(out_ref.dtype)


def terms_of(rows, pair):
    total, width = rows.shape
    block = min(512, total)
    out_width = 2 * pair.shape[2]
    return pl.pallas_call(
        terms_kernel,
        grid=(total // block,),
        out_shape=jax.ShapeDtypeStruct((total, out_width), rows.dtype),
        in_specs=[pl.BlockSpec((block, width), lambda i: (i, 0)), pl.BlockSpec(pair.shape, lambda i: (0, 0, 0))],
        out_specs=pl.BlockSpec((block, out_width), lambda i: (i, 0)),
        scratch_shapes=[pltpu.VMEM((width, out_width), rows.dtype)],
        cost_estimate=pl.CostEstimate(
            flops=2 * total * width * out_width, bytes_accessed=4 * rows.size, transcendentals=0
        ),
        compiler_params=pltpu.CompilerParams(vmem_limit_bytes=16 << 20),
    )(pltpu.with_memory_space_constraint(rows, pltpu.HBM), pltpu.with_memory_space_constraint(pair, pltpu.HBM))


def select_kernel(block, share, terms_ref, slots_ref, *outs):
    columns = iota((block, terms_ref.shape[0]), 1)
    for part, out in enumerate(outs):

        @pl.loop(0, share // block)
        def _(step):
            start = pl.multiple_of(step * block, block)
            chosen = mark(columns == slots_ref[pl.ds(part * share + start, block), :])
            out[pl.ds(start, block), :] = dot(chosen, terms_ref[...]).astype(out.dtype)


def select(terms, slots, parts):
    row_total, width = terms.shape
    slot_total = slots.shape[0]
    share = slot_total // parts
    return pl.pallas_call(
        functools.partial(select_kernel, min(256, share), share),
        out_shape=[jax.ShapeDtypeStruct((share, width), terms.dtype)] * parts,
        in_specs=[pl.BlockSpec(memory_space=pltpu.VMEM)] * 2,
        out_specs=[pl.BlockSpec(memory_space=pltpu.VMEM)] * parts,
        cost_estimate=pl.CostEstimate(
            flops=2 * row_total * width * slot_total,
            bytes_accessed=2 * (terms.size + slot_total * width),
            transcendentals=0,
        ),
        compiler_params=pltpu.CompilerParams(vmem_limit_bytes=24 << 20),
    )(terms, slots)


def static_plan(terms, turned, cuts):
    groups = lax.axis_size("group")
    group_total, own_rows, width = terms.shape
    mine = group_total // groups
    by_owner = terms.reshape(groups, mine, own_rows, width)
    sums, selected = [], []
    for k in range(mine):
        outgoing = by_owner[:, k]
        if k >= 2:
            outgoing, selected[k - 2] = lax.optimization_barrier((outgoing, selected[k - 2]))
        got = lax.all_to_all(outgoing, "group", split_axis=0, concat_axis=0, tiled=True)
        parts = select(got.reshape(groups * own_rows, width), turned[k][:, None], cuts)
        selected.append(parts)
    for parts in selected:
        total = parts[-1].astype(jnp.float32)
        for step in range(1, cuts):
            ring = [(i, (i + step) % cuts) for i in range(cuts)]
            total = total + lax.ppermute(parts[step - 1], "cuts", ring).astype(jnp.float32)
        sums.append(total.astype(terms.dtype))
    return jnp.stack(sums, axis=1)


KINDS = 8
LANES = 128
STEP = 8
PART = 2
EARLY = 56
LATES = 56, 64, 72
ADD_BYTES, EARLY_BYTES = 1<<34, 1<<34


def dot(a, b):
    return jnp.dot(a, b, preferred_element_type=jnp.float32)


def dot_nt(a, b):
    return lax.dot_general(a, b, (((1,), (1,)), ((), ())), preferred_element_type=jnp.float32)


def iota(shape, dim):
    return lax.broadcasted_iota(jnp.int32, shape, dim)


def mark(condition):
    return jnp.where(condition, 1.0, 0.0).astype(jnp.bfloat16)


def needs_kernel(own_rows, slots_ref, counts_ref, flags_ref):
    mine, slot_total = slots_ref.shape
    side = flags_ref.shape[0]
    hits = jnp.zeros((side, LANES), jnp.float32)
    place = iota((1, slot_total), 1)
    down = iota((side, slot_total), 0)
    across = iota((LANES, slot_total), 0)
    per = LANES // own_rows
    for k in range(mine):
        slots = slots_ref[k : k + 1, :]
        half = jnp.where(place >= slot_total // 2, 2, 0)
        row_key = (slots // own_rows) * KINDS + half + k // per
        row_key = jnp.where(place < counts_ref[k], row_key, -1)
        lane_key = slots % own_rows + (k % per) * own_rows
        hits = hits + dot_nt(mark(down == row_key), mark(across == lane_key))
    flags = jnp.minimum(hits, 1.0)
    sums = jnp.sum(flags, axis=1, keepdims=True)
    pairs = sums + jnp.concatenate([sums[1:], sums[:1]], axis=0)
    kind = iota((side, 1), 0) % KINDS
    most = jnp.max(jnp.where(kind == 0, pairs - EARLY, jnp.where(kind == 2, pairs, 0.0)), axis=0, keepdims=True)
    level = sum(jnp.where(most > late, 1.0, 0.0) for late in LATES)
    flags_ref[...] = jnp.where(iota((side, LANES), 0) % KINDS == 6, level, flags).astype(flags_ref.dtype)


def needs(slot_rows, counts, own_rows, groups):
    return pl.pallas_call(
        functools.partial(needs_kernel, own_rows),
        out_shape=jax.ShapeDtypeStruct((groups * KINDS, LANES), jnp.bfloat16),
        in_specs=[pl.BlockSpec(memory_space=pltpu.VMEM), pl.BlockSpec(memory_space=pltpu.SMEM)],
        out_specs=pl.BlockSpec(memory_space=pltpu.VMEM),
        cost_estimate=pl.CostEstimate(flops=1 << 28, bytes_accessed=1 << 17, transcendentals=0),
    )(slot_rows, counts)


def keys_of(flags):
    side = flags.shape[0]
    marks = flags
    lower = mark(iota((LANES, LANES), 0) < iota((LANES, LANES), 1))
    inside = dot(marks, lower)
    totals = dot(marks, jnp.ones((LANES, LANES), jnp.bfloat16))
    row, column = iota((side, side), 0), iota((side, side), 1)
    follows = ((row % KINDS == 1) | (row % KINDS == 3)) & (row - column == 1)
    ranks = inside + dot(mark(follows), totals.astype(jnp.bfloat16))
    return jnp.where(flags.astype(jnp.float32) > 0.0, ranks, -1.0)


def chosen_rows(capacity, upper, lower):
    rank = iota((capacity, LANES), 0).astype(jnp.float32)
    return jnp.concatenate([mark(rank == upper), mark(rank == lower)], axis=1)


def pack_kernel(lists, early, plane_ref, flags_ref, stem_ref, pair_ref, *refs):
    outs, (keys_ref, matrix, picked) = refs[: len(lists)], refs[len(lists) :]
    batch = stem_ref.shape[0]
    step = pl.program_id(0)

    @pl.when(step == 0)
    def _():
        keys_ref[...] = keys_of(flags_ref[...])
        build_matrix(pair_ref, matrix)

    plane = plane_ref[0]
    total = sum(out.shape[1] for out in outs)
    for i in range(batch):
        keys = keys_ref[pl.ds((step * batch + i) * KINDS, KINDS), :]
        second = keys[2:3], keys[3:4]
        beyond = keys[0:1] - early, keys[1:2] - early
        keyed = {
            "first": (keys[0:1], keys[1:2]),
            "send": [jnp.where(plane == 0, b, a) for a, b in zip(beyond, second)],
            "keep": [jnp.where(plane == 0, a, b) for a, b in zip(beyond, second)],
        }
        chosen = [chosen_rows(out.shape[1], *keyed[name]) for name, out in zip(lists, outs)]
        picked[i * total : (i + 1) * total, :] = dot(jnp.concatenate(chosen, axis=0), stem_ref[i]).astype(picked.dtype)
    terms = dot(picked[...], matrix[...]).astype(picked.dtype)
    at = 0
    for i in range(batch):
        for out in outs:
            out[i] = terms[at : at + out.shape[1]]
            at += out.shape[1]


def pack(lists, plane, flags, stem, pair, early, late):
    groups, rows, width = stem.shape
    batch = 8 if groups % 8 == 0 else 1
    out_width = 2 * pair.shape[2]
    sizes = [early if name == "first" else late for name in lists]
    return pl.pallas_call(
        functools.partial(pack_kernel, lists, early),
        grid=(groups // batch,),
        out_shape=[jax.ShapeDtypeStruct((groups, size, out_width), stem.dtype) for size in sizes],
        in_specs=[
            pl.BlockSpec(memory_space=pltpu.SMEM),
            pl.BlockSpec(flags.shape, lambda i: (0, 0)),
            pl.BlockSpec((batch, rows, width), lambda i: (i, 0, 0)),
            pl.BlockSpec(pair.shape, lambda i: (0, 0, 0)),
        ],
        out_specs=[pl.BlockSpec((batch, size, out_width), lambda i: (i, 0, 0)) for size in sizes],
        scratch_shapes=[
            pltpu.VMEM(flags.shape, jnp.float32),
            pltpu.VMEM((width, out_width), stem.dtype),
            pltpu.VMEM((batch * sum(sizes), width), stem.dtype),
        ],
        cost_estimate=pl.CostEstimate(
            flops=2 * groups * sum(sizes) * (rows + out_width) * width, bytes_accessed=3 * stem.size, transcendentals=0
        ),
        compiler_params=pltpu.CompilerParams(vmem_limit_bytes=20 << 20),
    )(plane, flags, pltpu.with_memory_space_constraint(stem, pltpu.HBM), pltpu.with_memory_space_constraint(pair, pltpu.HBM))


def add_kernel(level_ref, a_ref, b_ref, *refs):
    outs, (total, sent) = refs[:-2], refs[-2:]
    total[...] = (a_ref[...].astype(jnp.float32) + b_ref[...].astype(jnp.float32)).astype(total.dtype)
    for level, out in enumerate(outs):

        @pl.when(level_ref[0] == level)
        def _():
            copy = pltpu.make_async_copy(total.at[:, pl.ds(0, out.shape[1]), :], out, sent)
            copy.start()
            copy.wait()


def add(level, a, b, sizes):
    vmem, hbm = pl.BlockSpec(memory_space=pltpu.VMEM), pl.BlockSpec(memory_space=pltpu.HBM)
    return pl.pallas_call(
        add_kernel,
        out_shape=[pltpu.HBM((a.shape[0], size, a.shape[2]), a.dtype) for size in sizes],
        in_specs=[pl.BlockSpec(memory_space=pltpu.SMEM), vmem, vmem],
        out_specs=[hbm] * len(sizes),
        scratch_shapes=[pltpu.VMEM(a.shape, a.dtype), pltpu.SemaphoreType.DMA(())],
        cost_estimate=pl.CostEstimate(flops=ADD_BYTES, bytes_accessed=ADD_BYTES, transcendentals=0),
        compiler_params=pltpu.CompilerParams(vmem_limit_bytes=12 << 20),
    )(level, a, b)


def places_kernel(own_rows, early, late, plane_ref, slots_ref, column_ref, early_ref, late_ref):
    mine, share = slots_ref.shape
    rows = mine * own_rows
    down = iota((own_rows, share), 0)
    across = iota((LANES, share), 0)
    wanted = []
    for k in range(mine):
        slots = slots_ref[k : k + 1, :]
        source = jnp.where(slots >= 0, slots // own_rows, -1)
        wanted.append(dot_nt(mark(down == slots % own_rows), mark(across == source)))
    wanted = jnp.minimum(jnp.concatenate(wanted, axis=0), 1.0)
    before = mark(iota((rows, rows), 0) > iota((rows, rows), 1))
    ranks = dot(before, wanted.astype(jnp.bfloat16)).astype(jnp.bfloat16)
    shift = plane_ref[0] * early
    group = iota((LANES, 1), 0) % mine
    lane = iota((LANES, LANES), 1)
    for block in range(mine * share // LANES):
        at, spot = block // STEP, block % STEP
        if spot == 0:
            in_early = jnp.full((LANES, LANES), -1, jnp.int32)
            in_late = in_early
        slots = column_ref[:, block : block + 1]
        source = slots // own_rows
        row = jnp.where(slots >= 0, group * own_rows + slots % own_rows, -1)
        looked = dot(mark(iota((LANES, rows), 1) == row), ranks)
        found = jnp.where(lane == source, looked, 0.0)
        rank = jnp.sum(found, axis=1, keepdims=True).astype(jnp.int32) + shift
        live, low = slots >= 0, rank < early
        in_early = jnp.where((lane == spot) & live & low, source * early + rank, in_early)
        in_late = jnp.where((lane == spot) & live & ~low, source * late + rank - early, in_late)
        if spot == STEP - 1:
            early_ref[at] = in_early
            late_ref[at] = in_late


def places(plane, own_slots, own_rows, early, late):
    column = own_slots.T.reshape(-1, LANES).T
    vmem = pl.BlockSpec(memory_space=pltpu.VMEM)
    return pl.pallas_call(
        functools.partial(places_kernel, own_rows, early, late),
        out_shape=[jax.ShapeDtypeStruct((own_slots.size // (STEP * LANES), LANES, LANES), jnp.int32)] * 2,
        in_specs=[pl.BlockSpec(memory_space=pltpu.SMEM), vmem, vmem],
        out_specs=[vmem] * 2,
        cost_estimate=pl.CostEstimate(flops=1 << 28, bytes_accessed=1 << 18, transcendentals=0),
    )(plane, own_slots, column)


def chosen_places(places, part, total):
    columns = iota((LANES, total), 1)
    first = part * PART
    return jnp.concatenate([mark(columns == places[:, first + i : first + i + 1]) for i in range(PART)], axis=0)


def early_kernel(places_ref, own_ref, other_ref, out_ref, table):
    both = own_ref[...].astype(jnp.float32) + other_ref[...].astype(jnp.float32)
    table[...] = both.astype(table.dtype)
    size = PART * LANES
    for block in range(places_ref.shape[0]):
        for part in range(STEP // PART):
            chosen = chosen_places(places_ref.at[block], part, table.shape[0])
            at = (block * STEP + part * PART) * LANES
            out_ref[at : at + size, :] = dot(chosen, table[...]).astype(out_ref.dtype)


def late_kernel(places_ref, late_ref, early_ref, out_ref):
    size = PART * LANES
    per = out_ref.shape[0] // (STEP // PART)
    for part in range(STEP // PART):
        chosen = chosen_places(places_ref.at[0], part, late_ref.shape[0])
        early = early_ref[part * size : (part + 1) * size, :].astype(jnp.float32)
        total = (dot(chosen, late_ref[...]) + early).astype(out_ref.dtype)
        out_ref[part * per : (part + 1) * per] = total.reshape(per, *out_ref.shape[1:])


def early_part(where, own, other):
    rows, width = own.shape
    slots = where.shape[0] * STEP * LANES
    vmem = pl.BlockSpec(memory_space=pltpu.VMEM)
    return pl.pallas_call(
        early_kernel,
        out_shape=pltpu.HBM((slots, width), own.dtype),
        in_specs=[vmem] * 3,
        out_specs=vmem,
        scratch_shapes=[pltpu.VMEM((rows, width), own.dtype)],
        cost_estimate=pl.CostEstimate(flops=EARLY_BYTES, bytes_accessed=EARLY_BYTES, transcendentals=0),
        compiler_params=pltpu.CompilerParams(vmem_limit_bytes=12 << 20),
    )(pltpu.with_memory_space_constraint(where, pltpu.HBM), own, other)


def late_part(where, late, early, mine):
    rows, width = early.shape
    blocks = where.shape[0]
    step = STEP * LANES
    return pl.pallas_call(
        late_kernel,
        grid=(blocks,),
        out_shape=jax.ShapeDtypeStruct((rows // mine, mine, width), early.dtype),
        in_specs=[
            pl.BlockSpec((1, LANES, LANES), lambda i: (i, 0, 0)),
            pl.BlockSpec(late.shape, lambda i: (0, 0)),
            pl.BlockSpec((step, width), lambda i: (i, 0)),
        ],
        out_specs=pl.BlockSpec((step // mine, mine, width), lambda i: (i, 0, 0)),
        cost_estimate=pl.CostEstimate(
            flops=2 * rows * late.shape[0] * width, bytes_accessed=4 * late.size, transcendentals=0
        ),
        compiler_params=pltpu.CompilerParams(vmem_limit_bytes=12 << 20),
    )(pltpu.with_memory_space_constraint(where, pltpu.HBM), late, pltpu.with_memory_space_constraint(early, pltpu.HBM))


def exchange(blocks):
    return lax.all_to_all(blocks, "group", split_axis=0, concat_axis=0, tiled=True)


def local(stem_blocks, cap_tensor, slot_rows, counts):
    cuts, groups = lax.axis_size("cuts"), lax.axis_size("group")
    group_total, own_rows, width = stem_blocks.shape[1:]
    mine = group_total // groups
    slot_total = slot_rows.shape[1]
    share = slot_total // cuts
    stem = stem_blocks.reshape(group_total * own_rows, width)
    pair = cap_tensor[0]

    me = lax.axis_index("cuts").astype(jnp.int32)

    def turned_slots():
        positions = jnp.arange(slot_total, dtype=jnp.int32)
        marked = jnp.where(positions[None, :] < counts[:, None], slot_rows, -1)
        doubled = jnp.concatenate([marked, marked], axis=1)
        return lax.dynamic_slice_in_dim(doubled, (me + 1) * share, slot_total, 1)

    def all_rows():
        terms = terms_of(stem, pair)
        return static_plan(terms.reshape(group_total, own_rows, terms.shape[1]), turned_slots(), cuts)

    unfit = mine * own_rows != 2 * LANES or LANES % own_rows or groups > LANES or share * mine % (STEP * LANES)
    if cuts != 2 or unfit:
        return all_rows()

    plane = me[None]
    flags = needs(slot_rows, counts, own_rows, groups)
    flags = exchange(flags.reshape(groups, KINDS, LANES))
    level = jnp.max(flags[:, 6, :].astype(jnp.float32)).astype(jnp.int32)
    flags = flags.reshape(groups * KINDS, LANES)
    by_owner = stem.reshape(groups, mine * own_rows, width)
    first, send = pack(("first", "send"), plane, flags, by_owner, pair, EARLY, LATES[-1])
    (keep,) = pack(("keep",), plane, flags, by_owner, pair, EARLY, LATES[-1])
    other = lax.ppermute(send, "cuts", [(0, 1), (1, 0)])
    own_early = exchange(first).reshape(groups * EARLY, first.shape[2])
    own_early, sums = lax.optimization_barrier((own_early, add(level[None], keep, other, LATES)))

    def rest(summed):
        late = summed.shape[1]
        other_early = lax.ppermute(own_early, "cuts", [(0, 1), (1, 0)])
        own_late = exchange(summed).reshape(groups * late, summed.shape[2])
        own_slots = turned_slots()[:, (cuts - 1) * share :]
        where_early, where_late = places(plane, own_slots, own_rows, EARLY, late)
        return late_part(where_late, own_late, early_part(where_early, own_early, other_early), mine)

    return lax.switch(level, [functools.partial(rest, summed) for summed in sums] + [all_rows])


def solution(mesh):
    in_specs = (
        P("cuts", None, "group", None),
        P("cuts", None, None, None),
        P("group", None),
        P("group"),
    )
    out_specs = P("cuts", "group", None)
    return jax.shard_map(local, mesh=mesh, in_specs=in_specs, out_specs=out_specs, check_vma=False)
```

```python
import functools

import jax
import jax.numpy as jnp
from jax import lax
from jax.experimental import pallas as pl
from jax.experimental.pallas import tpu as pltpu
from jax.sharding import PartitionSpec as P


def build_matrix(pair_ref, matrix):
    half = pair_ref.shape[1]
    real_part, imag_part = pair_ref[0], pair_ref[1]
    matrix[:half, :half] = real_part
    matrix[:half, half:] = imag_part
    matrix[half:, :half] = -imag_part
    matrix[half:, half:] = real_part


def terms_kernel(rows_ref, pair_ref, out_ref, matrix):
    @pl.when(pl.program_id(0) == 0)
    def _():
        build_matrix(pair_ref, matrix)

    out_ref[...] = dot(rows_ref[...], matrix[...]).astype(out_ref.dtype)


def terms_of(rows, pair):
    total, width = rows.shape
    block = min(512, total)
    out_width = 2 * pair.shape[2]
    return pl.pallas_call(
        terms_kernel,
        grid=(total // block,),
        out_shape=jax.ShapeDtypeStruct((total, out_width), rows.dtype),
        in_specs=[pl.BlockSpec((block, width), lambda i: (i, 0)), pl.BlockSpec(pair.shape, lambda i: (0, 0, 0))],
        out_specs=pl.BlockSpec((block, out_width), lambda i: (i, 0)),
        scratch_shapes=[pltpu.VMEM((width, out_width), rows.dtype)],
        cost_estimate=pl.CostEstimate(
            flops=2 * total * width * out_width, bytes_accessed=4 * rows.size, transcendentals=0
        ),
        compiler_params=pltpu.CompilerParams(vmem_limit_bytes=16 << 20),
    )(pltpu.with_memory_space_constraint(rows, pltpu.HBM), pltpu.with_memory_space_constraint(pair, pltpu.HBM))


def select_kernel(block, share, terms_ref, slots_ref, *outs):
    columns = iota((block, terms_ref.shape[0]), 1)
    for part, out in enumerate(outs):

        @pl.loop(0, share // block)
        def _(step):
            start = pl.multiple_of(step * block, block)
            chosen = mark(columns == slots_ref[pl.ds(part * share + start, block), :])
            out[pl.ds(start, block), :] = dot(chosen, terms_ref[...]).astype(out.dtype)


def select(terms, slots, parts):
    row_total, width = terms.shape
    slot_total = slots.shape[0]
    share = slot_total // parts
    return pl.pallas_call(
        functools.partial(select_kernel, min(256, share), share),
        out_shape=[jax.ShapeDtypeStruct((share, width), terms.dtype)] * parts,
        in_specs=[pl.BlockSpec(memory_space=pltpu.VMEM)] * 2,
        out_specs=[pl.BlockSpec(memory_space=pltpu.VMEM)] * parts,
        cost_estimate=pl.CostEstimate(
            flops=2 * row_total * width * slot_total,
            bytes_accessed=2 * (terms.size + slot_total * width),
            transcendentals=0,
        ),
        compiler_params=pltpu.CompilerParams(vmem_limit_bytes=24 << 20),
    )(terms, slots)


def static_plan(terms, turned, cuts):
    groups = lax.axis_size("group")
    group_total, own_rows, width = terms.shape
    mine = group_total // groups
    by_owner = terms.reshape(groups, mine, own_rows, width)
    sums, selected = [], []
    for k in range(mine):
        outgoing = by_owner[:, k]
        if k >= 2:
            outgoing, selected[k - 2] = lax.optimization_barrier((outgoing, selected[k - 2]))
        got = lax.all_to_all(outgoing, "group", split_axis=0, concat_axis=0, tiled=True)
        parts = select(got.reshape(groups * own_rows, width), turned[k][:, None], cuts)
        selected.append(parts)
    for parts in selected:
        total = parts[-1].astype(jnp.float32)
        for step in range(1, cuts):
            ring = [(i, (i + step) % cuts) for i in range(cuts)]
            total = total + lax.ppermute(parts[step - 1], "cuts", ring).astype(jnp.float32)
        sums.append(total.astype(terms.dtype))
    return jnp.stack(sums, axis=1)


KINDS = 8
LANES = 128
STEP = 8
PART = 2
EARLY = 56
LATES = 56, 64, 72
ADD_BYTES, EARLY_BYTES = 1<<34, 1<<34


def dot(a, b):
    return jnp.dot(a, b, preferred_element_type=jnp.float32)


def dot_nt(a, b):
    return lax.dot_general(a, b, (((1,), (1,)), ((), ())), preferred_element_type=jnp.float32)


def iota(shape, dim):
    return lax.broadcasted_iota(jnp.int32, shape, dim)


def mark(condition):
    return jnp.where(condition, 1.0, 0.0).astype(jnp.bfloat16)


def needs_kernel(own_rows, slots_ref, counts_ref, flags_ref):
    mine, slot_total = slots_ref.shape
    side = flags_ref.shape[0]
    hits = jnp.zeros((side, LANES), jnp.float32)
    place = iota((1, slot_total), 1)
    down = iota((side, slot_total), 0)
    across = iota((LANES, slot_total), 0)
    per = LANES // own_rows
    for k in range(mine):
        slots = slots_ref[k : k + 1, :]
        half = jnp.where(place >= slot_total // 2, 2, 0)
        row_key = (slots // own_rows) * KINDS + half + k // per
        row_key = jnp.where(place < counts_ref[k], row_key, -1)
        lane_key = slots % own_rows + (k % per) * own_rows
        hits = hits + dot_nt(mark(down == row_key), mark(across == lane_key))
    flags = jnp.minimum(hits, 1.0)
    sums = jnp.sum(flags, axis=1, keepdims=True)
    pairs = sums + jnp.concatenate([sums[1:], sums[:1]], axis=0)
    kind = iota((side, 1), 0) % KINDS
    most = jnp.max(jnp.where(kind == 0, pairs - EARLY, jnp.where(kind == 2, pairs, 0.0)), axis=0, keepdims=True)
    level = sum(jnp.where(most > late, 1.0, 0.0) for late in LATES)
    flags_ref[...] = jnp.where(iota((side, LANES), 0) % KINDS == 6, level, flags).astype(flags_ref.dtype)


def needs(slot_rows, counts, own_rows, groups):
    return pl.pallas_call(
        functools.partial(needs_kernel, own_rows),
        out_shape=jax.ShapeDtypeStruct((groups * KINDS, LANES), jnp.bfloat16),
        in_specs=[pl.BlockSpec(memory_space=pltpu.VMEM), pl.BlockSpec(memory_space=pltpu.SMEM)],
        out_specs=pl.BlockSpec(memory_space=pltpu.VMEM),
        cost_estimate=pl.CostEstimate(flops=1 << 28, bytes_accessed=1 << 17, transcendentals=0),
    )(slot_rows, counts)


def keys_of(flags):
    side = flags.shape[0]
    marks = flags
    lower = mark(iota((LANES, LANES), 0) < iota((LANES, LANES), 1))
    inside = dot(marks, lower)
    totals = dot(marks, jnp.ones((LANES, LANES), jnp.bfloat16))
    row, column = iota((side, side), 0), iota((side, side), 1)
    follows = ((row % KINDS == 1) | (row % KINDS == 3)) & (row - column == 1)
    ranks = inside + dot(mark(follows), totals.astype(jnp.bfloat16))
    return jnp.where(flags.astype(jnp.float32) > 0.0, ranks, -1.0)


def chosen_rows(capacity, upper, lower):
    rank = iota((capacity, LANES), 0).astype(jnp.float32)
    return jnp.concatenate([mark(rank == upper), mark(rank == lower)], axis=1)


def pack_kernel(lists, early, plane_ref, flags_ref, stem_ref, pair_ref, *refs):
    outs, (keys_ref, matrix, picked) = refs[: len(lists)], refs[len(lists) :]
    batch = stem_ref.shape[0]
    step = pl.program_id(0)

    @pl.when(step == 0)
    def _():
        keys_ref[...] = keys_of(flags_ref[...])
        build_matrix(pair_ref, matrix)

    plane = plane_ref[0]
    total = sum(out.shape[1] for out in outs)
    for i in range(batch):
        keys = keys_ref[pl.ds((step * batch + i) * KINDS, KINDS), :]
        second = keys[2:3], keys[3:4]
        beyond = keys[0:1] - early, keys[1:2] - early
        keyed = {
            "first": (keys[0:1], keys[1:2]),
            "send": [jnp.where(plane == 0, b, a) for a, b in zip(beyond, second)],
            "keep": [jnp.where(plane == 0, a, b) for a, b in zip(beyond, second)],
        }
        chosen = [chosen_rows(out.shape[1], *keyed[name]) for name, out in zip(lists, outs)]
        picked[i * total : (i + 1) * total, :] = dot(jnp.concatenate(chosen, axis=0), stem_ref[i]).astype(picked.dtype)
    terms = dot(picked[...], matrix[...]).astype(picked.dtype)
    at = 0
    for i in range(batch):
        for out in outs:
            out[i] = terms[at : at + out.shape[1]]
            at += out.shape[1]


def pack(lists, plane, flags, stem, pair, early, late):
    groups, rows, width = stem.shape
    batch = 8 if groups % 8 == 0 else 1
    out_width = 2 * pair.shape[2]
    sizes = [early if name == "first" else late for name in lists]
    return pl.pallas_call(
        functools.partial(pack_kernel, lists, early),
        grid=(groups // batch,),
        out_shape=[jax.ShapeDtypeStruct((groups, size, out_width), stem.dtype) for size in sizes],
        in_specs=[
            pl.BlockSpec(memory_space=pltpu.SMEM),
            pl.BlockSpec(flags.shape, lambda i: (0, 0)),
            pl.BlockSpec((batch, rows, width), lambda i: (i, 0, 0)),
            pl.BlockSpec(pair.shape, lambda i: (0, 0, 0)),
        ],
        out_specs=[pl.BlockSpec((batch, size, out_width), lambda i: (i, 0, 0)) for size in sizes],
        scratch_shapes=[
            pltpu.VMEM(flags.shape, jnp.float32),
            pltpu.VMEM((width, out_width), stem.dtype),
            pltpu.VMEM((batch * sum(sizes), width), stem.dtype),
        ],
        cost_estimate=pl.CostEstimate(
            flops=2 * groups * sum(sizes) * (rows + out_width) * width, bytes_accessed=3 * stem.size, transcendentals=0
        ),
        compiler_params=pltpu.CompilerParams(vmem_limit_bytes=20 << 20),
    )(plane, flags, pltpu.with_memory_space_constraint(stem, pltpu.HBM), pltpu.with_memory_space_constraint(pair, pltpu.HBM))


def add_kernel(level_ref, a_ref, b_ref, *refs):
    outs, (total, sent) = refs[:-2], refs[-2:]
    total[...] = (a_ref[...].astype(jnp.float32) + b_ref[...].astype(jnp.float32)).astype(total.dtype)
    for level, out in enumerate(outs):

        @pl.when(level_ref[0] == level)
        def _():
            copy = pltpu.make_async_copy(total.at[:, pl.ds(0, out.shape[1]), :], out, sent)
            copy.start()
            copy.wait()


def add(level, a, b, sizes):
    vmem, hbm = pl.BlockSpec(memory_space=pltpu.VMEM), pl.BlockSpec(memory_space=pltpu.HBM)
    return pl.pallas_call(
        add_kernel,
        out_shape=[pltpu.HBM((a.shape[0], size, a.shape[2]), a.dtype) for size in sizes],
        in_specs=[pl.BlockSpec(memory_space=pltpu.SMEM), vmem, vmem],
        out_specs=[hbm] * len(sizes),
        scratch_shapes=[pltpu.VMEM(a.shape, a.dtype), pltpu.SemaphoreType.DMA(())],
        cost_estimate=pl.CostEstimate(flops=ADD_BYTES, bytes_accessed=ADD_BYTES, transcendentals=0),
        compiler_params=pltpu.CompilerParams(vmem_limit_bytes=12 << 20),
    )(level, a, b)


def places_kernel(own_rows, early, late, plane_ref, slots_ref, column_ref, early_ref, late_ref):
    mine, share = slots_ref.shape
    rows = mine * own_rows
    down = iota((own_rows, share), 0)
    across = iota((LANES, share), 0)
    wanted = []
    for k in range(mine):
        slots = slots_ref[k : k + 1, :]
        source = jnp.where(slots >= 0, slots // own_rows, -1)
        wanted.append(dot_nt(mark(down == slots % own_rows), mark(across == source)))
    wanted = jnp.minimum(jnp.concatenate(wanted, axis=0), 1.0)
    before = mark(iota((rows, rows), 0) > iota((rows, rows), 1))
    ranks = dot(before, wanted.astype(jnp.bfloat16)).astype(jnp.bfloat16)
    shift = plane_ref[0] * early
    group = iota((LANES, 1), 0) % mine
    lane = iota((LANES, LANES), 1)
    for block in range(mine * share // LANES):
        at, spot = block // STEP, block % STEP
        if spot == 0:
            in_early = jnp.full((LANES, LANES), -1, jnp.int32)
            in_late = in_early
        slots = column_ref[:, block : block + 1]
        source = slots // own_rows
        row = jnp.where(slots >= 0, group * own_rows + slots % own_rows, -1)
        looked = dot(mark(iota((LANES, rows), 1) == row), ranks)
        found = jnp.where(lane == source, looked, 0.0)
        rank = jnp.sum(found, axis=1, keepdims=True).astype(jnp.int32) + shift
        live, low = slots >= 0, rank < early
        in_early = jnp.where((lane == spot) & live & low, source * early + rank, in_early)
        in_late = jnp.where((lane == spot) & live & ~low, source * late + rank - early, in_late)
        if spot == STEP - 1:
            early_ref[at] = in_early
            late_ref[at] = in_late


def places(plane, own_slots, own_rows, early, late):
    column = own_slots.T.reshape(-1, LANES).T
    vmem = pl.BlockSpec(memory_space=pltpu.VMEM)
    return pl.pallas_call(
        functools.partial(places_kernel, own_rows, early, late),
        out_shape=[jax.ShapeDtypeStruct((own_slots.size // (STEP * LANES), LANES, LANES), jnp.int32)] * 2,
        in_specs=[pl.BlockSpec(memory_space=pltpu.SMEM), vmem, vmem],
        out_specs=[vmem] * 2,
        cost_estimate=pl.CostEstimate(flops=1 << 28, bytes_accessed=1 << 18, transcendentals=0),
    )(plane, own_slots, column)


def chosen_places(places, part, total):
    columns = iota((LANES, total), 1)
    first = part * PART
    return jnp.concatenate([mark(columns == places[:, first + i : first + i + 1]) for i in range(PART)], axis=0)


def early_kernel(places_ref, own_ref, other_ref, out_ref, table):
    both = own_ref[...].astype(jnp.float32) + other_ref[...].astype(jnp.float32)
    table[...] = both.astype(table.dtype)
    size = PART * LANES
    for block in range(places_ref.shape[0]):
        for part in range(STEP // PART):
            chosen = chosen_places(places_ref.at[block], part, table.shape[0])
            at = (block * STEP + part * PART) * LANES
            out_ref[at : at + size, :] = dot(chosen, table[...]).astype(out_ref.dtype)


def late_kernel(places_ref, late_ref, early_ref, out_ref):
    size = PART * LANES
    per = out_ref.shape[0] // (STEP // PART)
    for part in range(STEP // PART):
        chosen = chosen_places(places_ref.at[0], part, late_ref.shape[0])
        early = early_ref[part * size : (part + 1) * size, :].astype(jnp.float32)
        total = (dot(chosen, late_ref[...]) + early).astype(out_ref.dtype)
        out_ref[part * per : (part + 1) * per] = total.reshape(per, *out_ref.shape[1:])


def early_part(where, own, other):
    rows, width = own.shape
    slots = where.shape[0] * STEP * LANES
    vmem = pl.BlockSpec(memory_space=pltpu.VMEM)
    return pl.pallas_call(
        early_kernel,
        out_shape=pltpu.HBM((slots, width), own.dtype),
        in_specs=[vmem] * 3,
        out_specs=vmem,
        scratch_shapes=[pltpu.VMEM((rows, width), own.dtype)],
        cost_estimate=pl.CostEstimate(flops=EARLY_BYTES, bytes_accessed=EARLY_BYTES, transcendentals=0),
        compiler_params=pltpu.CompilerParams(vmem_limit_bytes=12 << 20),
    )(pltpu.with_memory_space_constraint(where, pltpu.HBM), own, other)


def late_part(where, late, early, mine):
    rows, width = early.shape
    blocks = where.shape[0]
    step = STEP * LANES
    return pl.pallas_call(
        late_kernel,
        grid=(blocks,),
        out_shape=jax.ShapeDtypeStruct((rows // mine, mine, width), early.dtype),
        in_specs=[
            pl.BlockSpec((1, LANES, LANES), lambda i: (i, 0, 0)),
            pl.BlockSpec(memory_space=pltpu.VMEM),
            pl.BlockSpec((step, width), lambda i: (i, 0)),
        ],
        out_specs=pl.BlockSpec((step // mine, mine, width), lambda i: (i, 0, 0)),
        cost_estimate=pl.CostEstimate(
            flops=2 * rows * late.shape[0] * width, bytes_accessed=4 * late.size, transcendentals=0
        ),
        compiler_params=pltpu.CompilerParams(vmem_limit_bytes=12 << 20),
    )(pltpu.with_memory_space_constraint(where, pltpu.HBM), late, pltpu.with_memory_space_constraint(early, pltpu.HBM))


def exchange(blocks):
    return lax.all_to_all(blocks, "group", split_axis=0, concat_axis=0, tiled=True)


def local(stem_blocks, cap_tensor, slot_rows, counts):
    cuts, groups = lax.axis_size("cuts"), lax.axis_size("group")
    group_total, own_rows, width = stem_blocks.shape[1:]
    mine = group_total // groups
    slot_total = slot_rows.shape[1]
    share = slot_total // cuts
    stem = stem_blocks.reshape(group_total * own_rows, width)
    pair = cap_tensor[0]

    me = lax.axis_index("cuts").astype(jnp.int32)

    def turned_slots():
        positions = jnp.arange(slot_total, dtype=jnp.int32)
        marked = jnp.where(positions[None, :] < counts[:, None], slot_rows, -1)
        doubled = jnp.concatenate([marked, marked], axis=1)
        return lax.dynamic_slice_in_dim(doubled, (me + 1) * share, slot_total, 1)

    def all_rows():
        terms = terms_of(stem, pair)
        return static_plan(terms.reshape(group_total, own_rows, terms.shape[1]), turned_slots(), cuts)

    unfit = mine * own_rows != 2 * LANES or LANES % own_rows or groups > LANES or share * mine % (STEP * LANES)
    if cuts != 2 or unfit:
        return all_rows()

    plane = me[None]
    flags = needs(slot_rows, counts, own_rows, groups)
    flags = exchange(flags.reshape(groups, KINDS, LANES))
    level = jnp.max(flags[:, 6, :].astype(jnp.float32)).astype(jnp.int32)
    flags = flags.reshape(groups * KINDS, LANES)
    by_owner = stem.reshape(groups, mine * own_rows, width)
    first, send = pack(("first", "send"), plane, flags, by_owner, pair, EARLY, LATES[-1])
    (keep,) = pack(("keep",), plane, flags, by_owner, pair, EARLY, LATES[-1])
    other = lax.ppermute(send, "cuts", [(0, 1), (1, 0)])
    own_early = exchange(first).reshape(groups * EARLY, first.shape[2])
    own_early, sums = lax.optimization_barrier((own_early, add(level[None], keep, other, LATES)))

    def rest(summed):
        late = summed.shape[1]
        other_early = lax.ppermute(own_early, "cuts", [(0, 1), (1, 0)])
        own_late = exchange(summed).reshape(groups * late, summed.shape[2])
        own_slots = turned_slots()[:, (cuts - 1) * share :]
        where_early, where_late = places(plane, own_slots, own_rows, EARLY, late)
        return late_part(where_late, own_late, early_part(where_early, own_early, other_early), mine)

    return lax.switch(level, [functools.partial(rest, summed) for summed in sums] + [all_rows])


def solution(mesh):
    in_specs = (
        P("cuts", None, "group", None),
        P("cuts", None, None, None),
        P("group", None),
        P("group"),
    )
    out_specs = P("cuts", "group", None)
    return jax.shard_map(local, mesh=mesh, in_specs=in_specs, out_specs=out_specs, check_vma=False)
```

```python
import functools

import jax
import jax.numpy as jnp
from jax import lax
from jax.experimental import pallas as pl
from jax.experimental.pallas import tpu as pltpu
from jax.sharding import PartitionSpec as P


def build_matrix(pair_ref, matrix):
    half = pair_ref.shape[1]
    real_part, imag_part = pair_ref[0], pair_ref[1]
    matrix[:half, :half] = real_part
    matrix[:half, half:] = imag_part
    matrix[half:, :half] = -imag_part
    matrix[half:, half:] = real_part


def terms_kernel(rows_ref, pair_ref, out_ref, matrix):
    @pl.when(pl.program_id(0) == 0)
    def _():
        build_matrix(pair_ref, matrix)

    out_ref[...] = dot(rows_ref[...], matrix[...]).astype(out_ref.dtype)


def terms_of(rows, pair):
    total, width = rows.shape
    block = min(512, total)
    out_width = 2 * pair.shape[2]
    return pl.pallas_call(
        terms_kernel,
        grid=(total // block,),
        out_shape=jax.ShapeDtypeStruct((total, out_width), rows.dtype),
        in_specs=[pl.BlockSpec((block, width), lambda i: (i, 0)), pl.BlockSpec(pair.shape, lambda i: (0, 0, 0))],
        out_specs=pl.BlockSpec((block, out_width), lambda i: (i, 0)),
        scratch_shapes=[pltpu.VMEM((width, out_width), rows.dtype)],
        cost_estimate=pl.CostEstimate(
            flops=2 * total * width * out_width, bytes_accessed=4 * rows.size, transcendentals=0
        ),
        compiler_params=pltpu.CompilerParams(vmem_limit_bytes=16 << 20),
    )(pltpu.with_memory_space_constraint(rows, pltpu.HBM), pltpu.with_memory_space_constraint(pair, pltpu.HBM))


def select_kernel(block, share, terms_ref, slots_ref, *outs):
    columns = iota((block, terms_ref.shape[0]), 1)
    for part, out in enumerate(outs):

        @pl.loop(0, share // block)
        def _(step):
            start = pl.multiple_of(step * block, block)
            chosen = mark(columns == slots_ref[pl.ds(part * share + start, block), :])
            out[pl.ds(start, block), :] = dot(chosen, terms_ref[...]).astype(out.dtype)


def select(terms, slots, parts):
    row_total, width = terms.shape
    slot_total = slots.shape[0]
    share = slot_total // parts
    return pl.pallas_call(
        functools.partial(select_kernel, min(256, share), share),
        out_shape=[jax.ShapeDtypeStruct((share, width), terms.dtype)] * parts,
        in_specs=[pl.BlockSpec(memory_space=pltpu.VMEM)] * 2,
        out_specs=[pl.BlockSpec(memory_space=pltpu.VMEM)] * parts,
        cost_estimate=pl.CostEstimate(
            flops=2 * row_total * width * slot_total,
            bytes_accessed=2 * (terms.size + slot_total * width),
            transcendentals=0,
        ),
        compiler_params=pltpu.CompilerParams(vmem_limit_bytes=24 << 20),
    )(terms, slots)


def static_plan(terms, turned, cuts):
    groups = lax.axis_size("group")
    group_total, own_rows, width = terms.shape
    mine = group_total // groups
    by_owner = terms.reshape(groups, mine, own_rows, width)
    sums, selected = [], []
    for k in range(mine):
        outgoing = by_owner[:, k]
        if k >= 2:
            outgoing, selected[k - 2] = lax.optimization_barrier((outgoing, selected[k - 2]))
        got = lax.all_to_all(outgoing, "group", split_axis=0, concat_axis=0, tiled=True)
        parts = select(got.reshape(groups * own_rows, width), turned[k][:, None], cuts)
        selected.append(parts)
    for parts in selected:
        total = parts[-1].astype(jnp.float32)
        for step in range(1, cuts):
            ring = [(i, (i + step) % cuts) for i in range(cuts)]
            total = total + lax.ppermute(parts[step - 1], "cuts", ring).astype(jnp.float32)
        sums.append(total.astype(terms.dtype))
    return jnp.stack(sums, axis=1)


KINDS = 8
LANES = 128
STEP = 8
PART = 2
EARLY = 56
LATES = 56, 64, 72
ADD_BYTES, EARLY_BYTES = 1<<34, 1<<34


def dot(a, b):
    return jnp.dot(a, b, preferred_element_type=jnp.float32)


def dot_nt(a, b):
    return lax.dot_general(a, b, (((1,), (1,)), ((), ())), preferred_element_type=jnp.float32)


def iota(shape, dim):
    return lax.broadcasted_iota(jnp.int32, shape, dim)


def mark(condition):
    return jnp.where(condition, 1.0, 0.0).astype(jnp.bfloat16)


def needs_kernel(own_rows, slots_ref, counts_ref, flags_ref):
    mine, slot_total = slots_ref.shape
    side = flags_ref.shape[0]
    hits = jnp.zeros((side, LANES), jnp.float32)
    place = iota((1, slot_total), 1)
    down = iota((side, slot_total), 0)
    across = iota((LANES, slot_total), 0)
    per = LANES // own_rows
    for k in range(mine):
        slots = slots_ref[k : k + 1, :]
        half = jnp.where(place >= slot_total // 2, 2, 0)
        row_key = (slots // own_rows) * KINDS + half + k // per
        row_key = jnp.where(place < counts_ref[k], row_key, -1)
        lane_key = slots % own_rows + (k % per) * own_rows
        hits = hits + dot_nt(mark(down == row_key), mark(across == lane_key))
    flags = jnp.minimum(hits, 1.0)
    sums = jnp.sum(flags, axis=1, keepdims=True)
    pairs = sums + jnp.concatenate([sums[1:], sums[:1]], axis=0)
    kind = iota((side, 1), 0) % KINDS
    most = jnp.max(jnp.where(kind == 0, pairs - EARLY, jnp.where(kind == 2, pairs, 0.0)), axis=0, keepdims=True)
    level = sum(jnp.where(most > late, 1.0, 0.0) for late in LATES)
    flags_ref[...] = jnp.where(iota((side, LANES), 0) % KINDS == 6, level, flags).astype(flags_ref.dtype)


def needs(slot_rows, counts, own_rows, groups):
    return pl.pallas_call(
        functools.partial(needs_kernel, own_rows),
        out_shape=jax.ShapeDtypeStruct((groups * KINDS, LANES), jnp.bfloat16),
        in_specs=[pl.BlockSpec(memory_space=pltpu.VMEM), pl.BlockSpec(memory_space=pltpu.SMEM)],
        out_specs=pl.BlockSpec(memory_space=pltpu.VMEM),
        cost_estimate=pl.CostEstimate(flops=1 << 28, bytes_accessed=1 << 17, transcendentals=0),
    )(slot_rows, counts)


def keys_of(flags):
    side = flags.shape[0]
    marks = flags
    lower = mark(iota((LANES, LANES), 0) < iota((LANES, LANES), 1))
    inside = dot(marks, lower)
    totals = dot(marks, jnp.ones((LANES, LANES), jnp.bfloat16))
    row, column = iota((side, side), 0), iota((side, side), 1)
    follows = ((row % KINDS == 1) | (row % KINDS == 3)) & (row - column == 1)
    ranks = inside + dot(mark(follows), totals.astype(jnp.bfloat16))
    return jnp.where(flags.astype(jnp.float32) > 0.0, ranks, -1.0)


def chosen_rows(capacity, upper, lower):
    rank = iota((capacity, LANES), 0).astype(jnp.float32)
    return jnp.concatenate([mark(rank == upper), mark(rank == lower)], axis=1)


def pack_kernel(lists, early, plane_ref, flags_ref, stem_ref, pair_ref, *refs):
    outs, (keys_ref, matrix, picked) = refs[: len(lists)], refs[len(lists) :]
    batch = stem_ref.shape[0]
    step = pl.program_id(0)

    @pl.when(step == 0)
    def _():
        keys_ref[...] = keys_of(flags_ref[...])
        build_matrix(pair_ref, matrix)

    plane = plane_ref[0]
    total = sum(out.shape[1] for out in outs)
    for i in range(batch):
        keys = keys_ref[pl.ds((step * batch + i) * KINDS, KINDS), :]
        second = keys[2:3], keys[3:4]
        beyond = keys[0:1] - early, keys[1:2] - early
        keyed = {
            "first": (keys[0:1], keys[1:2]),
            "send": [jnp.where(plane == 0, b, a) for a, b in zip(beyond, second)],
            "keep": [jnp.where(plane == 0, a, b) for a, b in zip(beyond, second)],
        }
        chosen = [chosen_rows(out.shape[1], *keyed[name]) for name, out in zip(lists, outs)]
        picked[i * total : (i + 1) * total, :] = dot(jnp.concatenate(chosen, axis=0), stem_ref[i]).astype(picked.dtype)
    terms = dot(picked[...], matrix[...]).astype(picked.dtype)
    at = 0
    for i in range(batch):
        for out in outs:
            out[i] = terms[at : at + out.shape[1]]
            at += out.shape[1]


def pack(lists, plane, flags, stem, pair, early, late):
    groups, rows, width = stem.shape
    batch = 8 if groups % 8 == 0 else 1
    out_width = 2 * pair.shape[2]
    sizes = [early if name == "first" else late for name in lists]
    return pl.pallas_call(
        functools.partial(pack_kernel, lists, early),
        grid=(groups // batch,),
        out_shape=[jax.ShapeDtypeStruct((groups, size, out_width), stem.dtype) for size in sizes],
        in_specs=[
            pl.BlockSpec(memory_space=pltpu.SMEM),
            pl.BlockSpec(flags.shape, lambda i: (0, 0)),
            pl.BlockSpec((batch, rows, width), lambda i: (i, 0, 0)),
            pl.BlockSpec(pair.shape, lambda i: (0, 0, 0)),
        ],
        out_specs=[pl.BlockSpec((batch, size, out_width), lambda i: (i, 0, 0)) for size in sizes],
        scratch_shapes=[
            pltpu.VMEM(flags.shape, jnp.float32),
            pltpu.VMEM((width, out_width), stem.dtype),
            pltpu.VMEM((batch * sum(sizes), width), stem.dtype),
        ],
        cost_estimate=pl.CostEstimate(
            flops=2 * groups * sum(sizes) * (rows + out_width) * width, bytes_accessed=3 * stem.size, transcendentals=0
        ),
        compiler_params=pltpu.CompilerParams(vmem_limit_bytes=20 << 20),
    )(plane, flags, pltpu.with_memory_space_constraint(stem, pltpu.HBM), pltpu.with_memory_space_constraint(pair, pltpu.HBM))


def add_kernel(level_ref, a_ref, b_ref, *refs):
    outs, (total, sent) = refs[:-2], refs[-2:]
    total[...] = (a_ref[...].astype(jnp.float32) + b_ref[...].astype(jnp.float32)).astype(total.dtype)
    for level, out in enumerate(outs):

        @pl.when(level_ref[0] == level)
        def _():
            copy = pltpu.make_async_copy(total.at[:, pl.ds(0, out.shape[1]), :], out, sent)
            copy.start()
            copy.wait()


def add(level, a, b, sizes):
    vmem, hbm = pl.BlockSpec(memory_space=pltpu.VMEM), pl.BlockSpec(memory_space=pltpu.HBM)
    return pl.pallas_call(
        add_kernel,
        out_shape=[pltpu.HBM((a.shape[0], size, a.shape[2]), a.dtype) for size in sizes],
        in_specs=[pl.BlockSpec(memory_space=pltpu.SMEM), vmem, vmem],
        out_specs=[hbm] * len(sizes),
        scratch_shapes=[pltpu.VMEM(a.shape, a.dtype), pltpu.SemaphoreType.DMA(())],
        cost_estimate=pl.CostEstimate(flops=ADD_BYTES, bytes_accessed=ADD_BYTES, transcendentals=0),
        compiler_params=pltpu.CompilerParams(vmem_limit_bytes=12 << 20),
    )(level, a, b)


def places_kernel(own_rows, early, late, plane_ref, slots_ref, column_ref, early_ref, late_ref):
    mine, share = slots_ref.shape
    rows = mine * own_rows
    down = iota((own_rows, share), 0)
    across = iota((LANES, share), 0)
    wanted = []
    for k in range(mine):
        slots = slots_ref[k : k + 1, :]
        source = jnp.where(slots >= 0, slots // own_rows, -1)
        wanted.append(dot_nt(mark(down == slots % own_rows), mark(across == source)))
    wanted = jnp.minimum(jnp.concatenate(wanted, axis=0), 1.0)
    before = mark(iota((rows, rows), 0) > iota((rows, rows), 1))
    ranks = dot(before, wanted.astype(jnp.bfloat16)).astype(jnp.bfloat16)
    shift = plane_ref[0] * early
    group = iota((LANES, 1), 0) % mine
    lane = iota((LANES, LANES), 1)
    for block in range(mine * share // LANES):
        at, spot = block // STEP, block % STEP
        if spot == 0:
            in_early = jnp.full((LANES, LANES), -1, jnp.int32)
            in_late = in_early
        slots = column_ref[:, block : block + 1]
        source = slots // own_rows
        row = jnp.where(slots >= 0, group * own_rows + slots % own_rows, -1)
        looked = dot(mark(iota((LANES, rows), 1) == row), ranks)
        found = jnp.where(lane == source, looked, 0.0)
        rank = jnp.sum(found, axis=1, keepdims=True).astype(jnp.int32) + shift
        live, low = slots >= 0, rank < early
        in_early = jnp.where((lane == spot) & live & low, source * early + rank, in_early)
        in_late = jnp.where((lane == spot) & live & ~low, source * late + rank - early, in_late)
        if spot == STEP - 1:
            early_ref[at] = in_early
            late_ref[at] = in_late


def places(plane, own_slots, own_rows, early, late):
    column = own_slots.T.reshape(-1, LANES).T
    vmem = pl.BlockSpec(memory_space=pltpu.VMEM)
    return pl.pallas_call(
        functools.partial(places_kernel, own_rows, early, late),
        out_shape=[jax.ShapeDtypeStruct((own_slots.size // (STEP * LANES), LANES, LANES), jnp.int32)] * 2,
        in_specs=[pl.BlockSpec(memory_space=pltpu.SMEM), vmem, vmem],
        out_specs=[vmem] * 2,
        cost_estimate=pl.CostEstimate(flops=1 << 28, bytes_accessed=1 << 18, transcendentals=0),
    )(plane, own_slots, column)


def chosen_places(places, part, total):
    columns = iota((LANES, total), 1)
    first = part * PART
    return jnp.concatenate([mark(columns == places[:, first + i : first + i + 1]) for i in range(PART)], axis=0)


def early_kernel(places_ref, own_ref, other_ref, out_ref, table):
    both = own_ref[...].astype(jnp.float32) + other_ref[...].astype(jnp.float32)
    table[...] = both.astype(table.dtype)
    size = PART * LANES
    for block in range(places_ref.shape[0]):
        for part in range(STEP // PART):
            chosen = chosen_places(places_ref.at[block], part, table.shape[0])
            at = (block * STEP + part * PART) * LANES
            out_ref[at : at + size, :] = dot(chosen, table[...]).astype(out_ref.dtype)


def late_kernel(places_ref, late_ref, early_ref, out_ref):
    size = PART * LANES
    per = out_ref.shape[0] // (STEP // PART)
    for part in range(STEP // PART):
        chosen = chosen_places(places_ref.at[0], part, late_ref.shape[0])
        early = early_ref[part * size : (part + 1) * size, :].astype(jnp.float32)
        total = (dot(chosen, late_ref[...]) + early).astype(out_ref.dtype)
        out_ref[part * per : (part + 1) * per] = total.reshape(per, *out_ref.shape[1:])


def early_part(where, own, other, cost):
    rows, width = own.shape
    slots = where.shape[0] * STEP * LANES
    vmem = pl.BlockSpec(memory_space=pltpu.VMEM)
    return pl.pallas_call(
        early_kernel,
        out_shape=pltpu.HBM((slots, width), own.dtype),
        in_specs=[vmem] * 3,
        out_specs=vmem,
        scratch_shapes=[pltpu.VMEM((rows, width), own.dtype)],
        cost_estimate=pl.CostEstimate(flops=cost, bytes_accessed=cost, transcendentals=0),
        compiler_params=pltpu.CompilerParams(vmem_limit_bytes=12 << 20),
    )(pltpu.with_memory_space_constraint(where, pltpu.HBM), own, other)


def late_part(where, late, early, mine):
    rows, width = early.shape
    blocks = where.shape[0]
    step = STEP * LANES
    return pl.pallas_call(
        late_kernel,
        grid=(blocks,),
        out_shape=jax.ShapeDtypeStruct((rows // mine, mine, width), early.dtype),
        in_specs=[
            pl.BlockSpec((1, LANES, LANES), lambda i: (i, 0, 0)),
            pl.BlockSpec(late.shape, lambda i: (0, 0)),
            pl.BlockSpec((step, width), lambda i: (i, 0)),
        ],
        out_specs=pl.BlockSpec((step // mine, mine, width), lambda i: (i, 0, 0)),
        cost_estimate=pl.CostEstimate(
            flops=2 * rows * late.shape[0] * width, bytes_accessed=4 * late.size, transcendentals=0
        ),
        compiler_params=pltpu.CompilerParams(vmem_limit_bytes=12 << 20),
    )(pltpu.with_memory_space_constraint(where, pltpu.HBM), late, pltpu.with_memory_space_constraint(early, pltpu.HBM))


def exchange(blocks):
    return lax.all_to_all(blocks, "group", split_axis=0, concat_axis=0, tiled=True)


def local(stem_blocks, cap_tensor, slot_rows, counts):
    cuts, groups = lax.axis_size("cuts"), lax.axis_size("group")
    group_total, own_rows, width = stem_blocks.shape[1:]
    mine = group_total // groups
    slot_total = slot_rows.shape[1]
    share = slot_total // cuts
    stem = stem_blocks.reshape(group_total * own_rows, width)
    pair = cap_tensor[0]

    me = lax.axis_index("cuts").astype(jnp.int32)

    def turned_slots():
        positions = jnp.arange(slot_total, dtype=jnp.int32)
        marked = jnp.where(positions[None, :] < counts[:, None], slot_rows, -1)
        doubled = jnp.concatenate([marked, marked], axis=1)
        return lax.dynamic_slice_in_dim(doubled, (me + 1) * share, slot_total, 1)

    def all_rows():
        terms = terms_of(stem, pair)
        return static_plan(terms.reshape(group_total, own_rows, terms.shape[1]), turned_slots(), cuts)

    unfit = mine * own_rows != 2 * LANES or LANES % own_rows or groups > LANES or share * mine % (STEP * LANES)
    if cuts != 2 or unfit:
        return all_rows()

    plane = me[None]
    flags = needs(slot_rows, counts, own_rows, groups)
    flags = exchange(flags.reshape(groups, KINDS, LANES))
    level = jnp.max(flags[:, 6, :].astype(jnp.float32)).astype(jnp.int32)
    flags = flags.reshape(groups * KINDS, LANES)
    by_owner = stem.reshape(groups, mine * own_rows, width)
    first, send = pack(("first", "send"), plane, flags, by_owner, pair, EARLY, LATES[-1])
    (keep,) = pack(("keep",), plane, flags, by_owner, pair, EARLY, LATES[-1])
    other = lax.ppermute(send, "cuts", [(0, 1), (1, 0)])
    own_early = exchange(first).reshape(groups * EARLY, first.shape[2])
    own_early, sums = lax.optimization_barrier((own_early, add(level[None], keep, other, LATES)))

    def rest(summed):
        late = summed.shape[1]
        other_early = lax.ppermute(own_early, "cuts", [(0, 1), (1, 0)])
        own_late = exchange(summed).reshape(groups * late, summed.shape[2])
        own_slots = turned_slots()[:, (cuts - 1) * share :]
        where_early, where_late = places(plane, own_slots, own_rows, EARLY, late)
        cost = EARLY_BYTES if late < LATES[-1] else 1 << 22
        early_sums = early_part(where_early, own_early, other_early, cost)
        return late_part(where_late, own_late, early_sums, mine)

    return lax.switch(level, [functools.partial(rest, summed) for summed in sums] + [all_rows])


def solution(mesh):
    in_specs = (
        P("cuts", None, "group", None),
        P("cuts", None, None, None),
        P("group", None),
        P("group"),
    )
    out_specs = P("cuts", "group", None)
    return jax.shard_map(local, mesh=mesh, in_specs=in_specs, out_specs=out_specs, check_vma=False)
```
